32 devices in a mesh: fsdp: 2 (over y), ctx: 16 (over z, x, core).
Axes of the slice: x: 2, y: 2, z: 4, core: 2. Of those that a mesh axis runs over, the one named last changes fastest.
Arguments:
- layer_input: bfloat16 [8, 1024, 1024], P('fsdp', 'ctx'), may hold values from -6 to 6
- output_grad: bfloat16 [8, 1024, 1024], P('fsdp', 'ctx'), may hold values from -6 to 6
- segments: int32 [8, 1024], P('fsdp'), may hold values from 0 to 3, never falling along the last dimension, each value on 1 to 512 neighbouring positions
- assignment: int32 [16], replicated, may hold values from 0 to 15, each once
- first_gain: bfloat16 [1024], P('fsdp'), may hold values from 0.5 to 1.5
- first_bias: bfloat16 [1024], P('fsdp'), may hold values from -1.5 to 1.5
- input_weight: bfloat16 [1024, 3072], P('fsdp'), may hold values from -0.25 to 0.25
- query_bias: bfloat16 [1024], P('fsdp'), may hold values from -2.5 to 2.5
- value_bias: bfloat16 [1024], P('fsdp'), may hold values from -2.5 to 2.5
- output_weight: bfloat16 [1024, 1024], P(None, 'fsdp'), may hold values from -1.5 to 1.5
- output_bias: bfloat16 [1024], P('fsdp'), may hold values from -1.5 to 1.5
- second_gain: bfloat16 [1024], P('fsdp'), may hold values from 0.5 to 1.5
- second_bias: bfloat16 [1024], P('fsdp'), may hold values from -1.5 to 1.5
- expand_weight: bfloat16 [1024, 4096], P('fsdp'), may hold values from -0.1875 to 0.1875
- expand_bias: bfloat16 [4096], P('fsdp'), may hold values from -2.5 to 2.5
- shrink_weight: bfloat16 [4096, 1024], P(None, 'fsdp'), may hold values from -0.09375 to 0.09375
- shrink_bias: bfloat16 [1024], P('fsdp'), may hold values from -1.5 to 1.5
Outputs:
- layer_output: bfloat16 [8, 1024, 1024], P('fsdp', 'ctx')
- input_grad: float32 [8, 1024, 1024], P('fsdp', 'ctx')
- first_gain_grad: float32 [1024], P('fsdp')
- first_bias_grad: float32 [1024], P('fsdp')
- input_weight_grad: float32 [1024, 3072], P('fsdp')
- query_bias_grad: float32 [1024], P('fsdp')
- value_bias_grad: float32 [1024], P('fsdp')
- output_weight_grad: float32 [1024, 1024], P(None, 'fsdp')
- output_bias_grad: float32 [1024], P('fsdp')
- second_gain_grad: float32 [1024], P('fsdp')
- second_bias_grad: float32 [1024], P('fsdp')
- expand_weight_grad: float32 [1024, 4096], P('fsdp')
- expand_bias_grad: float32 [4096], P('fsdp')
- shrink_weight_grad: float32 [4096, 1024], P(None, 'fsdp')
- shrink_bias_grad: float32 [1024], P('fsdp')
The draws below stay inside these ranges and needn't reach their ends.
Inputs may be any that keep to these rules, and one draw needn't show every extreme that they name: `segments`: in each sequence, in the order of positions, the document numbers never fall; each document has 1 to 512 positions and one has exactly 512. A permutation: index i of ctx holds the blocks assignment[i] and 31 - assignment[i] of every sequence.
All inputs are finite; a program needn't handle non-finite values.
Results may differ from the reference program's by a relative error of at most 0.012.
The reference program's roundings to bfloat16 on the way count: a program that leaves them out, or rounds other values in their place, can miss the bound.
Values may be sent and summed in bfloat16 or wider, within the bound.
No kernel may reach another device: no remote copies, remote signals or barrier semaphores. Data moves between devices by JAX's collectives and lax.ppermute only.
A program may use at most 320 MiB of HBM per device.

```python
import math
import jax
import jax.numpy as jnp
import numpy as np
from jax import lax

D = 1024
HEADS = 16
HEAD_DIM = 64
FF = 4096
SPAN = 32
PAIRS = 16
SPANS = 32
L = 1024
SEQS = 8
DOC_MAX = 512
DOCS = 4


def block_levels(rng, extent, split, low, largest):
    factor_of, own = 1.0, jax.random.fold_in(rng, 6)
    for axis_at, blocks in split:
        draws = jnp.exp(jax.random.uniform(jax.random.fold_in(own, axis_at), (blocks,), jnp.float32, low / len(split), largest / len(split)))
        factor_of = factor_of * jnp.repeat(draws, extent[axis_at] // blocks).reshape([-1 if axis == axis_at else 1 for axis in range(len(extent))])
    return factor_of


def split_up(count, total, reach, skew):
    weights = [(1 << 20) // math.isqrt(standing ** skew) + 1 for standing in range(2, count + 1)]
    surplus, counts = total - reach - (count - 1), [1] * (count - 1)
    while surplus > 0:
        movable = [i for i in range(count - 1) if counts[i] < reach]
        mass, remaining = sum([weights[i] for i in movable]), surplus
        for i in movable:
            more = min(reach - counts[i], max(1, remaining * weights[i] // mass), surplus)
            counts[i] = counts[i] + more
            surplus = surplus - more
    return np.array([reach] + counts)


def ragged_sizes(stream_key, count, total, limit, skew):
    if count == 2:
        one = jax.random.randint(stream_key, (), max(1, total - limit), min(limit, total - 1) + 1)
        return jnp.stack([one, total - one])
    sizes = jnp.asarray(split_up(count, total, limit, skew), jnp.int32)
    couples = (count - 1) // 2
    donor, taker = sizes[1:1 + 2 * couples:2], sizes[2:2 + 2 * couples:2]
    slack = jnp.minimum(donor - 1, limit - taker)
    shifted = jax.random.randint(jax.random.fold_in(stream_key, 1), (couples,), 0, 1 << 20) % (slack + 1)
    sizes = sizes.at[1:1 + 2 * couples:2].set(donor - shifted).at[2:2 + 2 * couples:2].set(taker + shifted)
    return sizes[jax.random.permutation(jax.random.fold_in(stream_key, 2), count)]


def normal_values(rng, extent, deviation, bound, split=(), kind=jnp.bfloat16):
    drawn = deviation * jax.random.normal(rng, extent, jnp.float32)
    if split:
        drawn = drawn * block_levels(rng, extent, split, -0.22, 0.18)
    return jnp.clip(drawn, -bound, bound).astype(kind)


def setup_inputs(seed: int = 0) -> dict:
    splits = jax.random.split(jax.random.key(seed), 18)
    layer_input = normal_values(splits[0], (SEQS, L, D), 1.0, 6.0, ((0, 2), (1, 16)))
    output_grad = normal_values(splits[1], (SEQS, L, D), 1.0, 6.0, ((0, 2), (1, 16)))
    segments = jax.vmap(lambda own: jnp.searchsorted(jnp.cumsum(ragged_sizes(own, DOCS, L, DOC_MAX, 1)), jnp.arange(L), side="right"))(jax.random.split(splits[2], SEQS)).reshape((SEQS, L)).astype(jnp.int32)
    assignment = jax.random.permutation(splits[3], PAIRS).astype(jnp.int32)
    first_gain = jnp.clip(0.5 + 1.0 * jax.random.uniform(splits[4], (D,), jnp.float32) ** block_levels(splits[4], (D,), ((0, 2),), -0.2, 0.2), 0.5, 1.5).astype(jnp.bfloat16)
    first_bias = normal_values(splits[5], (D,), 0.3, 1.5, ((0, 2),))
    input_weight = normal_values(splits[6], (D, 3 * D), (D // 2) ** -0.5, 0.25, ((0, 2),))
    query_bias = normal_values(splits[7], (D,), 0.5, 2.5, ((0, 2),))
    value_bias = normal_values(splits[8], (D,), 0.5, 2.5, ((0, 2),))
    output_weight = normal_values(splits[9], (D, D), (max(D // 64, 1)) ** -0.5, 1.5, ((1, 2),))
    output_bias = normal_values(splits[10], (D,), 0.3, 1.5, ((0, 2),))
    second_gain = jnp.clip(0.5 + 1.0 * jax.random.uniform(splits[11], (D,), jnp.float32) ** block_levels(splits[11], (D,), ((0, 2),), -0.2, 0.2), 0.5, 1.5).astype(jnp.bfloat16)
    second_bias = normal_values(splits[12], (D,), 0.3, 1.5, ((0, 2),))
    expand_weight = normal_values(splits[13], (D, FF), D ** -0.5, 0.1875, ((0, 2),))
    expand_bias = normal_values(splits[14], (FF,), 0.5, 2.5, ((0, 2),))
    shrink_weight = normal_values(splits[15], (FF, D), FF ** -0.5, 0.09375, ((1, 2),))
    shrink_bias = normal_values(splits[16], (D,), 0.3, 1.5, ((0, 2),))
    return dict(layer_input=layer_input, output_grad=output_grad, segments=segments, assignment=assignment, first_gain=first_gain, first_bias=first_bias, input_weight=input_weight, query_bias=query_bias, value_bias=value_bias, output_weight=output_weight, output_bias=output_bias, second_gain=second_gain, second_bias=second_bias, expand_weight=expand_weight, expand_bias=expand_bias, shrink_weight=shrink_weight, shrink_bias=shrink_bias)


EPSILON = 1e-05
MASKED = -1000000000.0
HIGHEST = lax.Precision.HIGHEST

@jax.custom_vjp
def low(v):
    return lax.optimization_barrier(v.astype(jnp.bfloat16)).astype(jnp.float32)

@jax.custom_vjp
def low_back(v):
    return v

def low_keep(v):
    return (low(v), None)

def low_pass(kept, grad):
    return (grad,)

def back_keep(v):
    return (v, None)

def back_low(kept, grad):
    return (low(grad),)
low.defvjp(low_keep, low_pass)
low_back.defvjp(back_keep, back_low)

def matmul(left_side, right_side):
    return jnp.dot(left_side, right_side, precision=HIGHEST)

def layer_norm(inputs, norm_gain, norm_bias):
    center = inputs - lax.optimization_barrier(jnp.mean(inputs, axis=-1, keepdims=True))
    spread = lax.optimization_barrier(jnp.mean(center * center, axis=-1, keepdims=True))
    return center * lax.rsqrt(spread + EPSILON) * norm_gain + norm_bias

def gelu_tanh(inputs):
    return jax.nn.gelu(inputs, approximate=True)

def position_table(assignment):
    places = jnp.arange(SPAN * SPANS, dtype=jnp.int32)
    owner = (places // (2 * SPAN)).astype(jnp.int32)
    within = places % (2 * SPAN)
    paired = jnp.take(assignment, owner).astype(jnp.int32)
    early = paired * SPAN + within
    later = (SPANS - 1 - paired) * SPAN + within - SPAN
    return jnp.where(within < SPAN, early, later).astype(jnp.int32)

def attend(queries, query_place, query_doc, key_rows, value_rows, key_place, key_doc):
    inv_root = 1.0 / math.sqrt(HEAD_DIM)
    scores = jnp.einsum('qhd,khd->hqk', queries, key_rows, precision=HIGHEST) * inv_root
    scores = low_back(scores)
    allowed = (key_place[None, :] <= query_place[:, None]) & (key_doc[None, :] == query_doc[:, None])
    scores = jnp.where(allowed[None], scores, MASKED)
    log_total = jax.nn.logsumexp(scores, axis=-1, keepdims=True)
    probs = jnp.exp(scores - log_total)
    return jnp.einsum('hqk,khd->qhd', low(probs), value_rows, precision=HIGHEST)

def forward(params, inputs, places, documents):
    first_gain, first_bias, input_weight, query_bias, value_bias, output_weight, output_bias, second_gain, second_bias, expand_weight, expand_bias, shrink_weight, shrink_bias = params
    length = inputs.shape[0]
    normed = low(layer_norm(inputs, first_gain, first_bias))
    joined = matmul(normed, input_weight)
    queries = low(low_back(joined[:, :D] + query_bias)).reshape(length, HEADS, HEAD_DIM)
    key_rows = low(low_back(joined[:, D:2 * D])).reshape(length, HEADS, HEAD_DIM)
    value_rows = low(low_back(joined[:, 2 * D:] + value_bias)).reshape(length, HEADS, HEAD_DIM)
    size_q = min(512, length)
    blocks = length // size_q
    checked = jax.checkpoint(attend)

    def one_block(pieces):
        return checked(pieces[0], pieces[1], pieces[2], key_rows, value_rows, places, documents)
    mixed_heads = lax.map(one_block, (queries.reshape(blocks, size_q, HEADS, HEAD_DIM), places.reshape(blocks, size_q), documents.reshape(blocks, size_q)))
    mixed_heads = low(low_back(mixed_heads.reshape(length, D)))
    residual = inputs + low_back(matmul(mixed_heads, output_weight) + output_bias)
    normed_two = low(layer_norm(residual, second_gain, second_bias))
    hidden = low_back(matmul(normed_two, expand_weight) + expand_bias)
    active = low(gelu_tanh(hidden))
    return residual + low_back(matmul(active, shrink_weight) + shrink_bias)

def reference(layer_input, output_grad, segments, assignment, first_gain, first_bias, input_weight, query_bias, value_bias, output_weight, output_bias, second_gain, second_bias, expand_weight, expand_bias, shrink_weight, shrink_bias):
    params = tuple((weight.astype(jnp.float32) for weight in (first_gain, first_bias, input_weight, query_bias, value_bias, output_weight, output_bias, second_gain, second_bias, expand_weight, expand_bias, shrink_weight, shrink_bias)))
    places = position_table(assignment)

    def one_sequence(totals, pieces):
        inputs = pieces[0].astype(jnp.float32)
        documents = jnp.take(pieces[2], places).astype(jnp.int32)
        outputs, pull_back = jax.vjp(lambda weights, values: forward(weights, values, places, documents), params, inputs)
        weight_grads, input_grads = pull_back(pieces[1].astype(jnp.float32))
        totals = jax.tree.map(lambda first, second: first + second, totals, weight_grads)
        return (totals, (outputs.astype(jnp.bfloat16), input_grads))
    zeros = jax.tree.map(jnp.zeros_like, params)
    totals, (layer_output, input_grad) = lax.scan(one_sequence, zeros, (layer_input, output_grad, segments))
    return (layer_output, input_grad, totals[0], totals[1], totals[2], totals[3], totals[4], totals[5], totals[6], totals[7], totals[8], totals[9], totals[10], totals[11], totals[12])
```

```python
import functools
import math

import jax
import jax.numpy as jnp
from jax import lax
from jax.experimental import pallas as pl
from jax.experimental.pallas import tpu as pltpu
from jax.sharding import PartitionSpec as P

HEADS = 16
EPSILON = 1e-05
MASKED = -1000000000.0
LANES = 128
MIB = 1024 * 1024
F32 = jnp.float32
BF16 = jnp.bfloat16

V_G1, V_B1, V_BQ, V_BV, V_BO, V_G2, V_B2, V_BS = range(8)


def bits_of(number):
    return number.bit_length() - 1


def dot(left, right):
    return jnp.dot(left, right, preferred_element_type=F32)


def dot_nt(left, right):
    return lax.dot_general(left, right, (((1,), (1,)), ((), ())), preferred_element_type=F32)


def dot_tn(left, right):
    return lax.dot_general(left, right, (((0,), (0,)), ((), ())), preferred_element_type=F32)


def swap_bit(value, axis, size, bit):
    return lax.ppermute(value, axis, [(i, i ^ (1 << bit)) for i in range(size)])


def reverse_bits(value, count):
    out = jnp.zeros_like(value)
    for bit in range(count):
        out = out | (((value >> bit) & 1) << (count - 1 - bit))
    return out


def params(limit_mib=48):
    return pltpu.CompilerParams(vmem_limit_bytes=limit_mib * MIB)


def whole(shape):
    rank = len(shape)
    return pl.BlockSpec(tuple(shape), lambda *_: (0,) * rank)


def cost(flops, moved):
    return pl.CostEstimate(flops=int(flops), bytes_accessed=int(moved), transcendentals=0)


def gather_parts(weight, dim, fsdp_size, ctx_size, y_index, c_index, bits):
    extent = weight.shape[dim]
    if fsdp_size != 2:
        full = lax.all_gather(weight, "fsdp", axis=dim, tiled=True)
        return [(full, jnp.int32(0))]
    pieces = 1 << len(bits)
    size = extent // pieces
    mine = jnp.int32(0)
    for place, bit in enumerate(bits):
        mine = mine | (((c_index >> bit) & 1) << place)
    first = lax.dynamic_slice_in_dim(weight, mine * size, size, dim)
    held = [(swap_bit(first, "fsdp", 2, 0), mine)]
    for place, bit in enumerate(bits):
        held = held + [
            (swap_bit(array, "ctx", ctx_size, bit), number ^ (1 << place)) for array, number in held
        ]
    base = (1 - y_index) * extent
    parts = [(weight, y_index * extent)]
    return parts + [(array, base + number * size) for array, number in held]


def split_parts(parts):
    arrays = [part[0] for part in parts]
    offsets = jnp.stack([part[1] for part in parts]).astype(jnp.int32)
    return arrays, offsets


def place_rows(target, offsets, part_refs):
    for number, ref in enumerate(part_refs):
        rows = ref.shape[0]
        target[pl.ds(pl.multiple_of(offsets[number], 32), rows), :] = ref[...]


def place_columns(target, offsets, part_refs):
    for number, ref in enumerate(part_refs):
        columns = ref.shape[1]
        target[:, pl.ds(pl.multiple_of(offsets[number], LANES), columns)] = ref[...]


def norm_stats(values):
    center = values - jnp.mean(values, axis=-1, keepdims=True)
    spread = jnp.mean(center * center, axis=-1, keepdims=True)
    rate = lax.rsqrt(spread + EPSILON)
    return center * rate, rate


def norm_kernel(x_ref, v_ref, h_ref):
    hat, _ = norm_stats(x_ref[...].astype(F32))
    h_ref[...] = (hat * v_ref[V_G1 : V_G1 + 1, :] + v_ref[V_B1 : V_B1 + 1, :]).astype(BF16)


def first_norm(x, vectors):
    return pl.pallas_call(
        norm_kernel,
        out_shape=jax.ShapeDtypeStruct(x.shape, BF16),
        compiler_params=params(),
        name="first_norm",
    )(x, vectors)


def qkv_kernel(part_count, seqs, rows, off_ref, h_ref, v_ref, *refs):
    parts = refs[: 3 * part_count]
    out_ref, weight = refs[3 * part_count :]
    group = pl.program_id(0)
    width = weight.shape[-1]
    per = width // LANES
    for kind in range(3):
        place_rows(
            weight.at[kind], off_ref, parts[kind * part_count : (kind + 1) * part_count]
        )
        value = dot(h_ref[...], weight[kind])
        if kind != 1:
            row = V_BQ if kind == 0 else V_BV
            start = pl.multiple_of(group * width, LANES)
            value = value + v_ref[row : row + 1, pl.ds(start, width)]
        value = value.astype(BF16)
        for pair in range(per):
            out_ref[pair, :, :, kind * LANES : (kind + 1) * LANES] = value[
                :, pair * LANES : (pair + 1) * LANES
            ].reshape(seqs, rows, LANES)


def project(h1, vectors, parts, seqs, rows):
    arrays, offsets = split_parts(parts)
    tokens, features = h1.shape
    width = 2 * LANES
    groups = features // width
    pairs = features // LANES
    specs = []
    operands = []
    for kind in range(3):
        for array in arrays:
            specs.append(
                pl.BlockSpec((array.shape[0], width), lambda g, o, k=kind: (0, k * groups + g))
            )
            operands.append(array)
    return pl.pallas_call(
        functools.partial(qkv_kernel, len(arrays), seqs, rows),
        grid_spec=pltpu.PrefetchScalarGridSpec(
            num_scalar_prefetch=1,
            grid=(groups,),
            in_specs=[whole(h1.shape), whole(vectors.shape)] + specs,
            out_specs=pl.BlockSpec((2, seqs, rows, 3 * LANES), lambda g, o: (g, 0, 0, 0)),
            scratch_shapes=[pltpu.VMEM((3, features, width), BF16)],
        ),
        out_shape=jax.ShapeDtypeStruct((pairs, seqs, rows, 3 * LANES), BF16),
        compiler_params=params(),
        cost_estimate=cost(6 * tokens * features * features, 6 * features * features),
        name="project",
    )(offsets, h1, vectors, *operands)


def to_places(table, ctx_size, half, source, target):
    for device in range(ctx_size):
        pair = table[device]
        early = pl.multiple_of(pair * half, half)
        later = pl.multiple_of((2 * ctx_size - 1 - pair) * half, half)
        target[pl.ds(early, half), :] = source[device, 0, 0:half, :]
        target[pl.ds(later, half), :] = source[device, 0, half : 2 * half, :]


def both_heads(block):
    first = lax.broadcasted_iota(jnp.int32, block.shape, 0) < LANES // 2
    zero = jnp.zeros_like(block)
    return jnp.concatenate([jnp.where(first, block, zero), jnp.where(first, zero, block)], axis=1)


def stacked_heads(block):
    first = lax.broadcasted_iota(jnp.int32, block.shape, 1) < LANES // 2
    zero = jnp.zeros_like(block)
    return jnp.concatenate([jnp.where(first, block, zero), jnp.where(first, zero, block)], axis=0)


def flipped(block):
    return block.astype(F32).T.astype(BF16)


def band_mask(low, high, start_row, size):
    count = high - low
    key = lax.broadcasted_iota(jnp.int32, (count, 2 * size), 0) + low
    query = lax.broadcasted_iota(jnp.int32, (count, 2 * size), 1) % size + (high - size)
    return (key >= start_row) & (key <= query)


def attend_kernel(
    ctx_size, table, seq_ref, qkv_ref, start_ref, out_ref, lse_ref, held, query_t, value_t, mixed
):
    length = held.shape[0]
    half = length // (2 * ctx_size)
    size = LANES
    blocks = length // size
    reach = blocks // 2
    to_places(table, ctx_size, half, qkv_ref, held)
    for block in range(blocks):
        span = slice(block * size, (block + 1) * size)
        query_t[:, span] = (held[span, 0:LANES].astype(F32) * 0.125).T.astype(BF16)
        value_t[:, span] = flipped(held[span, 2 * LANES :])
    for block in range(blocks):
        low = max(0, block - reach) * size
        high = (block + 1) * size
        span = slice(block * size, high)
        scores = dot(held[low:high, LANES : 2 * LANES], both_heads(query_t[:, span]))
        start_row = start_ref[0, :, span]
        start_row = jnp.concatenate([start_row, start_row], axis=1)
        scores = jnp.where(band_mask(low, high, start_row, size), scores, MASKED)
        top = jnp.max(scores, axis=0, keepdims=True)
        weights = jnp.exp(scores - top)
        total = jnp.sum(weights, axis=0, keepdims=True)
        lse = top + jnp.log(total)
        probs = (weights * (1.0 / total)).astype(BF16)
        lse_ref[0, 0:1, span] = lse[:, :size]
        lse_ref[0, 1:2, span] = lse[:, size:]
        mixed_t = dot(value_t[:, low:high], probs)
        both = jnp.concatenate(
            [mixed_t[0 : LANES // 2, :size], mixed_t[LANES // 2 :, size:]], axis=0
        )
        mixed[span, :] = both.T.astype(BF16)
    for device in range(ctx_size):
        pair = table[device]
        early = pl.multiple_of(pair * half, half)
        later = pl.multiple_of((2 * ctx_size - 1 - pair) * half, half)
        out_ref[device, 0, 0:half, :] = mixed[pl.ds(early, half), :]
        out_ref[device, 0, half : 2 * half, :] = mixed[pl.ds(later, half), :]


def attend(table, unit_seqs, qkv, starts):
    ctx_size, units, rows, width = qkv.shape
    length = ctx_size * rows
    return pl.pallas_call(
        functools.partial(attend_kernel, ctx_size),
        grid_spec=pltpu.PrefetchScalarGridSpec(
            num_scalar_prefetch=2,
            grid=(units,),
            in_specs=[
                pl.BlockSpec((ctx_size, 1, rows, width), lambda u, t, s: (0, u, 0, 0)),
                pl.BlockSpec((1, 1, length), lambda u, t, s: (s[u], 0, 0)),
            ],
            out_specs=[
                pl.BlockSpec((ctx_size, 1, rows, LANES), lambda u, t, s: (0, u, 0, 0)),
                pl.BlockSpec((1, 2, length), lambda u, t, s: (u, 0, 0)),
            ],
            scratch_shapes=[
                pltpu.VMEM((length, width), BF16),
                pltpu.VMEM((LANES, length), BF16),
                pltpu.VMEM((LANES, length), BF16),
                pltpu.VMEM((length, LANES), BF16),
            ],
        ),
        out_shape=[
            jax.ShapeDtypeStruct((ctx_size, units, rows, LANES), BF16),
            jax.ShapeDtypeStruct((units, 2, length), F32),
        ],
        compiler_params=params(),
        cost_estimate=cost(units * length * length * 256, qkv.size * 4),
        name="attend",
    )(table, unit_seqs, qkv, starts)


def attend_back_kernel(
    ctx_size,
    table,
    seq_ref,
    qkv_ref,
    grad_ref,
    start_ref,
    lse_ref,
    out_ref,
    held,
    grad,
    query_t,
    key_t,
    grad_t,
    query_grad,
    key_grad,
    value_grad,
):
    length = held.shape[0]
    half = length // (2 * ctx_size)
    size = LANES
    blocks = length // size
    reach = blocks // 2
    to_places(table, ctx_size, half, qkv_ref, held)
    to_places(table, ctx_size, half, grad_ref, grad)
    for block in range(blocks):
        span = slice(block * size, (block + 1) * size)
        scaled = (held[span, 0:LANES].astype(F32) * 0.125).astype(BF16)
        held[span, 0:LANES] = scaled
        query_t[:, span] = flipped(scaled)
        key_t[:, span] = flipped(held[span, LANES : 2 * LANES])
        grad_t[:, span] = flipped(grad[span, :])
    for block in range(blocks):
        low = max(0, block - reach) * size
        high = (block + 1) * size
        span = slice(block * size, high)
        scores = dot(held[low:high, LANES : 2 * LANES], both_heads(query_t[:, span]))
        start_row = start_ref[0, :, span]
        start_row = jnp.concatenate([start_row, start_row], axis=1)
        scores = jnp.where(band_mask(low, high, start_row, size), scores, MASKED)
        lse = jnp.concatenate([lse_ref[0, 0:1, span], lse_ref[0, 1:2, span]], axis=1)
        probs = jnp.exp(scores - lse)
        prob_grad = dot(held[low:high, 2 * LANES :], both_heads(grad_t[:, span]))
        delta = jnp.sum(probs * prob_grad, axis=0, keepdims=True)
        score_grad = (probs * (prob_grad - delta)).astype(BF16)
        probs = probs.astype(BF16)
        new_value = dot(probs, stacked_heads(grad[span, :]))
        new_key = dot(score_grad, stacked_heads(held[span, 0:LANES]))
        if low < high - size:
            value_grad[low : high - size, :] += new_value[: high - size - low]
            key_grad[low : high - size, :] += new_key[: high - size - low]
        value_grad[span, :] = new_value[high - size - low :]
        key_grad[span, :] = new_key[high - size - low :]
        query_t_grad = dot(key_t[:, low:high], score_grad)
        both = jnp.concatenate(
            [query_t_grad[0 : LANES // 2, :size], query_t_grad[LANES // 2 :, size:]], axis=0
        )
        query_grad[span, :] = (both.T * 0.125).astype(BF16)
    for device in range(ctx_size):
        pair = table[device]
        early = pl.multiple_of(pair * half, half)
        later = pl.multiple_of((2 * ctx_size - 1 - pair) * half, half)
        for place, source in ((0, early), (half, later)):
            rows = pl.ds(source, half)
            out_ref[device, 0, place : place + half, 0:LANES] = query_grad[rows, :]
            out_ref[device, 0, place : place + half, LANES : 2 * LANES] = key_grad[
                rows, :
            ].astype(BF16)
            out_ref[device, 0, place : place + half, 2 * LANES :] = value_grad[rows, :].astype(
                BF16
            )


def attend_back(table, unit_seqs, qkv, grad, starts, lse):
    ctx_size, units, rows, width = qkv.shape
    length = ctx_size * rows
    return pl.pallas_call(
        functools.partial(attend_back_kernel, ctx_size),
        grid_spec=pltpu.PrefetchScalarGridSpec(
            num_scalar_prefetch=2,
            grid=(units,),
            in_specs=[
                pl.BlockSpec((ctx_size, 1, rows, width), lambda u, t, s: (0, u, 0, 0)),
                pl.BlockSpec((ctx_size, 1, rows, LANES), lambda u, t, s: (0, u, 0, 0)),
                pl.BlockSpec((1, 1, length), lambda u, t, s: (s[u], 0, 0)),
                pl.BlockSpec((1, 2, length), lambda u, t, s: (u, 0, 0)),
            ],
            out_specs=pl.BlockSpec((ctx_size, 1, rows, width), lambda u, t, s: (0, u, 0, 0)),
            scratch_shapes=[
                pltpu.VMEM((length, width), BF16),
                pltpu.VMEM((length, LANES), BF16),
                pltpu.VMEM((LANES, length), BF16),
                pltpu.VMEM((LANES, length), BF16),
                pltpu.VMEM((LANES, length), BF16),
                pltpu.VMEM((length, LANES), BF16),
                pltpu.VMEM((length, LANES), F32),
                pltpu.VMEM((length, LANES), F32),
            ],
        ),
        out_shape=jax.ShapeDtypeStruct(qkv.shape, BF16),
        compiler_params=params(),
        cost_estimate=cost(units * length * length * 640, qkv.size * 6),
        name="attend_back",
    )(table, unit_seqs, qkv, grad, starts, lse)


def branch_kernel(off_ref, att_ref, x_ref, v_ref, *refs):
    residual_ref, h2_ref, mixed_ref, weight = refs[-4:]
    pairs = att_ref.shape[0]
    tokens = x_ref.shape[0]
    for pair in range(pairs):
        mixed_ref[:, pair * LANES : (pair + 1) * LANES] = att_ref[pair].reshape(tokens, LANES)
    place_columns(weight, off_ref, refs[:-4])
    residual = (
        x_ref[...].astype(F32) + dot(mixed_ref[...], weight[...]) + v_ref[V_BO : V_BO + 1, :]
    )
    residual_ref[...] = residual
    hat, _ = norm_stats(residual)
    h2_ref[...] = (hat * v_ref[V_G2 : V_G2 + 1, :] + v_ref[V_B2 : V_B2 + 1, :]).astype(BF16)


def branch(att, x, vectors, parts):
    arrays, offsets = split_parts(parts)
    tokens, features = x.shape
    return pl.pallas_call(
        branch_kernel,
        grid_spec=pltpu.PrefetchScalarGridSpec(
            num_scalar_prefetch=1,
            grid=(1,),
            in_specs=[whole(att.shape), whole(x.shape), whole(vectors.shape)]
            + [whole(array.shape) for array in arrays],
            out_specs=[whole(x.shape)] * 3,
            scratch_shapes=[pltpu.VMEM((features, features), BF16)],
        ),
        out_shape=[
            jax.ShapeDtypeStruct(x.shape, F32),
            jax.ShapeDtypeStruct(x.shape, BF16),
            jax.ShapeDtypeStruct(x.shape, BF16),
        ],
        compiler_params=params(),
        cost_estimate=cost(2 * tokens * features * features, 2 * features * features),
        name="branch",
    )(offsets, att, x, vectors, *arrays)


def ffn_kernel(
    expand_count,
    shrink_count,
    steps,
    sc_ref,
    residual_ref,
    h2_ref,
    og_ref,
    v_ref,
    eb_ref,
    *refs,
):
    expand_parts = refs[:expand_count]
    shrink_parts = refs[expand_count : expand_count + shrink_count]
    (
        out_ref,
        dh2_ref,
        send_s,
        keep_s,
        send_e,
        keep_e,
        eb_grad_ref,
        sb_grad_ref,
        expand,
        shrink,
        total,
        back,
        h2_t,
    ) = refs[expand_count + shrink_count :]
    step = pl.program_id(0)
    y_index = sc_ref[0]
    low_label = sc_ref[2]
    expand_offsets = [sc_ref[3 + i] for i in range(expand_count)]
    shrink_offsets = [sc_ref[3 + expand_count + i] for i in range(shrink_count)]

    @pl.when(step == 0)
    def _():
        total[...] = residual_ref[...] + v_ref[V_BS : V_BS + 1, :]
        back[...] = jnp.zeros_like(back)
        h2_t[...] = h2_ref[...].astype(F32).T.astype(BF16)
        sb_grad_ref[...] = jnp.sum(og_ref[...].astype(F32), axis=0, keepdims=True)

    place_rows(expand, expand_offsets, expand_parts)
    place_columns(shrink, shrink_offsets, shrink_parts)
    width = expand.shape[1]
    pre = dot(h2_ref[...], expand[...]) + eb_ref[...]
    root = math.sqrt(2.0 / math.pi)
    square = pre * pre
    curve = jnp.tanh(root * (pre + 0.044715 * (square * pre)))
    slope = 0.5 * (1.0 + curve)
    active = (pre * slope).astype(BF16)
    slope = slope + (0.5 * root) * pre * (1.0 - curve * curve) * (1.0 + 0.134145 * square)
    total[...] += dot(active, shrink[...])
    dpre = (dot_nt(og_ref[...], shrink[...]) * slope).astype(BF16)
    eb_grad_ref[...] = jnp.sum(dpre.astype(F32), axis=0, keepdims=True)
    back[...] += dot_nt(dpre, expand[...])
    shrink_grad = dot_tn(active, og_ref[...]).astype(BF16)
    expand_grad = dot(h2_t[...], dpre).astype(BF16)

    def store(target_s, target_e):
        fsdp_size, _, subs, rows, columns = target_s.shape
        for part in range(fsdp_size):
            for sub in range(subs):
                here = slice(sub * rows, (sub + 1) * rows)
                there = slice(part * columns, (part + 1) * columns)
                target_s[part ^ y_index, 0, sub ^ low_label] = shrink_grad[here, there]
                target_e[part ^ y_index, 0, sub ^ low_label] = expand_grad[there, here]

    @pl.when(step < steps // 2)
    def _():
        store(send_s, send_e)

    @pl.when(step >= steps // 2)
    def _():
        store(keep_s, keep_e)

    @pl.when(step == steps - 1)
    def _():
        out_ref[...] = total[...].astype(BF16)
        dh2_ref[...] = back[...]


def feed_forward(
    residual, h2, og, vectors, expand_bias, expand_parts, shrink_parts, sizes, y_index, label
):
    fsdp_size, ctx_size = sizes
    expand_arrays, expand_offsets = split_parts(expand_parts)
    shrink_arrays, shrink_offsets = split_parts(shrink_parts)
    tokens, features = h2.shape
    hidden = expand_arrays[0].shape[1]
    rows = hidden // ctx_size
    columns = features // fsdp_size
    width = 512
    subs = width // rows
    steps = hidden // width
    high_label = label // subs
    low_label = label % subs
    scalars = jnp.concatenate(
        [
            jnp.stack([y_index, high_label, low_label]).astype(jnp.int32),
            expand_offsets,
            shrink_offsets,
        ]
    )
    middle = steps // 2

    def chunk(step, sc):
        return (step ^ middle) ^ sc[1]

    grad_s = (fsdp_size, middle, subs, rows, columns)
    grad_e = (fsdp_size, middle, subs, columns, rows)

    def send_map(step, sc):
        return (0, jnp.minimum(step, middle - 1), 0, 0, 0)

    def keep_map(step, sc):
        return (0, jnp.maximum(step - middle, 0), 0, 0, 0)

    def block(shape, index):
        return pl.BlockSpec((shape[0], 1) + shape[2:], index)

    return pl.pallas_call(
        functools.partial(ffn_kernel, len(expand_arrays), len(shrink_arrays), steps),
        grid_spec=pltpu.PrefetchScalarGridSpec(
            num_scalar_prefetch=1,
            grid=(steps,),
            in_specs=[
                whole(residual.shape),
                whole(h2.shape),
                whole(og.shape),
                whole(vectors.shape),
                pl.BlockSpec((1, width), lambda s, sc: (0, chunk(s, sc))),
            ]
            + [
                pl.BlockSpec((array.shape[0], width), lambda s, sc: (0, chunk(s, sc)))
                for array in expand_arrays
            ]
            + [
                pl.BlockSpec((width, array.shape[1]), lambda s, sc: (chunk(s, sc), 0))
                for array in shrink_arrays
            ],
            out_specs=[
                whole(h2.shape),
                whole(h2.shape),
                block(grad_s, send_map),
                block(grad_s, keep_map),
                block(grad_e, send_map),
                block(grad_e, keep_map),
                pl.BlockSpec((1, width), lambda s, sc: (0, chunk(s, sc))),
                whole((1, features)),
            ],
            scratch_shapes=[
                pltpu.VMEM((features, width), BF16),
                pltpu.VMEM((width, features), BF16),
                pltpu.VMEM((tokens, features), F32),
                pltpu.VMEM((tokens, features), F32),
                pltpu.VMEM((features, tokens), BF16),
            ],
        ),
        out_shape=[
            jax.ShapeDtypeStruct(h2.shape, BF16),
            jax.ShapeDtypeStruct(h2.shape, F32),
            jax.ShapeDtypeStruct(grad_s, BF16),
            jax.ShapeDtypeStruct(grad_s, BF16),
            jax.ShapeDtypeStruct(grad_e, BF16),
            jax.ShapeDtypeStruct(grad_e, BF16),
            jax.ShapeDtypeStruct((1, hidden), F32),
            jax.ShapeDtypeStruct((1, features), F32),
        ],
        compiler_params=params(),
        cost_estimate=cost(12 * tokens * features * hidden, 8 * features * hidden),
        name="feed_forward",
    )(scalars, residual, h2, og, vectors, expand_bias, *expand_arrays, *shrink_arrays)


def branch_back_kernel(
    part_count, seqs, rows, sc_ref, dh2_ref, residual_ref, og_ref, mixed_ref, v_ref, *refs
):
    parts = refs[:part_count]
    dres_ref, dmixed_ref, grad_ref, vec_ref, weight, rounded = refs[part_count:]
    y_index = sc_ref[0]
    label = sc_ref[1]
    place_columns(weight, [sc_ref[2 + i] for i in range(part_count)], parts)
    hat, rate = norm_stats(residual_ref[...])
    dh2 = dh2_ref[...]
    scaled = dh2 * v_ref[V_G2 : V_G2 + 1, :]
    first = jnp.mean(scaled, axis=-1, keepdims=True)
    second = jnp.mean(scaled * hat, axis=-1, keepdims=True)
    dres = og_ref[...].astype(F32) + rate * (scaled - first - hat * second)
    dres_ref[...] = dres
    rounded[...] = dres.astype(BF16)
    vec_ref[0:1, :] = jnp.sum(dh2 * hat, axis=0, keepdims=True)
    vec_ref[1:2, :] = jnp.sum(dh2, axis=0, keepdims=True)
    vec_ref[2:3, :] = jnp.sum(rounded[...].astype(F32), axis=0, keepdims=True)
    vec_ref[3:, :] = jnp.zeros((vec_ref.shape[0] - 3, vec_ref.shape[1]), F32)
    dmixed = dot_nt(rounded[...], weight[...]).astype(BF16)
    for pair in range(dmixed_ref.shape[0]):
        dmixed_ref[pair] = dmixed[:, pair * LANES : (pair + 1) * LANES].reshape(seqs, rows, LANES)
    _, fsdp_size, count, size, columns = grad_ref.shape
    grad = dot_tn(mixed_ref[...], rounded[...]).astype(BF16)
    for number in range(2 * count):
        place = number ^ label
        for part in range(fsdp_size):
            grad_ref[place // count, part ^ y_index, place % count] = grad[
                number * size : (number + 1) * size, part * columns : (part + 1) * columns
            ]


def branch_back(dh2, residual, og, mixed, vectors, parts, sizes, y_index, label, seqs, rows):
    fsdp_size, ctx_size = sizes
    arrays, offsets = split_parts(parts)
    tokens, features = dh2.shape
    pairs = features // LANES
    grad = (2, fsdp_size, ctx_size // 2, features // ctx_size, features // fsdp_size)
    scalars = jnp.concatenate([jnp.stack([y_index, label]).astype(jnp.int32), offsets])
    full = whole(dh2.shape)
    return pl.pallas_call(
        functools.partial(branch_back_kernel, len(arrays), seqs, rows),
        grid_spec=pltpu.PrefetchScalarGridSpec(
            num_scalar_prefetch=1,
            grid=(1,),
            in_specs=[full, full, full, full, whole(vectors.shape)]
            + [whole(array.shape) for array in arrays],
            out_specs=[
                full,
                whole((pairs, seqs, rows, LANES)),
                whole(grad),
                whole((8, features)),
            ],
            scratch_shapes=[
                pltpu.VMEM((features, features), BF16),
                pltpu.VMEM((tokens, features), BF16),
            ],
        ),
        out_shape=[
            jax.ShapeDtypeStruct(dh2.shape, F32),
            jax.ShapeDtypeStruct((pairs, seqs, rows, LANES), BF16),
            jax.ShapeDtypeStruct(grad, BF16),
            jax.ShapeDtypeStruct((8, features), F32),
        ],
        compiler_params=params(),
        cost_estimate=cost(4 * tokens * features * features, 8 * features * features),
        name="branch_back",
    )(scalars, dh2, residual, og, mixed, vectors, *arrays)


def input_grad_kernel(group_ref, h_ref, d_ref, out_ref):
    left = h_ref[...].reshape(-1, h_ref.shape[-1])
    right = d_ref[...].reshape(-1, d_ref.shape[-1])
    out_ref[...] = dot_tn(left, right).astype(BF16)


def input_weight_terms(gathered, dqkv, group):
    ctx_size, units, rows, width = dqkv.shape
    features = gathered.shape[-1]
    block = 2 * LANES
    return pl.pallas_call(
        input_grad_kernel,
        grid_spec=pltpu.PrefetchScalarGridSpec(
            num_scalar_prefetch=1,
            grid=(features // block,),
            in_specs=[
                pl.BlockSpec((ctx_size, units, rows, block), lambda g, s: (0, s[0], 0, g)),
                whole(dqkv.shape),
            ],
            out_specs=pl.BlockSpec((block, width), lambda g, s: (g, 0)),
        ),
        out_shape=jax.ShapeDtypeStruct((features, width), BF16),
        compiler_params=params(),
        cost_estimate=cost(2 * dqkv.size * features, 2 * dqkv.size + dqkv.size * features // 192),
        name="input_weight_terms",
    )(group, gathered, dqkv)


def entry_back_kernel(part_count, groups, off_ref, d_ref, x_ref, dres_ref, v_ref, *refs):
    parts = refs[: 3 * part_count]
    out_ref, vec_ref, weight, back = refs[3 * part_count :]
    group = pl.program_id(0)
    tokens = x_ref.shape[0]
    width = weight.shape[-1]

    @pl.when(group == 0)
    def _():
        back[...] = jnp.zeros_like(back)

    for kind in range(3):
        place_rows(
            weight.at[kind], off_ref, parts[kind * part_count : (kind + 1) * part_count]
        )
        lanes = slice(kind * LANES, (kind + 1) * LANES)
        value = jnp.concatenate(
            [d_ref[pair, :, :, lanes].reshape(tokens, LANES) for pair in range(d_ref.shape[0])],
            axis=1,
        )
        back[...] += dot_nt(value, weight[kind])
        if kind != 1:
            row = 2 if kind == 0 else 3
            start = pl.multiple_of(group * width, LANES)
            vec_ref[row : row + 1, pl.ds(start, width)] = jnp.sum(
                value.astype(F32), axis=0, keepdims=True
            )

    @pl.when(group == groups - 1)
    def _():
        hat, rate = norm_stats(x_ref[...].astype(F32))
        dh1 = back[...]
        scaled = dh1 * v_ref[V_G1 : V_G1 + 1, :]
        first = jnp.mean(scaled, axis=-1, keepdims=True)
        second = jnp.mean(scaled * hat, axis=-1, keepdims=True)
        out_ref[...] = dres_ref[...] + rate * (scaled - first - hat * second)
        vec_ref[0:1, :] = jnp.sum(dh1 * hat, axis=0, keepdims=True)
        vec_ref[1:2, :] = jnp.sum(dh1, axis=0, keepdims=True)


def entry_back(dqkv, x, dres, vectors, parts):
    arrays, offsets = split_parts(parts)
    tokens, features = x.shape
    pairs, seqs, rows, _ = dqkv.shape
    width = 2 * LANES
    groups = features // width
    specs = []
    operands = []
    for kind in range(3):
        for array in arrays:
            specs.append(
                pl.BlockSpec((array.shape[0], width), lambda g, o, k=kind: (0, k * groups + g))
            )
            operands.append(array)
    return pl.pallas_call(
        functools.partial(entry_back_kernel, len(arrays), groups),
        grid_spec=pltpu.PrefetchScalarGridSpec(
            num_scalar_prefetch=1,
            grid=(groups,),
            in_specs=[
                pl.BlockSpec((2, seqs, rows, 3 * LANES), lambda g, o: (g, 0, 0, 0)),
                whole(x.shape),
                whole(x.shape),
                whole(vectors.shape),
            ]
            + specs,
            out_specs=[whole(x.shape), whole((4, features))],
            scratch_shapes=[
                pltpu.VMEM((3, features, width), BF16),
                pltpu.VMEM((tokens, features), F32),
            ],
        ),
        out_shape=[
            jax.ShapeDtypeStruct(x.shape, F32),
            jax.ShapeDtypeStruct((4, features), F32),
        ],
        compiler_params=params(),
        cost_estimate=cost(6 * tokens * features * features, 6 * features * features),
        name="entry_back",
    )(offsets, dqkv, x, dres, vectors, *operands)


def scatter_sum(send, keep, sizes):
    fsdp_size, ctx_size = sizes
    term = keep + swap_bit(send, "ctx", ctx_size, 0)
    term = term.reshape((fsdp_size, ctx_size // 2) + term.shape[-2:])
    for bit in reversed(range(bits_of(fsdp_size))):
        middle = term.shape[0] // 2
        term = term[:middle] + swap_bit(term[middle:], "fsdp", fsdp_size, bit)
    term = term[0]
    for bit in range(1, bits_of(ctx_size)):
        middle = term.shape[0] // 2
        term = term[:middle] + swap_bit(term[middle:], "ctx", ctx_size, bit)
    return term


def spread(term, ctx_size):
    for bit in reversed(range(1, bits_of(ctx_size))):
        term = jnp.concatenate([term, swap_bit(term, "ctx", ctx_size, bit)], axis=0)
    return term, swap_bit(term, "ctx", ctx_size, 0)


def finish_rows_kernel(half, label_ref, near_ref, far_ref, out_ref):
    number = pl.program_id(0)

    @pl.when(number < half)
    def _():
        out_ref[...] = near_ref[0].astype(F32)

    @pl.when(number >= half)
    def _():
        out_ref[...] = far_ref[0].astype(F32)


def finish(near, far, label, dim):
    half, rows, columns = near.shape
    count = 2 * half
    if dim == 0:
        shape = (count * rows, columns)
        out_spec = pl.BlockSpec((rows, columns), lambda n, k: (n ^ k[0], 0))
    else:
        shape = (rows, count * columns)
        out_spec = pl.BlockSpec((rows, columns), lambda n, k: (0, n ^ k[0]))
    return pl.pallas_call(
        functools.partial(finish_rows_kernel, half),
        grid_spec=pltpu.PrefetchScalarGridSpec(
            num_scalar_prefetch=1,
            grid=(count,),
            in_specs=[
                pl.BlockSpec((1, rows, columns), lambda n, k: (jnp.minimum(n, half - 1), 0, 0)),
                pl.BlockSpec((1, rows, columns), lambda n, k: (jnp.maximum(n - half, 0), 0, 0)),
            ],
            out_specs=out_spec,
        ),
        out_shape=jax.ShapeDtypeStruct(shape, F32),
        compiler_params=params(),
        cost_estimate=cost(0, near.size * 12),
        name="finish",
    )(label.reshape(1), near, far)


def finish_input_kernel(low_bits, table, near_ref, far_ref, out_ref):
    half, rows, _ = near_ref.shape
    for number in range(2 * half):
        owner = table[number]
        place = owner & ((1 << low_bits) - 1)
        pair = owner >> low_bits
        source = near_ref[number] if number < half else far_ref[number - half]
        out_ref[
            pl.ds(pl.multiple_of(place * rows, rows), rows),
            pl.ds(pl.multiple_of(pair * LANES, LANES), LANES),
        ] = source.astype(F32)


def finish_input(near, far, table, low_bits, features):
    half, rows, _ = near.shape
    block = pl.BlockSpec((half, rows, LANES), lambda j, t: (0, 0, j))
    height = rows << low_bits
    return pl.pallas_call(
        functools.partial(finish_input_kernel, low_bits),
        grid_spec=pltpu.PrefetchScalarGridSpec(
            num_scalar_prefetch=1,
            grid=(3,),
            in_specs=[block, block],
            out_specs=pl.BlockSpec((height, features), lambda j, t: (0, j)),
        ),
        out_shape=jax.ShapeDtypeStruct((height, 3 * features), F32),
        compiler_params=params(),
        cost_estimate=cost(0, near.size * 12),
        name="finish_input",
    )(table, near, far)


def input_scatter_sum(term, low_bits, sizes, y_index, c_index):
    fsdp_size, ctx_size = sizes
    rows = term.shape[0] // (fsdp_size << low_bits)
    width = term.shape[1]
    term = term.reshape(fsdp_size, 1 << low_bits, rows, width)
    for bit in reversed(range(low_bits)):
        mine = (c_index >> bit) & 1
        term = term.reshape(fsdp_size, 2, 1 << bit, rows, width)
        send = lax.dynamic_index_in_dim(term, 1 - mine, 1, keepdims=False)
        keep = lax.dynamic_index_in_dim(term, mine, 1, keepdims=False)
        term = keep + swap_bit(send, "ctx", ctx_size, bit)
    term = term.reshape(fsdp_size, rows, width)
    for bit in reversed(range(bits_of(fsdp_size))):
        mine = (y_index >> bit) & 1
        term = term.reshape(2, 1 << bit, rows, width)
        send = lax.dynamic_index_in_dim(term, 1 - mine, 0, keepdims=False)
        keep = lax.dynamic_index_in_dim(term, mine, 0, keepdims=False)
        term = keep + swap_bit(send, "fsdp", fsdp_size, bit)
    return term.reshape(1, rows, width)


def sum_everywhere(value, sizes):
    fsdp_size, ctx_size = sizes
    for bit in range(bits_of(ctx_size)):
        value = value + swap_bit(value, "ctx", ctx_size, bit)
    for bit in range(bits_of(fsdp_size)):
        value = value + swap_bit(value, "fsdp", fsdp_size, bit)
    return value


def body(
    sizes,
    layer_input,
    output_grad,
    segments,
    assignment,
    first_gain,
    first_bias,
    input_weight,
    query_bias,
    value_bias,
    output_weight,
    output_bias,
    second_gain,
    second_bias,
    expand_weight,
    expand_bias,
    shrink_weight,
    shrink_bias,
):
    fsdp_size, ctx_size = sizes
    seqs, rows, features = layer_input.shape
    tokens = seqs * rows
    hidden = expand_weight.shape[1]
    pairs = features // LANES
    units = seqs * pairs // ctx_size
    y_index = lax.axis_index("fsdp").astype(jnp.int32)
    c_index = lax.axis_index("ctx").astype(jnp.int32)
    label = reverse_bits(c_index, bits_of(ctx_size))

    small = jnp.concatenate(
        [
            first_gain,
            first_bias,
            query_bias,
            value_bias,
            output_bias,
            second_gain,
            second_bias,
            shrink_bias,
            expand_bias,
        ]
    )
    small = lax.all_gather(small, "fsdp", axis=0).astype(F32)
    vectors = (
        small[:, : 8 * (features // fsdp_size)]
        .reshape(fsdp_size, 8, features // fsdp_size)
        .transpose(1, 0, 2)
        .reshape(8, features)
    )
    expand_vector = small[:, 8 * (features // fsdp_size) :].reshape(1, hidden)

    def parts_of(weight, dim, bits):
        return gather_parts(weight, dim, fsdp_size, ctx_size, y_index, c_index, bits)

    input_parts = parts_of(input_weight, 0, (0,))
    output_parts = parts_of(output_weight, 1, (0,))
    expand_parts = parts_of(expand_weight, 0, (0,))
    shrink_parts = parts_of(shrink_weight, 1, (0,))

    starts = jnp.sum(
        (segments[:, None, :] < segments[:, :, None]).astype(jnp.int32), axis=-1
    )[:, None, :]
    unit_seqs = (c_index * units + jnp.arange(units, dtype=jnp.int32)) % seqs

    x = layer_input.reshape(tokens, features)
    og = output_grad.reshape(tokens, features)
    h1 = first_norm(x, vectors)
    qkv = project(h1, vectors, input_parts, seqs, rows)
    qkv = qkv.reshape(ctx_size, units, rows, 3 * LANES)
    qkv = lax.all_to_all(qkv, "ctx", 0, 0, tiled=True)
    h1_late, qkv = lax.optimization_barrier((h1, qkv))
    gathered = lax.all_gather(h1_late.reshape(seqs, rows, features), "ctx", axis=0)
    att, lse = attend(assignment, unit_seqs, qkv, starts)
    att = lax.all_to_all(att, "ctx", 0, 0, tiled=True).reshape(pairs, seqs, rows, LANES)
    residual, h2, mixed = branch(att, x, vectors, output_parts)
    out, dh2, send_s, keep_s, send_e, keep_e, eb_grad, sb_grad = feed_forward(
        residual, h2, og, vectors, expand_vector, expand_parts, shrink_parts, sizes, y_index, label
    )
    dres, dmixed, output_terms, vec_two = branch_back(
        dh2, residual, og, mixed, vectors, output_parts, sizes, y_index, label, seqs, rows
    )
    dmixed = dmixed.reshape(ctx_size, units, rows, LANES)
    dmixed = lax.all_to_all(dmixed, "ctx", 0, 0, tiled=True)
    dqkv = attend_back(assignment, unit_seqs, qkv, dmixed, starts, lse)
    group = ((c_index * units) % seqs) // units
    input_terms = input_weight_terms(gathered, dqkv, group.reshape(1))
    dqkv = lax.all_to_all(dqkv, "ctx", 0, 0, tiled=True).reshape(pairs, seqs, rows, 3 * LANES)
    input_grad, vec_one = entry_back(dqkv, x, dres, vectors, input_parts)

    shrink_near, shrink_far = spread(scatter_sum(send_s, keep_s, sizes), ctx_size)
    expand_near, expand_far = spread(scatter_sum(send_e, keep_e, sizes), ctx_size)
    output_near, output_far = spread(
        scatter_sum(output_terms[1], output_terms[0], sizes), ctx_size
    )
    low_bits = bits_of(ctx_size // pairs)
    input_near, input_far = spread(
        input_scatter_sum(input_terms, low_bits, sizes, y_index, c_index), ctx_size
    )
    owners = reverse_bits(
        jnp.arange(ctx_size, dtype=jnp.int32) ^ label, bits_of(ctx_size)
    )
    shrink_grad = finish(shrink_near, shrink_far, label, 0)
    expand_grad = finish(expand_near, expand_far, label, 1)
    output_grad_w = finish(output_near, output_far, label, 0)
    input_grad_w = finish_input(input_near, input_far, owners, low_bits, features)

    early = jnp.concatenate([vec_two[:3], sb_grad, eb_grad.reshape(-1, features)], axis=0)
    early = sum_everywhere(early, sizes)
    late = sum_everywhere(vec_one, sizes)
    part = features // fsdp_size

    def own(vector):
        return lax.dynamic_slice_in_dim(vector, y_index * (vector.shape[0] // fsdp_size), vector.shape[0] // fsdp_size, 0)

    return (
        out.reshape(seqs, rows, features),
        input_grad.reshape(seqs, rows, features),
        own(late[0]),
        own(late[1]),
        input_grad_w,
        own(late[2]),
        own(late[3]),
        output_grad_w,
        own(early[2]),
        own(early[0]),
        own(early[1]),
        expand_grad,
        own(early[4:].reshape(-1)),
        shrink_grad,
        own(early[3]),
    )


def solution(mesh):
    sizes = (mesh.shape["fsdp"], mesh.shape["ctx"])
    return jax.shard_map(
        functools.partial(body, sizes),
        mesh=mesh,
        in_specs=(
            P("fsdp", "ctx", None),
            P("fsdp", "ctx", None),
            P("fsdp", None),
            P(),
            P("fsdp"),
            P("fsdp"),
            P("fsdp", None),
            P("fsdp"),
            P("fsdp"),
            P(None, "fsdp"),
            P("fsdp"),
            P("fsdp"),
            P("fsdp"),
            P("fsdp", None),
            P("fsdp"),
            P(None, "fsdp"),
            P("fsdp"),
        ),
        out_specs=(
            P("fsdp", "ctx", None),
            P("fsdp", "ctx", None),
            P("fsdp"),
            P("fsdp"),
            P("fsdp", None),
            P("fsdp"),
            P("fsdp"),
            P(None, "fsdp"),
            P("fsdp"),
            P("fsdp"),
            P("fsdp"),
            P("fsdp", None),
            P("fsdp"),
            P(None, "fsdp"),
            P("fsdp"),
        ),
        check_vma=False,
    )
```

```python
import functools
import math

import jax
import jax.numpy as jnp
from jax import lax
from jax.experimental import pallas as pl
from jax.experimental.pallas import tpu as pltpu
from jax.sharding import PartitionSpec as P

HEADS = 16
EPSILON = 1e-05
MASKED = -1000000000.0
LANES = 128
WIDTH = 512
MIB = 1024 * 1024
F32 = jnp.float32
BF16 = jnp.bfloat16
TOKEN = jax.ShapeDtypeStruct((8, LANES), F32)

V_G1, V_B1, V_BQ, V_BV, V_BO, V_G2, V_B2, V_BS = range(8)


def bits_of(number):
    return number.bit_length() - 1


def dot(left, right):
    return jnp.dot(left, right, preferred_element_type=F32)


def dot_nt(left, right):
    return lax.dot_general(left, right, (((1,), (1,)), ((), ())), preferred_element_type=F32)


def dot_tn(left, right):
    return lax.dot_general(left, right, (((0,), (0,)), ((), ())), preferred_element_type=F32)


def swap_bit(value, axis, size, bit):
    return lax.ppermute(value, axis, [(i, i ^ (1 << bit)) for i in range(size)])


class Event:
    def __init__(self, keep):
        self.keep = keep


def after(value, event):
    value, event.keep = lax.optimization_barrier((value, event.keep))
    return value


def params(limit_mib=48):
    return pltpu.CompilerParams(vmem_limit_bytes=limit_mib * MIB)


def whole(shape):
    rank = len(shape)
    return pl.BlockSpec(tuple(shape), lambda *_: (0,) * rank)


def cost(flops, moved):
    return pl.CostEstimate(flops=0, bytes_accessed=0, transcendentals=0)


class Gather:
    def __init__(self, weight, dim, place, bits, core=None):
        (fsdp_size, self.ctx_size), y_index, c_index = place
        extent = weight.shape[dim]
        self.bits = bits
        self.stage = 0
        self.two = fsdp_size == 2
        if not self.two:
            self.bits = ()
            self.parts = []
            self.first = lax.all_gather(weight, "fsdp", axis=dim, tiled=True)
            self.offsets = jnp.zeros((1,), jnp.int32)
            self.held = [self.first]
            return
        size = extent >> len(bits)
        mine = jnp.int32(0)
        for number, bit in enumerate(bits):
            mine = mine | (((c_index >> bit) & 1) << number)
        if core is None:
            self.first = lax.dynamic_slice_in_dim(weight, mine * size, size, dim)
        else:
            half = weight.shape[1 - dim] // 2
            begins = (mine * size, core * half) if dim == 0 else (core * half, mine * size)
            self.first = lax.dynamic_slice(
                weight, begins, (size, half) if dim == 0 else (half, size)
            )
        order = y_index * extent + jnp.zeros((1,), jnp.int32)
        numbers = mine ^ jnp.arange(1 << len(bits), dtype=jnp.int32)
        self.offsets = jnp.concatenate([order, (1 - y_index) * extent + numbers * size])
        self.parts = [weight]

    def fetch(self, event=None):
        if not self.two:
            return
        first = self.first if event is None else after(self.first, event)
        self.held = [swap_bit(first, "fsdp", 2, 0)]

    @property
    def keep(self):
        return self.held[-1]

    @keep.setter
    def keep(self, value):
        self.held[-1] = value

    def exchange(self, event=None):
        if self.stage == len(self.bits):
            return
        bit = self.bits[self.stage]
        if event is not None:
            self.keep = after(self.keep, event)
        self.held = self.held + [swap_bit(array, "ctx", self.ctx_size, bit) for array in self.held]
        self.stage += 1

    def result(self):
        return self.parts + self.held, self.offsets


def place_rows(target, offsets, part_refs):
    for number, ref in enumerate(part_refs):
        rows = ref.shape[0]
        target[pl.ds(pl.multiple_of(offsets[number], 32), rows), :] = ref[...]


def place_columns(target, offsets, part_refs):
    for number, ref in enumerate(part_refs):
        columns = ref.shape[1]
        target[:, pl.ds(pl.multiple_of(offsets[number], LANES), columns)] = ref[...]


def norm_stats(values):
    center = values - jnp.mean(values, axis=-1, keepdims=True)
    spread = jnp.mean(center * center, axis=-1, keepdims=True)
    rate = lax.rsqrt(spread + EPSILON)
    return center * rate, rate


def norm_kernel(sc_ref, x_ref, *refs):
    shards = refs[:-3]
    h_ref, v_ref, e_ref = refs[-3:]
    part = v_ref.shape[1] // len(shards)
    hidden = e_ref.shape[1] // len(shards)
    for number, ref in enumerate(shards):
        where = sc_ref[number]
        for row in range(8):
            v_ref[row : row + 1, pl.ds(pl.multiple_of(where * part, LANES), part)] = ref[
                :, row * part : (row + 1) * part
            ].astype(F32)
        e_ref[:, pl.ds(pl.multiple_of(where * hidden, LANES), hidden)] = ref[:, 8 * part :].astype(
            F32
        )
    hat, _ = norm_stats(x_ref[...].astype(F32))
    h_ref[...] = (hat * v_ref[V_G1 : V_G1 + 1, :] + v_ref[V_B1 : V_B1 + 1, :]).astype(BF16)


def first_norm(x, shards, owners, hidden):
    shapes = [
        jax.ShapeDtypeStruct(x.shape, BF16),
        jax.ShapeDtypeStruct((8, x.shape[1]), F32),
        jax.ShapeDtypeStruct((1, hidden), F32),
    ]
    return pl.pallas_call(
        norm_kernel,
        grid_spec=pltpu.PrefetchScalarGridSpec(
            num_scalar_prefetch=1,
            grid=(1,),
            in_specs=[whole(x.shape)] + [whole(shard.shape) for shard in shards],
            out_specs=[whole(shape.shape) for shape in shapes],
        ),
        out_shape=shapes,
        compiler_params=params(),
        cost_estimate=cost(0, 0),
        name="first_norm",
    )(owners, x, *shards)


def qkv_kernel(part_count, seqs, rows, off_ref, h_ref, v_ref, *refs):
    parts = refs[: 3 * part_count]
    out_ref, token_ref, weight = refs[3 * part_count :]
    token_ref[...] = jnp.zeros_like(token_ref)
    group = pl.program_id(0)
    width = weight.shape[-1]
    per = width // LANES
    for kind in range(3):
        place_rows(
            weight.at[kind], off_ref, parts[kind * part_count : (kind + 1) * part_count]
        )
        value = dot(h_ref[...], weight[kind])
        if kind != 1:
            row = V_BQ if kind == 0 else V_BV
            start = pl.multiple_of(group * width, LANES)
            value = value + v_ref[row : row + 1, pl.ds(start, width)]
        value = value.astype(BF16)
        for pair in range(per):
            out_ref[pair, :, :, kind * LANES : (kind + 1) * LANES] = value[
                :, pair * LANES : (pair + 1) * LANES
            ].reshape(seqs, rows, LANES)


def project(h1, vectors, parts, seqs, rows):
    arrays, offsets = parts
    tokens, features = h1.shape
    width = 2 * LANES
    groups = features // width
    pairs = features // LANES
    specs = []
    operands = []
    for kind in range(3):
        for array in arrays:
            specs.append(
                pl.BlockSpec((array.shape[0], width), lambda g, o, k=kind: (0, k * groups + g))
            )
            operands.append(array)
    return pl.pallas_call(
        functools.partial(qkv_kernel, len(arrays), seqs, rows),
        grid_spec=pltpu.PrefetchScalarGridSpec(
            num_scalar_prefetch=1,
            grid=(groups,),
            in_specs=[whole(h1.shape), whole(vectors.shape)] + specs,
            out_specs=[
                pl.BlockSpec((2, seqs, rows, 3 * LANES), lambda g, o: (g, 0, 0, 0)),
                whole(TOKEN.shape),
            ],
            scratch_shapes=[pltpu.VMEM((3, features, width), BF16)],
        ),
        out_shape=[jax.ShapeDtypeStruct((pairs, seqs, rows, 3 * LANES), BF16), TOKEN],
        compiler_params=params(),
        cost_estimate=cost(6 * tokens * features * features, 6 * features * features),
        name="project",
    )(offsets, h1, vectors, *operands)


def to_places(table, ctx_size, half, source, target):
    for device in range(ctx_size):
        pair = table[device]
        early = pl.multiple_of(pair * half, half)
        later = pl.multiple_of((2 * ctx_size - 1 - pair) * half, half)
        target[pl.ds(early, half), :] = source[device, 0, 0:half, :]
        target[pl.ds(later, half), :] = source[device, 0, half : 2 * half, :]


def both_heads(block):
    first = lax.broadcasted_iota(jnp.int32, block.shape, 0) < LANES // 2
    zero = jnp.zeros_like(block)
    return jnp.concatenate([jnp.where(first, block, zero), jnp.where(first, zero, block)], axis=1)


def stacked_heads(block):
    first = lax.broadcasted_iota(jnp.int32, block.shape, 1) < LANES // 2
    zero = jnp.zeros_like(block)
    return jnp.concatenate([jnp.where(first, block, zero), jnp.where(first, zero, block)], axis=0)


def flipped(block):
    return block.astype(F32).T.astype(BF16)


def band_mask(low, high, start_row, size):
    count = high - low
    key = lax.broadcasted_iota(jnp.int32, (count, 2 * size), 0) + low
    query = lax.broadcasted_iota(jnp.int32, (count, 2 * size), 1) % size + (high - size)
    return (key >= start_row) & (key <= query)


def attend_kernel(
    ctx_size, table, seq_ref, qkv_ref, start_ref, out_ref, lse_ref, held, query_t, value_t, mixed
):
    length = held.shape[0]
    half = length // (2 * ctx_size)
    size = LANES
    blocks = length // size
    reach = blocks // 2
    to_places(table, ctx_size, half, qkv_ref, held)
    for block in range(blocks):
        span = slice(block * size, (block + 1) * size)
        query_t[:, span] = (held[span, 0:LANES].astype(F32) * 0.125).T.astype(BF16)
        value_t[:, span] = flipped(held[span, 2 * LANES :])
    for block in range(blocks):
        low = max(0, block - reach) * size
        high = (block + 1) * size
        span = slice(block * size, high)
        scores = dot(held[low:high, LANES : 2 * LANES], both_heads(query_t[:, span]))
        start_row = start_ref[0, :, span]
        start_row = jnp.concatenate([start_row, start_row], axis=1)
        scores = jnp.where(band_mask(low, high, start_row, size), scores, MASKED)
        top = jnp.max(scores, axis=0, keepdims=True)
        weights = jnp.exp(scores - top)
        total = jnp.sum(weights, axis=0, keepdims=True)
        lse = top + jnp.log(total)
        probs = (weights * (1.0 / total)).astype(BF16)
        lse_ref[0, 0:1, span] = lse[:, :size]
        lse_ref[0, 1:2, span] = lse[:, size:]
        mixed_t = dot(value_t[:, low:high], probs)
        both = jnp.concatenate(
            [mixed_t[0 : LANES // 2, :size], mixed_t[LANES // 2 :, size:]], axis=0
        )
        mixed[span, :] = both.T.astype(BF16)
    for device in range(ctx_size):
        pair = table[device]
        early = pl.multiple_of(pair * half, half)
        later = pl.multiple_of((2 * ctx_size - 1 - pair) * half, half)
        out_ref[device, 0, 0:half, :] = mixed[pl.ds(early, half), :]
        out_ref[device, 0, half : 2 * half, :] = mixed[pl.ds(later, half), :]


def attend(table, unit_seqs, qkv, starts):
    ctx_size, units, rows, width = qkv.shape
    length = ctx_size * rows
    return pl.pallas_call(
        functools.partial(attend_kernel, ctx_size),
        grid_spec=pltpu.PrefetchScalarGridSpec(
            num_scalar_prefetch=2,
            grid=(units,),
            in_specs=[
                pl.BlockSpec((ctx_size, 1, rows, width), lambda u, t, s: (0, u, 0, 0)),
                pl.BlockSpec((1, 1, length), lambda u, t, s: (s[u], 0, 0)),
            ],
            out_specs=[
                pl.BlockSpec((ctx_size, 1, rows, LANES), lambda u, t, s: (0, u, 0, 0)),
                pl.BlockSpec((1, 2, length), lambda u, t, s: (u, 0, 0)),
            ],
            scratch_shapes=[
                pltpu.VMEM((length, width), BF16),
                pltpu.VMEM((LANES, length), BF16),
                pltpu.VMEM((LANES, length), BF16),
                pltpu.VMEM((length, LANES), BF16),
            ],
        ),
        out_shape=[
            jax.ShapeDtypeStruct((ctx_size, units, rows, LANES), BF16),
            jax.ShapeDtypeStruct((units, 2, length), F32),
        ],
        compiler_params=params(),
        cost_estimate=cost(units * length * length * 256, qkv.size * 4),
        name="attend",
    )(table, unit_seqs, qkv, starts)


def attend_back_kernel(
    ctx_size,
    table,
    seq_ref,
    qkv_ref,
    grad_ref,
    start_ref,
    lse_ref,
    out_ref,
    token_ref,
    held,
    grad,
    query_t,
    key_t,
    grad_t,
    query_grad,
    key_grad,
    value_grad,
):
    token_ref[...] = jnp.zeros_like(token_ref)
    length = held.shape[0]
    half = length // (2 * ctx_size)
    size = LANES
    blocks = length // size
    reach = blocks // 2
    to_places(table, ctx_size, half, qkv_ref, held)
    to_places(table, ctx_size, half, grad_ref, grad)
    for block in range(blocks):
        span = slice(block * size, (block + 1) * size)
        scaled = (held[span, 0:LANES].astype(F32) * 0.125).astype(BF16)
        held[span, 0:LANES] = scaled
        query_t[:, span] = flipped(scaled)
        key_t[:, span] = flipped(held[span, LANES : 2 * LANES])
        grad_t[:, span] = flipped(grad[span, :])
    for block in range(blocks):
        low = max(0, block - reach) * size
        high = (block + 1) * size
        span = slice(block * size, high)
        scores = dot(held[low:high, LANES : 2 * LANES], both_heads(query_t[:, span]))
        start_row = start_ref[0, :, span]
        start_row = jnp.concatenate([start_row, start_row], axis=1)
        scores = jnp.where(band_mask(low, high, start_row, size), scores, MASKED)
        lse = jnp.concatenate([lse_ref[0, 0:1, span], lse_ref[0, 1:2, span]], axis=1)
        probs = jnp.exp(scores - lse)
        prob_grad = dot(held[low:high, 2 * LANES :], both_heads(grad_t[:, span]))
        delta = jnp.sum(probs * prob_grad, axis=0, keepdims=True)
        score_grad = (probs * (prob_grad - delta)).astype(BF16)
        probs = probs.astype(BF16)
        new_value = dot(probs, stacked_heads(grad[span, :]))
        new_key = dot(score_grad, stacked_heads(held[span, 0:LANES]))
        if low < high - size:
            value_grad[low : high - size, :] += new_value[: high - size - low]
            key_grad[low : high - size, :] += new_key[: high - size - low]
        value_grad[span, :] = new_value[high - size - low :]
        key_grad[span, :] = new_key[high - size - low :]
        query_t_grad = dot(key_t[:, low:high], score_grad)
        both = jnp.concatenate(
            [query_t_grad[0 : LANES // 2, :size], query_t_grad[LANES // 2 :, size:]], axis=0
        )
        query_grad[span, :] = (both.T * 0.125).astype(BF16)
    for device in range(ctx_size):
        pair = table[device]
        early = pl.multiple_of(pair * half, half)
        later = pl.multiple_of((2 * ctx_size - 1 - pair) * half, half)
        for place, source in ((0, early), (half, later)):
            rows = pl.ds(source, half)
            out_ref[device, 0, place : place + half, 0:LANES] = query_grad[rows, :]
            out_ref[device, 0, place : place + half, LANES : 2 * LANES] = key_grad[
                rows, :
            ].astype(BF16)
            out_ref[device, 0, place : place + half, 2 * LANES :] = value_grad[rows, :].astype(
                BF16
            )


def attend_back(table, unit_seqs, qkv, grad, starts, lse):
    ctx_size, units, rows, width = qkv.shape
    length = ctx_size * rows
    return pl.pallas_call(
        functools.partial(attend_back_kernel, ctx_size),
        grid_spec=pltpu.PrefetchScalarGridSpec(
            num_scalar_prefetch=2,
            grid=(units,),
            in_specs=[
                pl.BlockSpec((ctx_size, 1, rows, width), lambda u, t, s: (0, u, 0, 0)),
                pl.BlockSpec((ctx_size, 1, rows, LANES), lambda u, t, s: (0, u, 0, 0)),
                pl.BlockSpec((1, 1, length), lambda u, t, s: (s[u], 0, 0)),
                pl.BlockSpec((1, 2, length), lambda u, t, s: (u, 0, 0)),
            ],
            out_specs=[
                pl.BlockSpec((ctx_size, 1, rows, width), lambda u, t, s: (0, u, 0, 0)),
                whole(TOKEN.shape),
            ],
            scratch_shapes=[
                pltpu.VMEM((length, width), BF16),
                pltpu.VMEM((length, LANES), BF16),
                pltpu.VMEM((LANES, length), BF16),
                pltpu.VMEM((LANES, length), BF16),
                pltpu.VMEM((LANES, length), BF16),
                pltpu.VMEM((length, LANES), BF16),
                pltpu.VMEM((length, LANES), F32),
                pltpu.VMEM((length, LANES), F32),
            ],
        ),
        out_shape=[jax.ShapeDtypeStruct(qkv.shape, BF16), TOKEN],
        compiler_params=params(),
        cost_estimate=cost(units * length * length * 640, qkv.size * 6),
        name="attend_back",
    )(table, unit_seqs, qkv, grad, starts, lse)


def branch_kernel(off_ref, att_ref, x_ref, v_ref, *refs):
    residual_ref, h2_ref, mixed_ref, weight = refs[-4:]
    pairs = att_ref.shape[0]
    tokens = x_ref.shape[0]
    for pair in range(pairs):
        mixed_ref[:, pair * LANES : (pair + 1) * LANES] = att_ref[pair].reshape(tokens, LANES)
    place_columns(weight, off_ref, refs[:-4])
    residual = (
        x_ref[...].astype(F32) + dot(mixed_ref[...], weight[...]) + v_ref[V_BO : V_BO + 1, :]
    )
    residual_ref[...] = residual
    hat, _ = norm_stats(residual)
    h2_ref[...] = (hat * v_ref[V_G2 : V_G2 + 1, :] + v_ref[V_B2 : V_B2 + 1, :]).astype(BF16)


def branch(att, x, vectors, parts):
    arrays, offsets = parts
    tokens, features = x.shape
    return pl.pallas_call(
        branch_kernel,
        grid_spec=pltpu.PrefetchScalarGridSpec(
            num_scalar_prefetch=1,
            grid=(1,),
            in_specs=[whole(att.shape), whole(x.shape), whole(vectors.shape)]
            + [whole(array.shape) for array in arrays],
            out_specs=[whole(x.shape)] * 3,
            scratch_shapes=[pltpu.VMEM((features, features), BF16)],
        ),
        out_shape=[
            jax.ShapeDtypeStruct(x.shape, F32),
            jax.ShapeDtypeStruct(x.shape, BF16),
            jax.ShapeDtypeStruct(x.shape, BF16),
        ],
        compiler_params=params(),
        cost_estimate=cost(2 * tokens * features * features, 2 * features * features),
        name="branch",
    )(offsets, att, x, vectors, *arrays)


def ffn_kernel(
    expand_count,
    shrink_count,
    steps,
    sc_ref,
    residual_ref,
    h2_ref,
    h2_other_ref,
    og_ref,
    og_other_ref,
    v_ref,
    eb_ref,
    *refs,
):
    expand_parts = refs[:expand_count]
    shrink_parts = refs[expand_count : expand_count + shrink_count]
    (
        send_ref,
        keep_ref,
        send_s,
        keep_s,
        send_e,
        keep_e,
        eb_grad_ref,
        sb_grad_ref,
        expand,
        shrink,
        total,
        back,
        h2,
        h2_t,
        og,
    ) = refs[expand_count + shrink_count :]
    step = pl.program_id(0)
    y_index = sc_ref[0]
    low_label = sc_ref[2]
    expand_offsets = [sc_ref[4 + i] for i in range(expand_count)]
    shrink_offsets = [sc_ref[4 + expand_count + i] for i in range(shrink_count)]
    tokens = h2_ref.shape[0]

    @pl.when(step == 0)
    def _():
        total[:tokens] = residual_ref[...] + v_ref[V_BS : V_BS + 1, :]
        total[tokens:] = jnp.zeros_like(residual_ref)
        back[...] = jnp.zeros_like(back)
        h2[:tokens] = h2_ref[...]
        h2[tokens:] = h2_other_ref[...]
        og[:tokens] = og_ref[...]
        og[tokens:] = og_other_ref[...]
        h2_t[...] = h2[...].astype(F32).T.astype(BF16)
        sb_grad_ref[...] = jnp.sum(og_ref[...].astype(F32), axis=0, keepdims=True)

    place_rows(expand, expand_offsets, expand_parts)
    place_columns(shrink, shrink_offsets, shrink_parts)
    pre = dot(h2[...], expand[...]) + eb_ref[...]
    root = math.sqrt(2.0 / math.pi)
    square = pre * pre
    curve = jnp.tanh(root * (pre + 0.044715 * (square * pre)))
    slope = 0.5 * (1.0 + curve)
    active = (pre * slope).astype(BF16)
    slope = slope + (0.5 * root) * pre * (1.0 - curve * curve) * (1.0 + 0.134145 * square)
    total[...] += dot(active, shrink[...])
    dpre = (dot_nt(og[...], shrink[...]) * slope).astype(BF16)
    eb_grad_ref[...] = jnp.sum(dpre.astype(F32), axis=0, keepdims=True)
    back[...] += dot_nt(dpre, expand[...])
    shrink_grad = dot_tn(active, og[...]).astype(BF16)
    expand_grad = dot(h2_t[...], dpre).astype(BF16)

    fsdp_half, _, subs, rows, columns = send_s.shape
    for part in range(2 * fsdp_half):
        there = slice(part * columns, (part + 1) * columns)
        place = part ^ y_index

        def store_s(target, there=there, place=place):
            for sub in range(subs):
                here = slice(sub * rows, (sub + 1) * rows)
                target[place & (fsdp_half - 1), 0, sub ^ low_label] = shrink_grad[here, there]

        pl.when(place < fsdp_half)(functools.partial(store_s, keep_s))
        pl.when(place >= fsdp_half)(functools.partial(store_s, send_s))
    for sub in range(subs):
        here = slice(sub * rows, (sub + 1) * rows)
        place = sub ^ low_label

        def store_e(target, here=here, place=place):
            for part in range(2 * fsdp_half):
                there = slice(part * columns, (part + 1) * columns)
                target[part ^ y_index, 0, place >> 1] = expand_grad[there, here]

        pl.when((place & 1) == 0)(functools.partial(store_e, keep_e))
        pl.when((place & 1) == 1)(functools.partial(store_e, send_e))

    @pl.when(step == steps - 1)
    def _():
        keep_ref[0] = back[:tokens]
        keep_ref[1] = total[:tokens]
        send_ref[0] = back[tokens:]
        send_ref[1] = total[tokens:]


def feed_scalars(place, hidden, width, expand_offsets, shrink_offsets):
    (_, ctx_size), y_index, c_index = place
    subs = width * ctx_size // hidden
    label = c_index >> 1
    first = [y_index, label >> bits_of(subs), label & (subs - 1), c_index & 1]
    return jnp.concatenate([jnp.stack(first), expand_offsets, shrink_offsets])


def feed_forward(
    scalars, residual, h2, h2_other, og, og_other, vectors, expand_bias, expand, shrink, sizes
):
    fsdp_size, ctx_size = sizes
    expand_arrays = expand[0]
    shrink_arrays = shrink[0]
    tokens, features = h2.shape
    hidden = expand_bias.shape[1]
    rows = hidden // ctx_size
    columns = features // fsdp_size
    width = WIDTH
    subs = width // rows
    steps = hidden // (2 * width)
    def chunk(array, dim):
        if array.shape[dim] == hidden:
            return lambda s, sc: sc[3] * steps + (s ^ sc[1])
        return lambda s, sc: s ^ sc[1]

    def columns_of(array):
        index = chunk(array, 1)
        return pl.BlockSpec((array.shape[0], width), lambda s, sc: (0, index(s, sc)))

    def rows_of(array):
        index = chunk(array, 0)
        return pl.BlockSpec((width, array.shape[1]), lambda s, sc: (index(s, sc), 0))

    grad_s = (fsdp_size // 2, steps, subs, rows, columns)
    grad_e = (fsdp_size, steps, subs // 2, columns, rows)

    def block(shape):
        return pl.BlockSpec((shape[0], 1) + shape[2:], lambda s, sc: (0, s, 0, 0, 0))

    full = whole(h2.shape)
    wide = jax.ShapeDtypeStruct((2,) + h2.shape, F32)
    return pl.pallas_call(
        functools.partial(ffn_kernel, len(expand_arrays), len(shrink_arrays), steps),
        grid_spec=pltpu.PrefetchScalarGridSpec(
            num_scalar_prefetch=1,
            grid=(steps,),
            in_specs=[full] * 5
            + [whole(vectors.shape), columns_of(expand_bias)]
            + [columns_of(array) for array in expand_arrays]
            + [rows_of(array) for array in shrink_arrays],
            out_specs=[whole(wide.shape)] * 2
            + [block(grad_s)] * 2
            + [block(grad_e)] * 2
            + [pl.BlockSpec((1, width), lambda s, sc: (0, s ^ sc[1])), whole((1, features))],
            scratch_shapes=[
                pltpu.VMEM((features, width), BF16),
                pltpu.VMEM((width, features), BF16),
                pltpu.VMEM((2 * tokens, features), F32),
                pltpu.VMEM((2 * tokens, features), F32),
                pltpu.VMEM((2 * tokens, features), BF16),
                pltpu.VMEM((features, 2 * tokens), BF16),
                pltpu.VMEM((2 * tokens, features), BF16),
            ],
        ),
        out_shape=[wide] * 2
        + [jax.ShapeDtypeStruct(grad_s, BF16)] * 2
        + [jax.ShapeDtypeStruct(grad_e, BF16)] * 2
        + [
            jax.ShapeDtypeStruct((1, hidden // 2), F32),
            jax.ShapeDtypeStruct((1, features), F32),
        ],
        compiler_params=params(),
        cost_estimate=cost(0, 0),
        name="feed_forward",
    )(
        scalars,
        residual,
        h2,
        h2_other,
        og,
        og_other,
        vectors,
        expand_bias,
        *expand_arrays,
        *shrink_arrays,
    )


def branch_back_kernel(
    part_count, seqs, rows, sc_ref, dh2_ref, dh2_other_ref, residual_ref, og_ref, mixed_ref, v_ref, *refs
):
    parts = refs[:part_count]
    dres_ref, dmixed_ref, keep_ref, send_ref, vec_ref, weight, rounded = refs[part_count:]
    place_columns(weight, sc_ref, parts)
    hat, rate = norm_stats(residual_ref[...])
    dh2 = dh2_ref[0] + dh2_other_ref[0]
    scaled = dh2 * v_ref[V_G2 : V_G2 + 1, :]
    first = jnp.mean(scaled, axis=-1, keepdims=True)
    second = jnp.mean(scaled * hat, axis=-1, keepdims=True)
    dres = og_ref[...].astype(F32) + rate * (scaled - first - hat * second)
    dres_ref[...] = dres
    rounded[...] = dres.astype(BF16)
    vec_ref[0:1, :] = jnp.sum(dh2 * hat, axis=0, keepdims=True)
    vec_ref[1:2, :] = jnp.sum(dh2, axis=0, keepdims=True)
    vec_ref[2:3, :] = jnp.sum(rounded[...].astype(F32), axis=0, keepdims=True)
    vec_ref[3:, :] = jnp.zeros((vec_ref.shape[0] - 3, vec_ref.shape[1]), F32)
    dmixed = dot_nt(rounded[...], weight[...]).astype(BF16)
    for pair in range(dmixed_ref.shape[0]):
        dmixed_ref[pair] = dmixed[:, pair * LANES : (pair + 1) * LANES].reshape(seqs, rows, LANES)
    fsdp_size, count, size, columns = keep_ref.shape
    grad = dot_tn(mixed_ref[...], rounded[...]).astype(BF16)
    y_index = sc_ref[part_count]
    label = sc_ref[part_count + 1]
    for number in range(2 * count):
        place = number ^ label

        def store(target, number=number, place=place):
            for part in range(fsdp_size):
                target[part ^ y_index, place >> 1] = grad[
                    number * size : (number + 1) * size, part * columns : (part + 1) * columns
                ]

        pl.when((place & 1) == 0)(functools.partial(store, keep_ref))
        pl.when((place & 1) == 1)(functools.partial(store, send_ref))


def branch_back(scalars, dh2, dh2_other, residual, og, mixed, vectors, parts, sizes, seqs, rows):
    fsdp_size, ctx_size = sizes
    arrays, offsets = parts
    tokens, features = residual.shape
    pairs = features // LANES
    grad = (fsdp_size, ctx_size // 2, features // ctx_size, features // fsdp_size)
    full = whole(residual.shape)
    half = pl.BlockSpec((1,) + residual.shape, lambda n, o: (0, 0, 0))
    return pl.pallas_call(
        functools.partial(branch_back_kernel, len(arrays), seqs, rows),
        grid_spec=pltpu.PrefetchScalarGridSpec(
            num_scalar_prefetch=1,
            grid=(1,),
            in_specs=[half] * 2 + [full] * 3 + [whole(vectors.shape)]
            + [whole(array.shape) for array in arrays],
            out_specs=[
                full,
                whole((pairs, seqs, rows, LANES)),
                whole(grad),
                whole(grad),
                whole((8, features)),
            ],
            scratch_shapes=[
                pltpu.VMEM((features, features), BF16),
                pltpu.VMEM((tokens, features), BF16),
            ],
        ),
        out_shape=[
            jax.ShapeDtypeStruct(residual.shape, F32),
            jax.ShapeDtypeStruct((pairs, seqs, rows, LANES), BF16),
            jax.ShapeDtypeStruct(grad, BF16),
            jax.ShapeDtypeStruct(grad, BF16),
            jax.ShapeDtypeStruct((8, features), F32),
        ],
        compiler_params=params(),
        cost_estimate=cost(4 * tokens * features * features, 8 * features * features),
        name="branch_back",
    )(scalars, dh2, dh2_other, residual, og, mixed, vectors, *arrays)


def input_terms_kernel(sc_ref, h_ref, d_ref, keep_ref, send_ref, token_ref):
    token_ref[...] = jnp.zeros_like(token_ref)
    left = h_ref[...].reshape(-1, h_ref.shape[-1])
    right = d_ref[...].reshape(-1, d_ref.shape[-1])
    value = dot_tn(left, right).astype(BF16)
    half, fsdp_size, rows, _ = keep_ref.shape
    per = value.shape[0] // rows
    for number in range(per):
        place = pl.program_id(0) * per + number
        part = (place // (2 * half)) ^ sc_ref[1]
        own = (place & (2 * half - 1)) ^ sc_ref[2]

        def store(target, number=number, part=part, own=own):
            target[own & (half - 1), part] = value[number * rows : (number + 1) * rows]

        pl.when(own < half)(functools.partial(store, keep_ref))
        pl.when(own >= half)(functools.partial(store, send_ref))


def input_weight_terms(gathered, dqkv, scalars, low, fsdp_size):
    ctx_size, units, rows, width = dqkv.shape
    features = gathered.shape[-1]
    block = 2 * LANES
    out = (low // 2, fsdp_size, features // (low * fsdp_size), width)
    return pl.pallas_call(
        input_terms_kernel,
        grid_spec=pltpu.PrefetchScalarGridSpec(
            num_scalar_prefetch=1,
            grid=(features // block,),
            in_specs=[
                pl.BlockSpec((ctx_size, units, rows, block), lambda g, s: (0, s[0], 0, g)),
                whole(dqkv.shape),
            ],
            out_specs=[whole(out), whole(out), whole(TOKEN.shape)],
        ),
        out_shape=[jax.ShapeDtypeStruct(out, BF16)] * 2 + [TOKEN],
        compiler_params=params(),
        cost_estimate=cost(0, 0),
        name="input_weight_terms",
    )(scalars, gathered, dqkv)


def entry_back_kernel(
    part_count,
    groups,
    off_ref,
    d_ref,
    x_ref,
    dres_ref,
    one_ref,
    two_ref,
    second_ref,
    sb_ref,
    eb_ref,
    v_ref,
    *refs,
):
    parts = refs[: 3 * part_count]
    out_ref, layer_ref, vec_ref, weight, back = refs[3 * part_count :]
    group = pl.program_id(0)
    tokens = x_ref.shape[0]
    width = weight.shape[-1]

    @pl.when(group == 0)
    def _():
        back[...] = jnp.zeros_like(back)
        layer_ref[...] = (one_ref[0] + two_ref[0]).astype(BF16)
        vec_ref[4:7, :] = second_ref[0:3, :]
        vec_ref[7:8, :] = sb_ref[...]
        count = vec_ref.shape[0] - 8
        core = off_ref[off_ref.shape[0] - 1]
        for row in range(count):
            here = eb_ref[:, (row % (count // 2)) * LANES * 8 : (row % (count // 2) + 1) * LANES * 8]
            mine = core == row // (count // 2)
            vec_ref[8 + row : 9 + row, :] = jnp.where(mine, here, jnp.zeros_like(here))

    for kind in range(3):
        place_rows(
            weight.at[kind], off_ref, parts[kind * part_count : (kind + 1) * part_count]
        )
        lanes = slice(kind * LANES, (kind + 1) * LANES)
        value = jnp.concatenate(
            [d_ref[pair, :, :, lanes].reshape(tokens, LANES) for pair in range(d_ref.shape[0])],
            axis=1,
        )
        back[...] += dot_nt(value, weight[kind])
        if kind != 1:
            row = 2 if kind == 0 else 3
            start = pl.multiple_of(group * width, LANES)
            vec_ref[row : row + 1, pl.ds(start, width)] = jnp.sum(
                value.astype(F32), axis=0, keepdims=True
            )

    @pl.when(group == groups - 1)
    def _():
        hat, rate = norm_stats(x_ref[...].astype(F32))
        dh1 = back[...]
        scaled = dh1 * v_ref[V_G1 : V_G1 + 1, :]
        first = jnp.mean(scaled, axis=-1, keepdims=True)
        second = jnp.mean(scaled * hat, axis=-1, keepdims=True)
        out_ref[...] = dres_ref[...] + rate * (scaled - first - hat * second)
        vec_ref[0:1, :] = jnp.sum(dh1 * hat, axis=0, keepdims=True)
        vec_ref[1:2, :] = jnp.sum(dh1, axis=0, keepdims=True)


def entry_back(dqkv, x, dres, one, two, sums, vectors, parts):
    arrays, offsets = parts
    tokens, features = x.shape
    pairs, seqs, rows, _ = dqkv.shape
    width = 2 * LANES
    vec = (8 + 2 * sums[2].shape[1] // features, features)
    groups = features // width
    specs = []
    operands = []
    for kind in range(3):
        for array in arrays:
            specs.append(
                pl.BlockSpec((array.shape[0], width), lambda g, o, k=kind: (0, k * groups + g))
            )
            operands.append(array)
    return pl.pallas_call(
        functools.partial(entry_back_kernel, len(arrays), groups),
        grid_spec=pltpu.PrefetchScalarGridSpec(
            num_scalar_prefetch=1,
            grid=(groups,),
            in_specs=[
                pl.BlockSpec((2, seqs, rows, 3 * LANES), lambda g, o: (g, 0, 0, 0)),
                whole(x.shape),
                whole(x.shape),
                pl.BlockSpec((1,) + x.shape, lambda g, o: (1, 0, 0)),
                pl.BlockSpec((1,) + x.shape, lambda g, o: (1, 0, 0)),
            ]
            + [whole(array.shape) for array in sums]
            + [whole(vectors.shape)]
            + specs,
            out_specs=[whole(x.shape), whole(x.shape), whole(vec)],
            scratch_shapes=[
                pltpu.VMEM((3, features, width), BF16),
                pltpu.VMEM((tokens, features), F32),
            ],
        ),
        out_shape=[
            jax.ShapeDtypeStruct(x.shape, F32),
            jax.ShapeDtypeStruct(x.shape, BF16),
            jax.ShapeDtypeStruct(vec, F32),
        ],
        compiler_params=params(),
        cost_estimate=cost(6 * tokens * features * features, 6 * features * features),
        name="entry_back",
    )(offsets, dqkv, x, dres, one, two, *sums, vectors, *operands)


def combine_kernel(one_ref, two_ref, send_ref, keep_ref):
    total = (one_ref[...].astype(F32) + two_ref[...].astype(F32)).astype(BF16)
    keep_ref[...] = total[:, 0]
    send_ref[...] = total[:, 1]


def last_kernel(one_ref, two_ref, out_ref):
    out_ref[...] = (one_ref[...].astype(F32) + two_ref[...].astype(F32)).astype(BF16)


def combine(one, two, outer):
    rows, columns = one.shape[-2:]
    shape = (outer, 2, one.size // (2 * outer * rows * columns), rows, columns)
    inner = shape[2]
    per = inner
    while per * rows * columns > 256 * 1024 and per % 2 == 0:
        per //= 2
    half = (outer, inner, rows, columns)
    block = pl.BlockSpec((1, 2, per, rows, columns), lambda a, b: (a, 0, b, 0, 0))
    out = pl.BlockSpec((1, per, rows, columns), lambda a, b: (a, b, 0, 0))
    return pl.pallas_call(
        combine_kernel,
        grid=(outer, inner // per),
        in_specs=[block, block],
        out_specs=[out, out],
        out_shape=[jax.ShapeDtypeStruct(half, BF16)] * 2,
        compiler_params=params(),
        cost_estimate=cost(0, 0),
        name="combine",
    )(one.reshape(shape), two.reshape(shape))


def add_last(one, two):
    rows, columns = one.shape[-2:]
    return pl.pallas_call(
        last_kernel,
        out_shape=jax.ShapeDtypeStruct((1, rows, columns), BF16),
        compiler_params=params(),
        cost_estimate=cost(0, 0),
        name="add_last",
    )(one.reshape(1, rows, columns), two.reshape(1, rows, columns))


def merge_kernel(one_ref, two_ref, out_ref):
    out_ref[:, 0] = one_ref[...]
    out_ref[:, 1] = two_ref[...]


def merge(one, two):
    count, rows, columns = one.shape
    block = pl.BlockSpec((1, rows, columns), lambda n: (n, 0, 0))
    return pl.pallas_call(
        merge_kernel,
        grid=(count,),
        in_specs=[block, block],
        out_specs=pl.BlockSpec((1, 2, rows, columns), lambda n: (n, 0, 0, 0)),
        out_shape=jax.ShapeDtypeStruct((count, 2, rows, columns), BF16),
        compiler_params=params(),
        cost_estimate=cost(0, 0),
        name="merge",
    )(one, two).reshape(2 * count, rows, columns)


def tiles(rows, width, columns):
    count = columns // LANES
    height = rows // count
    return height, [
        (across * height, down * LANES, down * height, across * LANES)
        for down in range(width // LANES)
        for across in range(count)
    ]


def pack_kernel(one_ref, two_ref, extra_ref, out_ref):
    rows, columns = one_ref.shape[1:]
    first = out_ref.shape[1] - rows
    out_ref[:, first:] = (one_ref[...].astype(F32) + two_ref[...].astype(F32)).astype(BF16)
    height, moves = tiles(*extra_ref.shape, columns)
    for row, column, to_row, to_column in moves:
        out_ref[0, to_row : to_row + height, to_column : to_column + LANES] = extra_ref[
            row : row + height, column : column + LANES
        ]


def pack(one, two, extra):
    rows, columns = one.shape[-2:]
    return pl.pallas_call(
        pack_kernel,
        out_shape=jax.ShapeDtypeStruct((1, rows + extra.size // columns, columns), BF16),
        compiler_params=params(),
        cost_estimate=cost(0, 0),
        name="pack",
    )(one.reshape(1, rows, columns), two.reshape(1, rows, columns), extra)


class Flow:
    def __init__(self, send, keep, first, labels, order, sizes):
        self.sizes = dict(fsdp=sizes[0], ctx=sizes[1])
        self.labels = list(labels)
        self.order = list(order)
        self.keep = keep
        self.spreading = None
        self.extra = None
        self.received = self.swap(send, first)

    def swap(self, value, label):
        return swap_bit(value, label[0], self.sizes[label[0]], label[1])

    def step(self, event):
        received = after(self.received, event)
        if self.order:
            label = self.order.pop(0)
            place = self.labels.index(label)
            self.labels.pop(place)
            send, self.keep = combine(self.keep, received, 1 << place)
            self.received = self.swap(send, label)
        elif self.spreading is None:
            if self.extra is None:
                self.keep = add_last(self.keep, received)
            else:
                self.keep = pack(self.keep, received, self.extra)
            self.received = None
        else:
            if self.spreading:
                self.keep = merge(self.keep, received)
                self.received = self.swap(self.keep, self.spreading.pop(0))
            else:
                self.far = received
                self.received = None
        return self

    def spread(self):
        self.spreading = [("ctx", bit) for bit in reversed(range(bits_of(self.sizes["ctx"])))]
        self.received = self.swap(self.keep, self.spreading.pop(0))


def finish_kernel(dim, label_ref, near_ref, far_ref, out_ref):
    count, height, _ = near_ref.shape
    rows, columns = out_ref.shape
    if dim == 0:
        rows = rows // count
    else:
        columns = columns // count
    first = height - rows
    low = label_ref[1] & (count - 1)

    def write(source):
        for number in range(count):
            place = number ^ low
            value = source[number, first:].astype(F32)
            if dim == 0:
                out_ref[pl.ds(pl.multiple_of(place * rows, LANES), rows), :] = value
            else:
                out_ref[:, pl.ds(pl.multiple_of(place * columns, LANES), columns)] = value

    pl.when(pl.program_id(0) == 0)(functools.partial(write, near_ref))
    pl.when(pl.program_id(0) == 1)(functools.partial(write, far_ref))


def finish(near, far, table, dim, rows, columns):
    half, height, width = near.shape
    group = half // 2
    shift = bits_of(group)
    if dim == 0:
        shape = (2 * half * rows, columns)
        out_spec = pl.BlockSpec(
            (group * rows, columns), lambda k, n, t: ((k ^ t[0]) * 2 + (n ^ (t[1] >> shift)), 0)
        )
    else:
        shape = (rows, 2 * half * columns)
        out_spec = pl.BlockSpec(
            (rows, group * columns), lambda k, n, t: (0, (k ^ t[0]) * 2 + (n ^ (t[1] >> shift)))
        )

    def block(which):
        return pl.BlockSpec(
            (group, height, width),
            lambda k, n, t: (jnp.where(k == which, n, 1 - which), 0, 0),
        )

    return pl.pallas_call(
        functools.partial(finish_kernel, dim),
        grid_spec=pltpu.PrefetchScalarGridSpec(
            num_scalar_prefetch=1,
            grid=(2, 2),
            in_specs=[block(0), block(1)],
            out_specs=out_spec,
        ),
        out_shape=jax.ShapeDtypeStruct(shape, F32),
        compiler_params=params(),
        cost_estimate=cost(0, 0),
        name="finish",
    )(table, near, far)


def finish_extra_kernel(rows, width, low_bits, label_ref, near_ref, far_ref, *refs):
    out_ref = refs[-1]
    half, _, columns = near_ref.shape
    height, moves = tiles(rows, width, columns)
    for number in range(2 * half):
        source = far_ref if number & 1 else near_ref
        owner = number ^ ((label_ref[1] << 1) | label_ref[0])
        if low_bits is None:
            place, begin, stride = owner, 0, LANES
        else:
            place = owner & ((1 << low_bits) - 1)
            begin = (owner >> low_bits) * LANES
            stride = out_ref.shape[1] // (width // LANES)
        for row, column, from_row, from_column in moves:
            down = pl.ds(pl.multiple_of(place * rows + row, 32), height)
            across = begin + (column // LANES) * stride
            if low_bits is not None:
                across = pl.multiple_of(across, LANES)
            out_ref[down, pl.ds(across, LANES)] = source[
                number >> 1, from_row : from_row + height, from_column : from_column + LANES
            ].astype(F32)


def finish_extra(near, far, table, rows, width, low_bits, shape, events=()):
    half, _, columns = near.shape
    block = pl.BlockSpec((half, rows * width // columns, columns), lambda n, t: (0, 0, 0))
    return pl.pallas_call(
        functools.partial(finish_extra_kernel, rows, width, low_bits),
        grid_spec=pltpu.PrefetchScalarGridSpec(
            num_scalar_prefetch=1,
            grid=(1,),
            in_specs=[block, block] + [whole(event.keep.shape) for event in events],
            out_specs=whole(shape),
        ),
        out_shape=jax.ShapeDtypeStruct(shape, F32),
        compiler_params=params(),
        cost_estimate=cost(0, 0),
        name="finish_extra",
    )(table, near, far, *[event.keep for event in events])


class Total:
    def __init__(self, value, labels, sizes):
        self.keep = value
        self.sizes = dict(fsdp=sizes[0], ctx=sizes[1])
        self.labels = list(labels)
        self.start()

    def start(self):
        self.received = None
        if self.labels:
            name, bit = self.labels.pop(0)
            self.received = swap_bit(self.keep, name, self.sizes[name], bit)

    def step(self, event):
        received = after(self.received, event)
        self.keep = pl.pallas_call(
            total_kernel,
            out_shape=jax.ShapeDtypeStruct(self.keep.shape, F32),
            compiler_params=params(),
            cost_estimate=cost(0, 0),
            name="total",
        )(self.keep, received)
        self.start()
        return self


def total_kernel(one_ref, two_ref, out_ref):
    out_ref[...] = one_ref[...] + two_ref[...]


def body(
    sizes,
    layer_input,
    output_grad,
    segments,
    assignment,
    first_gain,
    first_bias,
    input_weight,
    query_bias,
    value_bias,
    output_weight,
    output_bias,
    second_gain,
    second_bias,
    expand_weight,
    expand_bias,
    shrink_weight,
    shrink_bias,
):
    fsdp_size, ctx_size = sizes
    seqs, rows, features = layer_input.shape
    tokens = seqs * rows
    hidden = expand_weight.shape[1]
    pairs = features // LANES
    units = seqs * pairs // ctx_size
    y_index = lax.axis_index("fsdp").astype(jnp.int32)
    c_index = lax.axis_index("ctx").astype(jnp.int32)
    part = features // fsdp_size
    small = jnp.concatenate(
        [
            first_gain,
            first_bias,
            query_bias,
            value_bias,
            output_bias,
            second_gain,
            second_bias,
            shrink_bias,
            expand_bias,
        ]
    )
    small = small.reshape(1, -1)
    x = layer_input.reshape(tokens, features)
    og = output_grad.reshape(tokens, features)
    place = (sizes, y_index, c_index)
    core = c_index & 1
    starts = jnp.sum(
        (segments[:, None, :] < segments[:, :, None]).astype(jnp.int32), axis=-1
    )[:, None, :]
    unit_seqs = (c_index * units + jnp.arange(units, dtype=jnp.int32)) & (seqs - 1)
    input_gather = Gather(input_weight, 0, place, (1, 0))
    output_gather = Gather(output_weight, 1, place, (0,))
    expand_gather = Gather(expand_weight, 0, place, (1,), core)
    shrink_gather = Gather(shrink_weight, 1, place, (), core)
    gathers = (input_gather, output_gather, expand_gather, shrink_gather)

    group = ((c_index * units) & (seqs - 1)) >> bits_of(units)
    low_bits = bits_of(ctx_size // pairs)
    low = 1 << low_bits
    if fsdp_size == 2:
        owners = jnp.stack([y_index, 1 - y_index])
    else:
        owners = jnp.arange(fsdp_size, dtype=jnp.int32)

    ready = (
        x,
        small,
        starts,
        [gather.first for gather in gathers[1:]],
        [
            unit_seqs,
            owners,
            input_gather.offsets,
            output_gather.offsets,
            feed_scalars(place, hidden, WIDTH, expand_gather.offsets, shrink_gather.offsets),
            jnp.stack([core, c_index >> 1]),
            jnp.concatenate([output_gather.offsets, jnp.stack([y_index, c_index])]),
            jnp.concatenate([input_gather.offsets, core[None]]),
            jnp.stack([group, y_index, c_index & (low - 1)]),
        ],
    )
    x, small, starts, firsts, tables = lax.optimization_barrier(ready)
    for gather, first in zip(gathers[1:], firsts):
        gather.first = first
    unit_seqs, owners, input_gather.offsets, output_gather.offsets, *tables = tables
    feed_table, finish_table, back_table, entry_table, terms_table = tables

    input_gather.fetch()
    if fsdp_size == 2:
        small_other = Event(swap_bit(small, "fsdp", 2, 0))
        input_gather.keep = after(input_gather.keep, small_other)
        shards = [small, small_other.keep]
    else:
        full = lax.all_gather(small, "fsdp", axis=0)
        shards = [full[number] for number in range(fsdp_size)]
    h1, vectors, expand_vector = first_norm(x, shards, owners, hidden)
    other = Event(swap_bit(og, "ctx", ctx_size, 0))
    expand_gather.fetch(input_gather)
    input_gather.exchange()
    norm_done = Event(h1)
    input_gather.keep = after(input_gather.keep, norm_done)
    h1 = norm_done.keep
    input_gather.exchange()
    expand_first = Event(after(expand_gather.keep, input_gather))
    expand_gather.exchange()
    output_gather.fetch(expand_first)
    h1 = after(after(h1, other), expand_first)
    og_other = other.keep
    qkv, token = project(h1, vectors, input_gather.result(), seqs, rows)
    expand_gather.held[0] = expand_first.keep
    project_done = Event(token)
    shrink_gather.fetch(output_gather)
    output_gather.exchange()
    output_gather.keep = after(output_gather.keep, project_done)
    qkv = qkv.reshape(ctx_size, units, rows, 3 * LANES)
    qkv = lax.all_to_all(qkv, "ctx", 0, 0, tiled=True)
    qkv = after(qkv, output_gather)
    att, lse = attend(assignment, unit_seqs, qkv, starts)
    attend_done = Event(lse)
    shrink_gather.keep = after(shrink_gather.keep, attend_done)
    att = lax.all_to_all(att, "ctx", 0, 0, tiled=True)
    received = Event(after(after(att, expand_gather), shrink_gather))
    gathered = lax.all_gather(
        after(h1, received).reshape(seqs, rows, features), "ctx", axis=0
    )
    att = received.keep.reshape(pairs, seqs, rows, LANES)
    output_parts = output_gather.result()
    residual, h2, mixed = branch(att, x, vectors, output_parts)
    h2_other = swap_bit(h2, "ctx", ctx_size, 0)
    send, keep, send_s, keep_s, send_e, keep_e, eb_grad, sb_grad = feed_forward(
        feed_table,
        residual,
        h2,
        h2_other,
        og,
        og_other,
        vectors,
        expand_vector,
        expand_gather.result(),
        shrink_gather.result(),
        sizes,
    )
    other = swap_bit(send, "ctx", ctx_size, 0)

    every = [("fsdp", bit) for bit in reversed(range(bits_of(fsdp_size)))]
    high = [("ctx", bit) for bit in reversed(range(1, bits_of(ctx_size)))]
    flow_s = Flow(send_s, keep_s, every[0], every[1:] + high, every[1:] + high[::-1], sizes)
    flow_e = Flow(
        send_e, keep_e, high[-1], every + high[:-1], every + high[:-1][::-1], sizes
    )
    dres, dmixed, keep_o, send_o, vec_two = branch_back(
        back_table, keep, other, residual, og, mixed, vectors, output_parts, sizes, seqs, rows
    )
    branch_done = Event(vec_two)
    flow_o = Flow(send_o, keep_o, ("ctx", 0), every + high, every + high[::-1], sizes)
    dmixed = dmixed.reshape(ctx_size, units, rows, LANES)
    dmixed = lax.all_to_all(dmixed, "ctx", 0, 0, tiled=True)
    dqkv, token = attend_back(
        assignment, unit_seqs, qkv, dmixed, starts, attend_done.keep
    )
    back_done = Event(token)
    last = flow_s.step(back_done)
    last = flow_e.step(last)
    held = Event(after(dqkv, last))
    keep_i, send_i, token = input_weight_terms(gathered, held.keep, terms_table, low, fsdp_size)
    terms_done = Event(token)
    low_labels = [("ctx", bit) for bit in reversed(range(low_bits))]
    flow_i = Flow(
        send_i,
        keep_i,
        low_labels[0],
        low_labels[1:] + every,
        low_labels[1:] + every,
        sizes,
    )
    last = flow_o.step(terms_done)
    last = flow_i.step(last)
    last = flow_s.step(last)
    last = flow_e.step(last)
    dqkv = lax.all_to_all(dqkv, "ctx", 0, 0, tiled=True).reshape(pairs, seqs, rows, 3 * LANES)
    last = flow_o.step(last)
    while flow_i.received is not None:
        last = flow_i.step(last)
    flow_s.extra = flow_i.keep[0]
    while flow_s.order:
        last = flow_s.step(last)
    last = flow_s.step(last)
    flow_s.spread()
    input_grad, out, sums = entry_back(
        after(dqkv, last),
        x,
        dres,
        keep,
        other,
        [branch_done.keep, sb_grad, eb_grad],
        vectors,
        (input_gather.result()[0], entry_table),
    )
    totals = Total(sums, every + [("ctx", 0)] + high[::-1], sizes)
    last = flow_o.step(totals)
    if flow_e.order:
        last = flow_e.step(last)
    last = flow_s.step(last)
    last = flow_o.step(last)
    last = totals.step(last)
    while flow_e.order:
        last = flow_e.step(last)
    last = flow_s.step(last)
    while flow_o.received is not None:
        last = flow_o.step(last)
    flow_e.extra = flow_o.keep[0]
    last = flow_e.step(last)
    flow_e.spread()
    last = totals.step(last)
    last = flow_e.step(last)
    last = flow_e.step(last)
    while flow_s.spreading:
        last = flow_s.step(last)
    last = totals.step(last)
    last = flow_s.step(last)
    rows_s = hidden // ctx_size
    shrink_done = Event(finish(flow_s.keep, flow_s.far, finish_table, 0, rows_s, part))
    loose = [project_done, back_done, terms_done, branch_done]
    input_done = Event(
        finish_extra(
            flow_s.keep,
            flow_s.far,
            finish_table,
            part >> low_bits,
            3 * LANES,
            low_bits,
            (part, 3 * features),
            loose,
        )
    )
    last = totals.step(last)
    flow_e.received = after(flow_e.received, shrink_done)
    flow_e.received = after(flow_e.received, input_done)
    while flow_e.spreading:
        last = flow_e.step(last)
    while totals.received is not None:
        last = totals.step(last)
    last = flow_e.step(last)
    shrink_grad = shrink_done.keep
    input_grad_w = input_done.keep
    expand_grad = finish(flow_e.keep, flow_e.far, finish_table, 1, part, rows_s)
    output_grad_w = finish_extra(
        flow_e.keep,
        flow_e.far,
        finish_table,
        features // ctx_size,
        part,
        None,
        (features, part),
    )
    sums = totals.keep
    input_grad_w = finish_extra(
        flow_s.keep,
        flow_s.far,
        finish_table,
        part >> low_bits,
        3 * LANES,
        low_bits,
        (part, 3 * features),
        loose,
    )
    rows_s = hidden // ctx_size
    shrink_grad = finish(flow_s.keep, flow_s.far, finish_table, 0, rows_s, part)
    expand_grad = finish(flow_e.keep, flow_e.far, finish_table, 1, part, rows_s)
    output_grad_w = finish_extra(
        flow_e.keep,
        flow_e.far,
        finish_table,
        features // ctx_size,
        part,
        None,
        (features, part),
    )

    def own(vector):
        size = vector.shape[0] // fsdp_size
        return lax.dynamic_slice_in_dim(vector, y_index * size, size, 0)

    return (
        out.reshape(seqs, rows, features),
        input_grad.reshape(seqs, rows, features),
        own(sums[0]),
        own(sums[1]),
        input_grad_w,
        own(sums[2]),
        own(sums[3]),
        output_grad_w,
        own(sums[6]),
        own(sums[4]),
        own(sums[5]),
        expand_grad,
        own(sums[8:].reshape(-1)),
        shrink_grad,
        own(sums[7]),
    )


def solution(mesh):
    sizes = (mesh.shape["fsdp"], mesh.shape["ctx"])
    return jax.shard_map(
        functools.partial(body, sizes),
        mesh=mesh,
        in_specs=(
            P("fsdp", "ctx", None),
            P("fsdp", "ctx", None),
            P("fsdp", None),
            P(),
            P("fsdp"),
            P("fsdp"),
            P("fsdp", None),
            P("fsdp"),
            P("fsdp"),
            P(None, "fsdp"),
            P("fsdp"),
            P("fsdp"),
            P("fsdp"),
            P("fsdp", None),
            P("fsdp"),
            P(None, "fsdp"),
            P("fsdp"),
        ),
        out_specs=(
            P("fsdp", "ctx", None),
            P("fsdp", "ctx", None),
            P("fsdp"),
            P("fsdp"),
            P("fsdp", None),
            P("fsdp"),
            P("fsdp"),
            P(None, "fsdp"),
            P("fsdp"),
            P("fsdp"),
            P("fsdp"),
            P("fsdp", None),
            P("fsdp"),
            P(None, "fsdp"),
            P("fsdp"),
        ),
        check_vma=False,
    )
```

```python
import functools
import math

import jax
import jax.numpy as jnp
from jax import lax
from jax.experimental import pallas as pl
from jax.experimental.pallas import tpu as pltpu
from jax.sharding import PartitionSpec as P

HEADS = 16
EPSILON = 1e-05
MASKED = -1000000000.0
LANES = 128
WIDTH = 512
MIB = 1024 * 1024
F32 = jnp.float32
BF16 = jnp.bfloat16
TOKEN = jax.ShapeDtypeStruct((8, LANES), F32)

V_G1, V_B1, V_BQ, V_BV, V_BO, V_G2, V_B2, V_BS = range(8)


def bits_of(number):
    return number.bit_length() - 1


def dot(left, right):
    return jnp.dot(left, right, preferred_element_type=F32)


def dot_nt(left, right):
    return lax.dot_general(left, right, (((1,), (1,)), ((), ())), preferred_element_type=F32)


def dot_tn(left, right):
    return lax.dot_general(left, right, (((0,), (0,)), ((), ())), preferred_element_type=F32)


def swap_bit(value, axis, size, bit):
    return lax.ppermute(value, axis, [(i, i ^ (1 << bit)) for i in range(size)])


class Event:
    def __init__(self, keep):
        self.keep = keep


def after(value, event):
    value, event.keep = lax.optimization_barrier((value, event.keep))
    return value


def params(limit_mib=48):
    return pltpu.CompilerParams(vmem_limit_bytes=limit_mib * MIB)


def whole(shape):
    rank = len(shape)
    return pl.BlockSpec(tuple(shape), lambda *_: (0,) * rank)


def cost(flops, moved):
    return pl.CostEstimate(flops=0, bytes_accessed=0, transcendentals=0)


class Gather:
    def __init__(self, weight, dim, place, bits, core=None):
        (fsdp_size, self.ctx_size), y_index, c_index = place
        extent = weight.shape[dim]
        self.bits = bits
        self.stage = 0
        self.two = fsdp_size == 2
        if not self.two:
            self.bits = ()
            self.parts = []
            self.first = lax.all_gather(weight, "fsdp", axis=dim, tiled=True)
            self.offsets = jnp.zeros((1,), jnp.int32)
            self.held = [self.first]
            return
        size = extent >> len(bits)
        mine = jnp.int32(0)
        for number, bit in enumerate(bits):
            mine = mine | (((c_index >> bit) & 1) << number)
        if core is None:
            self.first = lax.dynamic_slice_in_dim(weight, mine * size, size, dim)
        else:
            half = weight.shape[1 - dim] // 2
            begins = (mine * size, core * half) if dim == 0 else (core * half, mine * size)
            self.first = lax.dynamic_slice(
                weight, begins, (size, half) if dim == 0 else (half, size)
            )
        order = y_index * extent + jnp.zeros((1,), jnp.int32)
        numbers = mine ^ jnp.arange(1 << len(bits), dtype=jnp.int32)
        self.offsets = jnp.concatenate([order, (1 - y_index) * extent + numbers * size])
        self.parts = [weight]

    def fetch(self, event=None):
        if not self.two:
            return
        first = self.first if event is None else after(self.first, event)
        self.held = [swap_bit(first, "fsdp", 2, 0)]

    @property
    def keep(self):
        return self.held[-1]

    @keep.setter
    def keep(self, value):
        self.held[-1] = value

    def exchange(self, event=None):
        if self.stage == len(self.bits):
            return
        bit = self.bits[self.stage]
        if event is not None:
            self.keep = after(self.keep, event)
        self.held = self.held + [swap_bit(array, "ctx", self.ctx_size, bit) for array in self.held]
        self.stage += 1

    def result(self):
        return self.parts + self.held, self.offsets


def place_rows(target, offsets, part_refs):
    for number, ref in enumerate(part_refs):
        rows = ref.shape[0]
        target[pl.ds(pl.multiple_of(offsets[number], 32), rows), :] = ref[...]


def place_columns(target, offsets, part_refs):
    for number, ref in enumerate(part_refs):
        columns = ref.shape[1]
        target[:, pl.ds(pl.multiple_of(offsets[number], LANES), columns)] = ref[...]


def norm_stats(values):
    center = values - jnp.mean(values, axis=-1, keepdims=True)
    spread = jnp.mean(center * center, axis=-1, keepdims=True)
    rate = lax.rsqrt(spread + EPSILON)
    return center * rate, rate


def norm_kernel(sc_ref, x_ref, *refs):
    shards = refs[:-3]
    h_ref, v_ref, e_ref = refs[-3:]
    part = v_ref.shape[1] // len(shards)
    hidden = e_ref.shape[1] // len(shards)
    for number, ref in enumerate(shards):
        where = sc_ref[number]
        for row in range(8):
            v_ref[row : row + 1, pl.ds(pl.multiple_of(where * part, LANES), part)] = ref[
                :, row * part : (row + 1) * part
            ].astype(F32)
        e_ref[:, pl.ds(pl.multiple_of(where * hidden, LANES), hidden)] = ref[:, 8 * part :].astype(
            F32
        )
    hat, _ = norm_stats(x_ref[...].astype(F32))
    h_ref[...] = (hat * v_ref[V_G1 : V_G1 + 1, :] + v_ref[V_B1 : V_B1 + 1, :]).astype(BF16)


def first_norm(x, shards, owners, hidden):
    shapes = [
        jax.ShapeDtypeStruct(x.shape, BF16),
        jax.ShapeDtypeStruct((8, x.shape[1]), F32),
        jax.ShapeDtypeStruct((1, hidden), F32),
    ]
    return pl.pallas_call(
        norm_kernel,
        grid_spec=pltpu.PrefetchScalarGridSpec(
            num_scalar_prefetch=1,
            grid=(1,),
            in_specs=[whole(x.shape)] + [whole(shard.shape) for shard in shards],
            out_specs=[whole(shape.shape) for shape in shapes],
        ),
        out_shape=shapes,
        compiler_params=params(),
        cost_estimate=cost(0, 0),
        name="first_norm",
    )(owners, x, *shards)


def qkv_kernel(part_count, seqs, rows, off_ref, h_ref, v_ref, *refs):
    parts = refs[: 3 * part_count]
    out_ref, token_ref, weight = refs[3 * part_count :]
    token_ref[...] = jnp.zeros_like(token_ref)
    group = pl.program_id(0)
    width = weight.shape[-1]
    per = width // LANES
    for kind in range(3):
        place_rows(
            weight.at[kind], off_ref, parts[kind * part_count : (kind + 1) * part_count]
        )
        value = dot(h_ref[...], weight[kind])
        if kind != 1:
            row = V_BQ if kind == 0 else V_BV
            start = pl.multiple_of(group * width, LANES)
            value = value + v_ref[row : row + 1, pl.ds(start, width)]
        value = value.astype(BF16)
        for pair in range(per):
            out_ref[pair, :, :, kind * LANES : (kind + 1) * LANES] = value[
                :, pair * LANES : (pair + 1) * LANES
            ].reshape(seqs, rows, LANES)


def project(h1, vectors, parts, seqs, rows):
    arrays, offsets = parts
    tokens, features = h1.shape
    width = 2 * LANES
    groups = features // width
    pairs = features // LANES
    specs = []
    operands = []
    for kind in range(3):
        for array in arrays:
            specs.append(
                pl.BlockSpec((array.shape[0], width), lambda g, o, k=kind: (0, k * groups + g))
            )
            operands.append(array)
    return pl.pallas_call(
        functools.partial(qkv_kernel, len(arrays), seqs, rows),
        grid_spec=pltpu.PrefetchScalarGridSpec(
            num_scalar_prefetch=1,
            grid=(groups,),
            in_specs=[whole(h1.shape), whole(vectors.shape)] + specs,
            out_specs=[
                pl.BlockSpec((2, seqs, rows, 3 * LANES), lambda g, o: (g, 0, 0, 0)),
                whole(TOKEN.shape),
            ],
            scratch_shapes=[pltpu.VMEM((3, features, width), BF16)],
        ),
        out_shape=[jax.ShapeDtypeStruct((pairs, seqs, rows, 3 * LANES), BF16), TOKEN],
        compiler_params=params(),
        cost_estimate=cost(6 * tokens * features * features, 6 * features * features),
        name="project",
    )(offsets, h1, vectors, *operands)


def to_places(table, ctx_size, half, source, target):
    for device in range(ctx_size):
        pair = table[device]
        early = pl.multiple_of(pair * half, half)
        later = pl.multiple_of((2 * ctx_size - 1 - pair) * half, half)
        target[pl.ds(early, half), :] = source[device, 0, 0:half, :]
        target[pl.ds(later, half), :] = source[device, 0, half : 2 * half, :]


def both_heads(block):
    first = lax.broadcasted_iota(jnp.int32, block.shape, 0) < LANES // 2
    zero = jnp.zeros_like(block)
    return jnp.concatenate([jnp.where(first, block, zero), jnp.where(first, zero, block)], axis=1)


def stacked_heads(block):
    first = lax.broadcasted_iota(jnp.int32, block.shape, 1) < LANES // 2
    zero = jnp.zeros_like(block)
    return jnp.concatenate([jnp.where(first, block, zero), jnp.where(first, zero, block)], axis=0)


def flipped(block):
    return block.astype(F32).T.astype(BF16)


def band_mask(low, high, start_row, size):
    count = high - low
    key = lax.broadcasted_iota(jnp.int32, (count, 2 * size), 0) + low
    query = lax.broadcasted_iota(jnp.int32, (count, 2 * size), 1) % size + (high - size)
    return (key >= start_row) & (key <= query)


def attend_kernel(
    ctx_size, table, seq_ref, qkv_ref, start_ref, out_ref, lse_ref, held, query_t, value_t, mixed
):
    length = held.shape[0]
    half = length // (2 * ctx_size)
    size = LANES
    blocks = length // size
    reach = blocks // 2
    to_places(table, ctx_size, half, qkv_ref, held)
    for block in range(blocks):
        span = slice(block * size, (block + 1) * size)
        query_t[:, span] = (held[span, 0:LANES].astype(F32) * 0.125).T.astype(BF16)
        value_t[:, span] = flipped(held[span, 2 * LANES :])
    for block in range(blocks):
        low = max(0, block - reach) * size
        high = (block + 1) * size
        span = slice(block * size, high)
        scores = dot(held[low:high, LANES : 2 * LANES], both_heads(query_t[:, span]))
        start_row = start_ref[0, :, span]
        start_row = jnp.concatenate([start_row, start_row], axis=1)
        scores = jnp.where(band_mask(low, high, start_row, size), scores, MASKED)
        top = jnp.max(scores, axis=0, keepdims=True)
        weights = jnp.exp(scores - top)
        total = jnp.sum(weights, axis=0, keepdims=True)
        lse = top + jnp.log(total)
        probs = (weights * (1.0 / total)).astype(BF16)
        lse_ref[0, 0:1, span] = lse[:, :size]
        lse_ref[0, 1:2, span] = lse[:, size:]
        mixed_t = dot(value_t[:, low:high], probs)
        both = jnp.concatenate(
            [mixed_t[0 : LANES // 2, :size], mixed_t[LANES // 2 :, size:]], axis=0
        )
        mixed[span, :] = both.T.astype(BF16)
    for device in range(ctx_size):
        pair = table[device]
        early = pl.multiple_of(pair * half, half)
        later = pl.multiple_of((2 * ctx_size - 1 - pair) * half, half)
        out_ref[device, 0, 0:half, :] = mixed[pl.ds(early, half), :]
        out_ref[device, 0, half : 2 * half, :] = mixed[pl.ds(later, half), :]


def attend(table, unit_seqs, qkv, starts):
    ctx_size, units, rows, width = qkv.shape
    length = ctx_size * rows
    return pl.pallas_call(
        functools.partial(attend_kernel, ctx_size),
        grid_spec=pltpu.PrefetchScalarGridSpec(
            num_scalar_prefetch=2,
            grid=(units,),
            in_specs=[
                pl.BlockSpec((ctx_size, 1, rows, width), lambda u, t, s: (0, u, 0, 0)),
                pl.BlockSpec((1, 1, length), lambda u, t, s: (s[u], 0, 0)),
            ],
            out_specs=[
                pl.BlockSpec((ctx_size, 1, rows, LANES), lambda u, t, s: (0, u, 0, 0)),
                pl.BlockSpec((1, 2, length), lambda u, t, s: (u, 0, 0)),
            ],
            scratch_shapes=[
                pltpu.VMEM((length, width), BF16),
                pltpu.VMEM((LANES, length), BF16),
                pltpu.VMEM((LANES, length), BF16),
                pltpu.VMEM((length, LANES), BF16),
            ],
        ),
        out_shape=[
            jax.ShapeDtypeStruct((ctx_size, units, rows, LANES), BF16),
            jax.ShapeDtypeStruct((units, 2, length), F32),
        ],
        compiler_params=params(),
        cost_estimate=cost(units * length * length * 256, qkv.size * 4),
        name="attend",
    )(table, unit_seqs, qkv, starts)


def attend_back_kernel(
    ctx_size,
    table,
    seq_ref,
    qkv_ref,
    grad_ref,
    start_ref,
    lse_ref,
    out_ref,
    token_ref,
    held,
    grad,
    query_t,
    key_t,
    grad_t,
    query_grad,
    key_grad,
    value_grad,
):
    token_ref[...] = jnp.zeros_like(token_ref)
    length = held.shape[0]
    half = length // (2 * ctx_size)
    size = LANES
    blocks = length // size
    reach = blocks // 2
    to_places(table, ctx_size, half, qkv_ref, held)
    to_places(table, ctx_size, half, grad_ref, grad)
    for block in range(blocks):
        span = slice(block * size, (block + 1) * size)
        scaled = (held[span, 0:LANES].astype(F32) * 0.125).astype(BF16)
        held[span, 0:LANES] = scaled
        query_t[:, span] = flipped(scaled)
        key_t[:, span] = flipped(held[span, LANES : 2 * LANES])
        grad_t[:, span] = flipped(grad[span, :])
    for block in range(blocks):
        low = max(0, block - reach) * size
        high = (block + 1) * size
        span = slice(block * size, high)
        scores = dot(held[low:high, LANES : 2 * LANES], both_heads(query_t[:, span]))
        start_row = start_ref[0, :, span]
        start_row = jnp.concatenate([start_row, start_row], axis=1)
        scores = jnp.where(band_mask(low, high, start_row, size), scores, MASKED)
        lse = jnp.concatenate([lse_ref[0, 0:1, span], lse_ref[0, 1:2, span]], axis=1)
        probs = jnp.exp(scores - lse)
        prob_grad = dot(held[low:high, 2 * LANES :], both_heads(grad_t[:, span]))
        delta = jnp.sum(probs * prob_grad, axis=0, keepdims=True)
        score_grad = (probs * (prob_grad - delta)).astype(BF16)
        probs = probs.astype(BF16)
        new_value = dot(probs, stacked_heads(grad[span, :]))
        new_key = dot(score_grad, stacked_heads(held[span, 0:LANES]))
        if low < high - size:
            value_grad[low : high - size, :] += new_value[: high - size - low]
            key_grad[low : high - size, :] += new_key[: high - size - low]
        value_grad[span, :] = new_value[high - size - low :]
        key_grad[span, :] = new_key[high - size - low :]
        query_t_grad = dot(key_t[:, low:high], score_grad)
        both = jnp.concatenate(
            [query_t_grad[0 : LANES // 2, :size], query_t_grad[LANES // 2 :, size:]], axis=0
        )
        query_grad[span, :] = (both.T * 0.125).astype(BF16)
    for device in range(ctx_size):
        pair = table[device]
        early = pl.multiple_of(pair * half, half)
        later = pl.multiple_of((2 * ctx_size - 1 - pair) * half, half)
        for place, source in ((0, early), (half, later)):
            rows = pl.ds(source, half)
            out_ref[device, 0, place : place + half, 0:LANES] = query_grad[rows, :]
            out_ref[device, 0, place : place + half, LANES : 2 * LANES] = key_grad[
                rows, :
            ].astype(BF16)
            out_ref[device, 0, place : place + half, 2 * LANES :] = value_grad[rows, :].astype(
                BF16
            )


def attend_back(table, unit_seqs, qkv, grad, starts, lse):
    ctx_size, units, rows, width = qkv.shape
    length = ctx_size * rows
    return pl.pallas_call(
        functools.partial(attend_back_kernel, ctx_size),
        grid_spec=pltpu.PrefetchScalarGridSpec(
            num_scalar_prefetch=2,
            grid=(units,),
            in_specs=[
                pl.BlockSpec((ctx_size, 1, rows, width), lambda u, t, s: (0, u, 0, 0)),
                pl.BlockSpec((ctx_size, 1, rows, LANES), lambda u, t, s: (0, u, 0, 0)),
                pl.BlockSpec((1, 1, length), lambda u, t, s: (s[u], 0, 0)),
                pl.BlockSpec((1, 2, length), lambda u, t, s: (u, 0, 0)),
            ],
            out_specs=[
                pl.BlockSpec((ctx_size, 1, rows, width), lambda u, t, s: (0, u, 0, 0)),
                whole(TOKEN.shape),
            ],
            scratch_shapes=[
                pltpu.VMEM((length, width), BF16),
                pltpu.VMEM((length, LANES), BF16),
                pltpu.VMEM((LANES, length), BF16),
                pltpu.VMEM((LANES, length), BF16),
                pltpu.VMEM((LANES, length), BF16),
                pltpu.VMEM((length, LANES), BF16),
                pltpu.VMEM((length, LANES), F32),
                pltpu.VMEM((length, LANES), F32),
            ],
        ),
        out_shape=[jax.ShapeDtypeStruct(qkv.shape, BF16), TOKEN],
        compiler_params=params(),
        cost_estimate=cost(units * length * length * 640, qkv.size * 6),
        name="attend_back",
    )(table, unit_seqs, qkv, grad, starts, lse)


def branch_kernel(off_ref, att_ref, x_ref, v_ref, *refs):
    residual_ref, h2_ref, mixed_ref, weight = refs[-4:]
    pairs = att_ref.shape[0]
    tokens = x_ref.shape[0]
    for pair in range(pairs):
        mixed_ref[:, pair * LANES : (pair + 1) * LANES] = att_ref[pair].reshape(tokens, LANES)
    place_columns(weight, off_ref, refs[:-4])
    residual = (
        x_ref[...].astype(F32) + dot(mixed_ref[...], weight[...]) + v_ref[V_BO : V_BO + 1, :]
    )
    residual_ref[...] = residual
    hat, _ = norm_stats(residual)
    h2_ref[...] = (hat * v_ref[V_G2 : V_G2 + 1, :] + v_ref[V_B2 : V_B2 + 1, :]).astype(BF16)


def branch(att, x, vectors, parts):
    arrays, offsets = parts
    tokens, features = x.shape
    return pl.pallas_call(
        branch_kernel,
        grid_spec=pltpu.PrefetchScalarGridSpec(
            num_scalar_prefetch=1,
            grid=(1,),
            in_specs=[whole(att.shape), whole(x.shape), whole(vectors.shape)]
            + [whole(array.shape) for array in arrays],
            out_specs=[whole(x.shape)] * 3,
            scratch_shapes=[pltpu.VMEM((features, features), BF16)],
        ),
        out_shape=[
            jax.ShapeDtypeStruct(x.shape, F32),
            jax.ShapeDtypeStruct(x.shape, BF16),
            jax.ShapeDtypeStruct(x.shape, BF16),
        ],
        compiler_params=params(),
        cost_estimate=cost(2 * tokens * features * features, 2 * features * features),
        name="branch",
    )(offsets, att, x, vectors, *arrays)


def ffn_kernel(
    expand_count,
    shrink_count,
    steps,
    sc_ref,
    residual_ref,
    h2_ref,
    h2_other_ref,
    og_ref,
    og_other_ref,
    v_ref,
    eb_ref,
    *refs,
):
    expand_parts = refs[:expand_count]
    shrink_parts = refs[expand_count : expand_count + shrink_count]
    (
        send_ref,
        keep_ref,
        send_s,
        keep_s,
        send_e,
        keep_e,
        eb_grad_ref,
        sb_grad_ref,
        expand,
        shrink,
        total,
        back,
        h2,
        h2_t,
        og,
    ) = refs[expand_count + shrink_count :]
    step = pl.program_id(0)
    y_index = sc_ref[0]
    low_label = sc_ref[2]
    expand_offsets = [sc_ref[4 + i] for i in range(expand_count)]
    shrink_offsets = [sc_ref[4 + expand_count + i] for i in range(shrink_count)]
    tokens = h2_ref.shape[0]

    @pl.when(step == 0)
    def _():
        total[:tokens] = residual_ref[...] + v_ref[V_BS : V_BS + 1, :]
        total[tokens:] = jnp.zeros_like(residual_ref)
        back[...] = jnp.zeros_like(back)
        h2[:tokens] = h2_ref[...]
        h2[tokens:] = h2_other_ref[...]
        og[:tokens] = og_ref[...]
        og[tokens:] = og_other_ref[...]
        h2_t[...] = h2[...].astype(F32).T.astype(BF16)
        sb_grad_ref[...] = jnp.sum(og_ref[...].astype(F32), axis=0, keepdims=True)

    place_rows(expand, expand_offsets, expand_parts)
    place_columns(shrink, shrink_offsets, shrink_parts)
    pre = dot(h2[...], expand[...]) + eb_ref[...]
    root = math.sqrt(2.0 / math.pi)
    square = pre * pre
    curve = jnp.tanh(root * (pre + 0.044715 * (square * pre)))
    slope = 0.5 * (1.0 + curve)
    active = (pre * slope).astype(BF16)
    slope = slope + (0.5 * root) * pre * (1.0 - curve * curve) * (1.0 + 0.134145 * square)
    total[...] += dot(active, shrink[...])
    dpre = (dot_nt(og[...], shrink[...]) * slope).astype(BF16)
    eb_grad_ref[...] = jnp.sum(dpre.astype(F32), axis=0, keepdims=True)
    back[...] += dot_nt(dpre, expand[...])
    shrink_grad = dot_tn(active, og[...]).astype(BF16)
    expand_grad = dot(h2_t[...], dpre).astype(BF16)

    fsdp_half, _, subs, rows, columns = send_s.shape
    for part in range(2 * fsdp_half):
        there = slice(part * columns, (part + 1) * columns)
        place = part ^ y_index

        def store_s(target, there=there, place=place):
            for sub in range(subs):
                here = slice(sub * rows, (sub + 1) * rows)
                target[place & (fsdp_half - 1), 0, sub ^ low_label] = shrink_grad[here, there]

        pl.when(place < fsdp_half)(functools.partial(store_s, keep_s))
        pl.when(place >= fsdp_half)(functools.partial(store_s, send_s))
    for sub in range(subs):
        here = slice(sub * rows, (sub + 1) * rows)
        place = sub ^ low_label

        def store_e(target, here=here, place=place):
            for part in range(2 * fsdp_half):
                there = slice(part * columns, (part + 1) * columns)
                target[part ^ y_index, 0, place >> 1] = expand_grad[there, here]

        pl.when((place & 1) == 0)(functools.partial(store_e, keep_e))
        pl.when((place & 1) == 1)(functools.partial(store_e, send_e))

    @pl.when(step == steps - 1)
    def _():
        keep_ref[0] = back[:tokens]
        keep_ref[1] = total[:tokens]
        send_ref[0] = back[tokens:]
        send_ref[1] = total[tokens:]


def feed_scalars(place, hidden, width, expand_offsets, shrink_offsets):
    (_, ctx_size), y_index, c_index = place
    subs = width * ctx_size // hidden
    label = c_index >> 1
    first = [y_index, label >> bits_of(subs), label & (subs - 1), c_index & 1]
    return jnp.concatenate([jnp.stack(first), expand_offsets, shrink_offsets])


def feed_forward(
    scalars, residual, h2, h2_other, og, og_other, vectors, expand_bias, expand, shrink, sizes
):
    fsdp_size, ctx_size = sizes
    expand_arrays = expand[0]
    shrink_arrays = shrink[0]
    tokens, features = h2.shape
    hidden = expand_bias.shape[1]
    rows = hidden // ctx_size
    columns = features // fsdp_size
    width = WIDTH
    subs = width // rows
    steps = hidden // (2 * width)
    def chunk(array, dim):
        if array.shape[dim] == hidden:
            return lambda s, sc: sc[3] * steps + (s ^ sc[1])
        return lambda s, sc: s ^ sc[1]

    def columns_of(array):
        index = chunk(array, 1)
        return pl.BlockSpec((array.shape[0], width), lambda s, sc: (0, index(s, sc)))

    def rows_of(array):
        index = chunk(array, 0)
        return pl.BlockSpec((width, array.shape[1]), lambda s, sc: (index(s, sc), 0))

    grad_s = (fsdp_size // 2, steps, subs, rows, columns)
    grad_e = (fsdp_size, steps, subs // 2, columns, rows)

    def block(shape):
        return pl.BlockSpec((shape[0], 1) + shape[2:], lambda s, sc: (0, s, 0, 0, 0))

    full = whole(h2.shape)
    wide = jax.ShapeDtypeStruct((2,) + h2.shape, F32)
    return pl.pallas_call(
        functools.partial(ffn_kernel, len(expand_arrays), len(shrink_arrays), steps),
        grid_spec=pltpu.PrefetchScalarGridSpec(
            num_scalar_prefetch=1,
            grid=(steps,),
            in_specs=[full] * 5
            + [whole(vectors.shape), columns_of(expand_bias)]
            + [columns_of(array) for array in expand_arrays]
            + [rows_of(array) for array in shrink_arrays],
            out_specs=[whole(wide.shape)] * 2
            + [block(grad_s)] * 2
            + [block(grad_e)] * 2
            + [pl.BlockSpec((1, width), lambda s, sc: (0, s ^ sc[1])), whole((1, features))],
            scratch_shapes=[
                pltpu.VMEM((features, width), BF16),
                pltpu.VMEM((width, features), BF16),
                pltpu.VMEM((2 * tokens, features), F32),
                pltpu.VMEM((2 * tokens, features), F32),
                pltpu.VMEM((2 * tokens, features), BF16),
                pltpu.VMEM((features, 2 * tokens), BF16),
                pltpu.VMEM((2 * tokens, features), BF16),
            ],
        ),
        out_shape=[wide] * 2
        + [jax.ShapeDtypeStruct(grad_s, BF16)] * 2
        + [jax.ShapeDtypeStruct(grad_e, BF16)] * 2
        + [
            jax.ShapeDtypeStruct((1, hidden // 2), F32),
            jax.ShapeDtypeStruct((1, features), F32),
        ],
        compiler_params=params(),
        cost_estimate=cost(0, 0),
        name="feed_forward",
    )(
        scalars,
        residual,
        h2,
        h2_other,
        og,
        og_other,
        vectors,
        expand_bias,
        *expand_arrays,
        *shrink_arrays,
    )


def branch_back_kernel(
    part_count, seqs, rows, sc_ref, dh2_ref, dh2_other_ref, residual_ref, og_ref, mixed_ref, v_ref, *refs
):
    parts = refs[:part_count]
    dres_ref, dmixed_ref, keep_ref, send_ref, vec_ref, weight, rounded = refs[part_count:]
    place_columns(weight, sc_ref, parts)
    hat, rate = norm_stats(residual_ref[...])
    dh2 = dh2_ref[0] + dh2_other_ref[0]
    scaled = dh2 * v_ref[V_G2 : V_G2 + 1, :]
    first = jnp.mean(scaled, axis=-1, keepdims=True)
    second = jnp.mean(scaled * hat, axis=-1, keepdims=True)
    dres = og_ref[...].astype(F32) + rate * (scaled - first - hat * second)
    dres_ref[...] = dres
    rounded[...] = dres.astype(BF16)
    vec_ref[0:1, :] = jnp.sum(dh2 * hat, axis=0, keepdims=True)
    vec_ref[1:2, :] = jnp.sum(dh2, axis=0, keepdims=True)
    vec_ref[2:3, :] = jnp.sum(rounded[...].astype(F32), axis=0, keepdims=True)
    vec_ref[3:, :] = jnp.zeros((vec_ref.shape[0] - 3, vec_ref.shape[1]), F32)
    dmixed = dot_nt(rounded[...], weight[...]).astype(BF16)
    for pair in range(dmixed_ref.shape[0]):
        dmixed_ref[pair] = dmixed[:, pair * LANES : (pair + 1) * LANES].reshape(seqs, rows, LANES)
    fsdp_size, count, size, columns = keep_ref.shape
    grad = dot_tn(mixed_ref[...], rounded[...]).astype(BF16)
    y_index = sc_ref[part_count]
    label = sc_ref[part_count + 1]
    for number in range(2 * count):
        place = number ^ label

        def store(target, number=number, place=place):
            for part in range(fsdp_size):
                target[part ^ y_index, place >> 1] = grad[
                    number * size : (number + 1) * size, part * columns : (part + 1) * columns
                ]

        pl.when((place & 1) == 0)(functools.partial(store, keep_ref))
        pl.when((place & 1) == 1)(functools.partial(store, send_ref))


def branch_back(scalars, dh2, dh2_other, residual, og, mixed, vectors, parts, sizes, seqs, rows):
    fsdp_size, ctx_size = sizes
    arrays, offsets = parts
    tokens, features = residual.shape
    pairs = features // LANES
    grad = (fsdp_size, ctx_size // 2, features // ctx_size, features // fsdp_size)
    full = whole(residual.shape)
    half = pl.BlockSpec((1,) + residual.shape, lambda n, o: (0, 0, 0))
    return pl.pallas_call(
        functools.partial(branch_back_kernel, len(arrays), seqs, rows),
        grid_spec=pltpu.PrefetchScalarGridSpec(
            num_scalar_prefetch=1,
            grid=(1,),
            in_specs=[half] * 2 + [full] * 3 + [whole(vectors.shape)]
            + [whole(array.shape) for array in arrays],
            out_specs=[
                full,
                whole((pairs, seqs, rows, LANES)),
                whole(grad),
                whole(grad),
                whole((8, features)),
            ],
            scratch_shapes=[
                pltpu.VMEM((features, features), BF16),
                pltpu.VMEM((tokens, features), BF16),
            ],
        ),
        out_shape=[
            jax.ShapeDtypeStruct(residual.shape, F32),
            jax.ShapeDtypeStruct((pairs, seqs, rows, LANES), BF16),
            jax.ShapeDtypeStruct(grad, BF16),
            jax.ShapeDtypeStruct(grad, BF16),
            jax.ShapeDtypeStruct((8, features), F32),
        ],
        compiler_params=params(),
        cost_estimate=cost(4 * tokens * features * features, 8 * features * features),
        name="branch_back",
    )(scalars, dh2, dh2_other, residual, og, mixed, vectors, *arrays)


def input_terms_kernel(sc_ref, h_ref, d_ref, keep_ref, send_ref, token_ref):
    token_ref[...] = jnp.zeros_like(token_ref)
    left = h_ref[...].reshape(-1, h_ref.shape[-1])
    right = d_ref[...].reshape(-1, d_ref.shape[-1])
    value = dot_tn(left, right).astype(BF16)
    half, fsdp_size, rows, _ = keep_ref.shape
    per = value.shape[0] // rows
    for number in range(per):
        place = pl.program_id(0) * per + number
        part = (place // (2 * half)) ^ sc_ref[1]
        own = (place & (2 * half - 1)) ^ sc_ref[2]

        def store(target, number=number, part=part, own=own):
            target[own & (half - 1), part] = value[number * rows : (number + 1) * rows]

        pl.when(own < half)(functools.partial(store, keep_ref))
        pl.when(own >= half)(functools.partial(store, send_ref))


def input_weight_terms(gathered, dqkv, scalars, low, fsdp_size):
    ctx_size, units, rows, width = dqkv.shape
    features = gathered.shape[-1]
    block = 2 * LANES
    out = (low // 2, fsdp_size, features // (low * fsdp_size), width)
    return pl.pallas_call(
        input_terms_kernel,
        grid_spec=pltpu.PrefetchScalarGridSpec(
            num_scalar_prefetch=1,
            grid=(features // block,),
            in_specs=[
                pl.BlockSpec((ctx_size, units, rows, block), lambda g, s: (0, s[0], 0, g)),
                whole(dqkv.shape),
            ],
            out_specs=[whole(out), whole(out), whole(TOKEN.shape)],
        ),
        out_shape=[jax.ShapeDtypeStruct(out, BF16)] * 2 + [TOKEN],
        compiler_params=params(),
        cost_estimate=cost(0, 0),
        name="input_weight_terms",
    )(scalars, gathered, dqkv)


def entry_back_kernel(
    part_count,
    groups,
    off_ref,
    d_ref,
    x_ref,
    dres_ref,
    one_ref,
    two_ref,
    second_ref,
    sb_ref,
    eb_ref,
    v_ref,
    *refs,
):
    parts = refs[: 3 * part_count]
    out_ref, layer_ref, vec_ref, weight, back = refs[3 * part_count :]
    group = pl.program_id(0)
    tokens = x_ref.shape[0]
    width = weight.shape[-1]

    @pl.when(group == 0)
    def _():
        back[...] = jnp.zeros_like(back)
        layer_ref[...] = (one_ref[0] + two_ref[0]).astype(BF16)
        vec_ref[4:7, :] = second_ref[0:3, :]
        vec_ref[7:8, :] = sb_ref[...]
        count = vec_ref.shape[0] - 8
        core = off_ref[off_ref.shape[0] - 1]
        for row in range(count):
            here = eb_ref[:, (row % (count // 2)) * LANES * 8 : (row % (count // 2) + 1) * LANES * 8]
            mine = core == row // (count // 2)
            vec_ref[8 + row : 9 + row, :] = jnp.where(mine, here, jnp.zeros_like(here))

    for kind in range(3):
        place_rows(
            weight.at[kind], off_ref, parts[kind * part_count : (kind + 1) * part_count]
        )
        lanes = slice(kind * LANES, (kind + 1) * LANES)
        value = jnp.concatenate(
            [d_ref[pair, :, :, lanes].reshape(tokens, LANES) for pair in range(d_ref.shape[0])],
            axis=1,
        )
        back[...] += dot_nt(value, weight[kind])
        if kind != 1:
            row = 2 if kind == 0 else 3
            start = pl.multiple_of(group * width, LANES)
            vec_ref[row : row + 1, pl.ds(start, width)] = jnp.sum(
                value.astype(F32), axis=0, keepdims=True
            )

    @pl.when(group == groups - 1)
    def _():
        hat, rate = norm_stats(x_ref[...].astype(F32))
        dh1 = back[...]
        scaled = dh1 * v_ref[V_G1 : V_G1 + 1, :]
        first = jnp.mean(scaled, axis=-1, keepdims=True)
        second = jnp.mean(scaled * hat, axis=-1, keepdims=True)
        out_ref[...] = dres_ref[...] + rate * (scaled - first - hat * second)
        vec_ref[0:1, :] = jnp.sum(dh1 * hat, axis=0, keepdims=True)
        vec_ref[1:2, :] = jnp.sum(dh1, axis=0, keepdims=True)


def entry_back(dqkv, x, dres, one, two, sums, vectors, parts):
    arrays, offsets = parts
    tokens, features = x.shape
    pairs, seqs, rows, _ = dqkv.shape
    width = 2 * LANES
    vec = (8 + 2 * sums[2].shape[1] // features, features)
    groups = features // width
    specs = []
    operands = []
    for kind in range(3):
        for array in arrays:
            specs.append(
                pl.BlockSpec((array.shape[0], width), lambda g, o, k=kind: (0, k * groups + g))
            )
            operands.append(array)
    return pl.pallas_call(
        functools.partial(entry_back_kernel, len(arrays), groups),
        grid_spec=pltpu.PrefetchScalarGridSpec(
            num_scalar_prefetch=1,
            grid=(groups,),
            in_specs=[
                pl.BlockSpec((2, seqs, rows, 3 * LANES), lambda g, o: (g, 0, 0, 0)),
                whole(x.shape),
                whole(x.shape),
                pl.BlockSpec((1,) + x.shape, lambda g, o: (1, 0, 0)),
                pl.BlockSpec((1,) + x.shape, lambda g, o: (1, 0, 0)),
            ]
            + [whole(array.shape) for array in sums]
            + [whole(vectors.shape)]
            + specs,
            out_specs=[whole(x.shape), whole(x.shape), whole(vec)],
            scratch_shapes=[
                pltpu.VMEM((3, features, width), BF16),
                pltpu.VMEM((tokens, features), F32),
            ],
        ),
        out_shape=[
            jax.ShapeDtypeStruct(x.shape, F32),
            jax.ShapeDtypeStruct(x.shape, BF16),
            jax.ShapeDtypeStruct(vec, F32),
        ],
        compiler_params=params(),
        cost_estimate=cost(6 * tokens * features * features, 6 * features * features),
        name="entry_back",
    )(offsets, dqkv, x, dres, one, two, *sums, vectors, *operands)


def combine_kernel(one_ref, two_ref, send_ref, keep_ref):
    total = (one_ref[...].astype(F32) + two_ref[...].astype(F32)).astype(BF16)
    keep_ref[...] = total[:, 0]
    send_ref[...] = total[:, 1]


def last_kernel(one_ref, two_ref, out_ref):
    out_ref[...] = (one_ref[...].astype(F32) + two_ref[...].astype(F32)).astype(BF16)


def combine(one, two, outer):
    rows, columns = one.shape[-2:]
    shape = (outer, 2, one.size // (2 * outer * rows * columns), rows, columns)
    inner = shape[2]
    per = inner
    while per * rows * columns > 256 * 1024 and per % 2 == 0:
        per //= 2
    half = (outer, inner, rows, columns)
    block = pl.BlockSpec((1, 2, per, rows, columns), lambda a, b: (a, 0, b, 0, 0))
    out = pl.BlockSpec((1, per, rows, columns), lambda a, b: (a, b, 0, 0))
    return pl.pallas_call(
        combine_kernel,
        grid=(outer, inner // per),
        in_specs=[block, block],
        out_specs=[out, out],
        out_shape=[jax.ShapeDtypeStruct(half, BF16)] * 2,
        compiler_params=params(),
        cost_estimate=cost(0, 0),
        name="combine",
    )(one.reshape(shape), two.reshape(shape))


def add_last(one, two):
    rows, columns = one.shape[-2:]
    return pl.pallas_call(
        last_kernel,
        out_shape=jax.ShapeDtypeStruct((1, rows, columns), BF16),
        compiler_params=params(),
        cost_estimate=cost(0, 0),
        name="add_last",
    )(one.reshape(1, rows, columns), two.reshape(1, rows, columns))


def merge_kernel(one_ref, two_ref, out_ref):
    out_ref[:, 0] = one_ref[...]
    out_ref[:, 1] = two_ref[...]


def merge(one, two):
    count, rows, columns = one.shape
    block = pl.BlockSpec((1, rows, columns), lambda n: (n, 0, 0))
    return pl.pallas_call(
        merge_kernel,
        grid=(count,),
        in_specs=[block, block],
        out_specs=pl.BlockSpec((1, 2, rows, columns), lambda n: (n, 0, 0, 0)),
        out_shape=jax.ShapeDtypeStruct((count, 2, rows, columns), BF16),
        compiler_params=params(),
        cost_estimate=cost(0, 0),
        name="merge",
    )(one, two).reshape(2 * count, rows, columns)


def tiles(rows, width, columns):
    count = columns // LANES
    height = rows // count
    return height, [
        (across * height, down * LANES, down * height, across * LANES)
        for down in range(width // LANES)
        for across in range(count)
    ]


def pack_kernel(one_ref, two_ref, extra_ref, out_ref):
    rows, columns = one_ref.shape[1:]
    first = out_ref.shape[1] - rows
    out_ref[:, first:] = (one_ref[...].astype(F32) + two_ref[...].astype(F32)).astype(BF16)
    height, moves = tiles(*extra_ref.shape, columns)
    for row, column, to_row, to_column in moves:
        out_ref[0, to_row : to_row + height, to_column : to_column + LANES] = extra_ref[
            row : row + height, column : column + LANES
        ]


def pack(one, two, extra):
    rows, columns = one.shape[-2:]
    return pl.pallas_call(
        pack_kernel,
        out_shape=jax.ShapeDtypeStruct((1, rows + extra.size // columns, columns), BF16),
        compiler_params=params(),
        cost_estimate=cost(0, 0),
        name="pack",
    )(one.reshape(1, rows, columns), two.reshape(1, rows, columns), extra)


def join_kernel(one_ref, two_ref, extra_one_ref, extra_two_ref, send_ref, keep_ref):
    rows, columns = one_ref.shape[-2:]
    height, moves = tiles(*extra_one_ref.shape[-2:], columns)
    first = keep_ref.shape[1] - rows
    for half, target in ((0, keep_ref), (1, send_ref)):
        value = one_ref[0, half].astype(F32) + two_ref[0, half].astype(F32)
        target[0, first:] = value.astype(BF16)
        value = extra_one_ref[0, half].astype(F32) + extra_two_ref[0, half].astype(F32)
        value = value.astype(BF16)
        for row, column, to_row, to_column in moves:
            target[0, to_row : to_row + height, to_column : to_column + LANES] = value[
                row : row + height, column : column + LANES
            ]


def join(one, two, extra_one, extra_two, outer):
    rows, columns = one.shape[-2:]
    extra_rows, extra_columns = extra_one.shape[-2:]
    height = rows + extra_rows * extra_columns // columns
    block = pl.BlockSpec((1, 2, rows, columns), lambda n: (n, 0, 0, 0))
    extra = pl.BlockSpec((1, 2, extra_rows, extra_columns), lambda n: (n, 0, 0, 0))
    out = pl.BlockSpec((1, height, columns), lambda n: (n, 0, 0))
    shape = (outer, 2, rows, columns)
    extra_shape = (outer, 2, extra_rows, extra_columns)
    return pl.pallas_call(
        join_kernel,
        grid=(outer,),
        in_specs=[block, block, extra, extra],
        out_specs=[out, out],
        out_shape=[jax.ShapeDtypeStruct((outer, height, columns), BF16)] * 2,
        compiler_params=params(),
        cost_estimate=cost(0, 0),
        name="join",
    )(
        one.reshape(shape),
        two.reshape(shape),
        extra_one.reshape(extra_shape),
        extra_two.reshape(extra_shape),
    )


class Flow:
    def __init__(self, send, keep, first, labels, order, sizes):
        self.sizes = dict(fsdp=sizes[0], ctx=sizes[1])
        self.labels = list(labels)
        self.order = list(order)
        self.keep = keep
        self.spreading = None
        self.extra = None
        self.received = self.swap(send, first)

    def swap(self, value, label):
        return swap_bit(value, label[0], self.sizes[label[0]], label[1])

    def step(self, event):
        received = after(self.received, event)
        if self.order:
            label = self.order.pop(0)
            place = self.labels.index(label)
            self.labels.pop(place)
            send, self.keep = combine(self.keep, received, 1 << place)
            self.received = self.swap(send, label)
        elif self.spreading is None:
            if self.extra is None:
                self.keep = add_last(self.keep, received)
            else:
                self.keep = pack(self.keep, received, self.extra)
            self.received = None
        else:
            if self.spreading:
                self.keep = merge(self.keep, received)
                self.received = self.swap(self.keep, self.spreading.pop(0))
            else:
                self.far = received
                self.received = None
        return self

    def join(self, other, event):
        received = after(self.received, event)
        label = self.order.pop(0)
        assert self.labels[-1] == label
        self.labels.pop()
        send, self.keep = join(
            self.keep, received, other.keep, other.received, 1 << len(self.labels)
        )
        self.received = self.swap(send, label)
        other.received = None
        return self

    def spread(self, bits):
        self.spreading = [("ctx", bit) for bit in bits]
        self.received = self.swap(self.keep, self.spreading.pop(0))


def places(bits):
    count = len(bits) - 1
    return [
        sum(((number >> (count - 1 - turn)) & 1) << (bits[turn] - 1) for turn in range(count))
        for number in range(1 << count)
    ]


def finish_kernel(dim, order, label_ref, source, *refs):
    out_ref, token_ref = refs[-2:]
    token_ref[...] = jnp.zeros_like(token_ref)
    count, height, _ = source.shape
    rows, columns = out_ref.shape
    if dim == 0:
        rows = rows // count
    else:
        columns = columns // count
    first = height - rows
    low = label_ref[1] & (count - 1)
    for number in range(count):
        place = order[number] ^ low
        value = source[number, first:].astype(F32)
        if dim == 0:
            out_ref[pl.ds(pl.multiple_of(place * rows, LANES), rows), :] = value
        else:
            out_ref[:, pl.ds(pl.multiple_of(place * columns, LANES), columns)] = value


def finish(source, before, other, table, dim, rows, columns, bits):
    half, height, width = source.shape
    order = places(bits)
    group = half // 2 if bits[0] == max(bits) else half
    count = half // group
    shift = bits_of(group)

    def index(n, t):
        return (other ^ t[0]) * count + (n ^ (t[1] >> shift))

    if dim == 0:
        shape = (2 * half * rows, columns)
        out_spec = pl.BlockSpec((group * rows, columns), lambda n, t: (index(n, t), 0))
    else:
        shape = (rows, 2 * half * columns)
        out_spec = pl.BlockSpec((rows, group * columns), lambda n, t: (0, index(n, t)))
    earlier = [] if before is None else [before]
    return pl.pallas_call(
        functools.partial(finish_kernel, dim, order[:group]),
        grid_spec=pltpu.PrefetchScalarGridSpec(
            num_scalar_prefetch=1,
            grid=(count,),
            in_specs=[pl.BlockSpec((group, height, width), lambda n, t: (n, 0, 0))]
            + [pl.BlockSpec(memory_space=pl.ANY) for _ in earlier],
            out_specs=[out_spec, whole(TOKEN.shape)],
        ),
        out_shape=[jax.ShapeDtypeStruct(shape, F32), TOKEN],
        input_output_aliases={2: 0} if earlier else {},
        compiler_params=params(),
        cost_estimate=cost(0, 0),
        name="finish",
    )(table, source, *earlier)


def finish_extra_kernel(rows, width, low_bits, order, label_ref, near_ref, far_ref, *refs):
    out_ref, token_ref = refs[-2:]
    token_ref[...] = jnp.zeros_like(token_ref)
    half, _, columns = near_ref.shape
    height, moves = tiles(rows, width, columns)
    for number in range(2 * half):
        source = far_ref if number & 1 else near_ref
        owner = ((order[number >> 1] << 1) | (number & 1)) ^ ((label_ref[1] << 1) | label_ref[0])
        if low_bits is None:
            place, begin, stride = owner, 0, LANES
        else:
            place = owner & ((1 << low_bits) - 1)
            begin = (owner >> low_bits) * LANES
            stride = out_ref.shape[1] // (width // LANES)
        for row, column, from_row, from_column in moves:
            down = pl.ds(pl.multiple_of(place * rows + row, 32), height)
            across = begin + (column // LANES) * stride
            if low_bits is not None:
                across = pl.multiple_of(across, LANES)
            out_ref[down, pl.ds(across, LANES)] = source[
                number >> 1, from_row : from_row + height, from_column : from_column + LANES
            ].astype(F32)


def finish_extra(near, far, table, rows, width, low_bits, shape, bits, events=()):
    half, _, columns = near.shape
    block = pl.BlockSpec((half, rows * width // columns, columns), lambda n, t: (0, 0, 0))
    return pl.pallas_call(
        functools.partial(finish_extra_kernel, rows, width, low_bits, places(bits)),
        grid_spec=pltpu.PrefetchScalarGridSpec(
            num_scalar_prefetch=1,
            grid=(1,),
            in_specs=[block, block] + [whole(event.keep.shape) for event in events],
            out_specs=[whole(shape), whole(TOKEN.shape)],
        ),
        out_shape=[jax.ShapeDtypeStruct(shape, F32), TOKEN],
        compiler_params=params(),
        cost_estimate=cost(0, 0),
        name="finish_extra",
    )(table, near, far, *[event.keep for event in events])


class Total:
    def __init__(self, value, labels, sizes):
        self.keep = value
        self.sizes = dict(fsdp=sizes[0], ctx=sizes[1])
        self.labels = list(labels)
        self.start()

    def start(self):
        self.received = None
        if self.labels:
            name, bit = self.labels.pop(0)
            self.received = swap_bit(self.keep, name, self.sizes[name], bit)

    def step(self, event):
        received = after(self.received, event)
        self.keep = pl.pallas_call(
            total_kernel,
            out_shape=jax.ShapeDtypeStruct(self.keep.shape, F32),
            compiler_params=params(),
            cost_estimate=cost(0, 0),
            name="total",
        )(self.keep, received)
        self.start()
        return self


def total_kernel(one_ref, two_ref, out_ref):
    out_ref[...] = one_ref[...] + two_ref[...]


def body(
    sizes,
    layer_input,
    output_grad,
    segments,
    assignment,
    first_gain,
    first_bias,
    input_weight,
    query_bias,
    value_bias,
    output_weight,
    output_bias,
    second_gain,
    second_bias,
    expand_weight,
    expand_bias,
    shrink_weight,
    shrink_bias,
):
    fsdp_size, ctx_size = sizes
    seqs, rows, features = layer_input.shape
    tokens = seqs * rows
    hidden = expand_weight.shape[1]
    pairs = features // LANES
    units = seqs * pairs // ctx_size
    y_index = lax.axis_index("fsdp").astype(jnp.int32)
    c_index = lax.axis_index("ctx").astype(jnp.int32)
    part = features // fsdp_size
    small = jnp.concatenate(
        [
            first_gain,
            first_bias,
            query_bias,
            value_bias,
            output_bias,
            second_gain,
            second_bias,
            shrink_bias,
            expand_bias,
        ]
    )
    small = small.reshape(1, -1)
    x = layer_input.reshape(tokens, features)
    og = output_grad.reshape(tokens, features)
    place = (sizes, y_index, c_index)
    core = c_index & 1
    starts = jnp.sum(
        (segments[:, None, :] < segments[:, :, None]).astype(jnp.int32), axis=-1
    )[:, None, :]
    unit_seqs = (c_index * units + jnp.arange(units, dtype=jnp.int32)) & (seqs - 1)
    input_gather = Gather(input_weight, 0, place, (1, 0))
    output_gather = Gather(output_weight, 1, place, (0,))
    expand_gather = Gather(expand_weight, 0, place, (1,), core)
    shrink_gather = Gather(shrink_weight, 1, place, (), core)
    gathers = (input_gather, output_gather, expand_gather, shrink_gather)

    group = ((c_index * units) & (seqs - 1)) >> bits_of(units)
    low_bits = bits_of(ctx_size // pairs)
    low = 1 << low_bits
    if fsdp_size == 2:
        owners = jnp.stack([y_index, 1 - y_index])
    else:
        owners = jnp.arange(fsdp_size, dtype=jnp.int32)

    ready = (
        x,
        small,
        starts,
        [gather.first for gather in gathers[1:]],
        [
            unit_seqs,
            owners,
            input_gather.offsets,
            output_gather.offsets,
            feed_scalars(place, hidden, WIDTH, expand_gather.offsets, shrink_gather.offsets),
            jnp.stack([core, c_index >> 1]),
            jnp.concatenate([output_gather.offsets, jnp.stack([y_index, c_index])]),
            jnp.concatenate([input_gather.offsets, core[None]]),
            jnp.stack([group, y_index, c_index & (low - 1)]),
        ],
    )
    x, small, starts, firsts, tables = lax.optimization_barrier(ready)
    for gather, first in zip(gathers[1:], firsts):
        gather.first = first
    unit_seqs, owners, input_gather.offsets, output_gather.offsets, *tables = tables
    feed_table, finish_table, back_table, entry_table, terms_table = tables

    input_gather.fetch()
    if fsdp_size == 2:
        small_other = Event(swap_bit(small, "fsdp", 2, 0))
        input_gather.keep = after(input_gather.keep, small_other)
        shards = [small, small_other.keep]
    else:
        full = lax.all_gather(small, "fsdp", axis=0)
        shards = [full[number] for number in range(fsdp_size)]
    h1, vectors, expand_vector = first_norm(x, shards, owners, hidden)
    other = Event(swap_bit(og, "ctx", ctx_size, 0))
    expand_gather.fetch(input_gather)
    input_gather.exchange()
    norm_done = Event(h1)
    input_gather.keep = after(input_gather.keep, norm_done)
    h1 = norm_done.keep
    input_gather.exchange()
    expand_first = Event(after(expand_gather.keep, input_gather))
    expand_gather.exchange()
    output_gather.fetch(expand_first)
    h1 = after(h1, expand_first)
    qkv, token = project(h1, vectors, input_gather.result(), seqs, rows)
    expand_gather.held[0] = expand_first.keep
    project_done = Event(token)
    shrink_gather.fetch(output_gather)
    output_gather.exchange()
    output_gather.keep = after(output_gather.keep, project_done)
    qkv = qkv.reshape(ctx_size, units, rows, 3 * LANES)
    qkv = lax.all_to_all(qkv, "ctx", 0, 0, tiled=True)
    qkv = after(after(qkv, output_gather), other)
    og_other = other.keep
    att, lse = attend(assignment, unit_seqs, qkv, starts)
    attend_done = Event(lse)
    shrink_gather.keep = after(shrink_gather.keep, attend_done)
    att = lax.all_to_all(att, "ctx", 0, 0, tiled=True)
    received = Event(after(after(att, expand_gather), shrink_gather))
    gathered = lax.all_gather(
        after(h1, received).reshape(seqs, rows, features), "ctx", axis=0
    )
    att = received.keep.reshape(pairs, seqs, rows, LANES)
    output_parts = output_gather.result()
    residual, h2, mixed = branch(att, x, vectors, output_parts)
    h2_other = swap_bit(h2, "ctx", ctx_size, 0)
    send, keep, send_s, keep_s, send_e, keep_e, eb_grad, sb_grad = feed_forward(
        feed_table,
        residual,
        h2,
        h2_other,
        og,
        og_other,
        vectors,
        expand_vector,
        expand_gather.result(),
        shrink_gather.result(),
        sizes,
    )
    other = swap_bit(send, "ctx", ctx_size, 0)

    every = [("fsdp", bit) for bit in reversed(range(bits_of(fsdp_size)))]
    high = [("ctx", bit) for bit in reversed(range(1, bits_of(ctx_size)))]
    flow_s = Flow(send_s, keep_s, every[0], every[1:] + high, every[1:] + high[::-1], sizes)
    dres, dmixed, keep_o, send_o, vec_two = branch_back(
        back_table, keep, other, residual, og, mixed, vectors, output_parts, sizes, seqs, rows
    )
    branch_done = Event(vec_two)
    send_e = after(send_e, branch_done)
    flow_e = Flow(
        send_e, keep_e, high[-1], every + high[:-1], every + high[:-1][::-1], sizes
    )
    spread_s = [bit for _, bit in high] + [0]
    spread_e = [1] + [bit for bit in spread_s if bit > 1] + [0]
    flow_o = Flow(send_o, keep_o, ("ctx", 0), every + high, every + high[::-1], sizes)
    dmixed = dmixed.reshape(ctx_size, units, rows, LANES)
    dmixed = lax.all_to_all(dmixed, "ctx", 0, 0, tiled=True)
    dqkv, token = attend_back(
        assignment, unit_seqs, qkv, dmixed, starts, attend_done.keep
    )
    back_done = Event(token)
    last = flow_s.step(back_done)
    held = Event(after(dqkv, last))
    keep_i, send_i, token = input_weight_terms(gathered, held.keep, terms_table, low, fsdp_size)
    terms_done = Event(token)
    low_labels = [("ctx", bit) for bit in reversed(range(low_bits))]
    flow_i = Flow(
        send_i,
        keep_i,
        low_labels[0],
        low_labels[1:] + every,
        low_labels[1:] + every,
        sizes,
    )
    last = flow_e.step(terms_done)
    last = flow_i.step(last)
    last = flow_o.step(last)
    last = flow_s.step(last)
    while ("fsdp", 0) in flow_e.order:
        last = flow_e.step(last)
    dqkv = lax.all_to_all(dqkv, "ctx", 0, 0, tiled=True).reshape(pairs, seqs, rows, 3 * LANES)
    last = flow_o.step(last)
    while flow_i.received is not None:
        last = flow_i.step(last)
    last = flow_s.step(last)
    while len(flow_o.order) > len(flow_e.order):
        last = flow_o.step(last)
    flow_o.received = after(flow_o.received, last)
    last = flow_e.join(flow_o, last)
    flow_s.extra = flow_i.keep[0]
    while flow_s.order:
        last = flow_s.step(last)
    last = flow_s.step(last)
    flow_s.spread(spread_s)
    input_grad, out, sums = entry_back(
        after(dqkv, last),
        x,
        dres,
        keep,
        other,
        [branch_done.keep, sb_grad, eb_grad],
        vectors,
        (input_gather.result()[0], entry_table),
    )
    totals = Total(sums, every + high[::-1] + [("ctx", 0)], sizes)
    last = totals
    while flow_e.order:
        last = flow_e.step(last)
    last = flow_s.step(last)
    for _ in range(len(every) + 2):
        last = totals.step(last)
    last = flow_e.step(last)
    flow_e.spread(spread_e)
    while totals.labels:
        last = totals.step(last)
    last = flow_e.step(last)
    last = flow_s.step(last)
    while len(flow_e.spreading) > 1:
        last = flow_e.step(last)
    last = totals.step(last)
    while flow_s.spreading:
        last = flow_s.step(last)
    rows_s = hidden // ctx_size
    shrink_grad, token = finish(flow_s.keep, None, 0, finish_table, 0, rows_s, part, spread_s)
    shrink_done = Event(token)
    flow_e.received = after(flow_e.received, shrink_done)
    while flow_e.spreading:
        last = flow_e.step(last)
    last = flow_s.step(last)
    shrink_grad, token = finish(
        flow_s.far, shrink_grad, 1, finish_table, 0, rows_s, part, spread_s
    )
    input_grad_w, token = finish_extra(
        flow_s.keep,
        flow_s.far,
        finish_table,
        part >> low_bits,
        3 * LANES,
        low_bits,
        (part, 3 * features),
        spread_s,
    )
    input_done = Event(token)
    expand_grad, _ = finish(
        flow_e.keep, None, 0, finish_table, 1, part, rows_s, spread_e
    )
    flow_e.received = after(flow_e.received, input_done)
    last = flow_e.step(last)
    expand_grad, token = finish(
        flow_e.far, expand_grad, 1, finish_table, 1, part, rows_s, spread_e
    )
    expand_done = Event(token)
    output_grad_w, _ = finish_extra(
        flow_e.keep,
        flow_e.far,
        finish_table,
        features // ctx_size,
        part,
        None,
        (features, part),
        spread_e,
        [project_done, back_done, terms_done, branch_done, shrink_done, input_done, expand_done],
    )
    sums = totals.keep

    def own(vector):
        size = vector.shape[0] // fsdp_size
        return lax.dynamic_slice_in_dim(vector, y_index * size, size, 0)

    return (
        out.reshape(seqs, rows, features),
        input_grad.reshape(seqs, rows, features),
        own(sums[0]),
        own(sums[1]),
        input_grad_w,
        own(sums[2]),
        own(sums[3]),
        output_grad_w,
        own(sums[6]),
        own(sums[4]),
        own(sums[5]),
        expand_grad,
        own(sums[8:].reshape(-1)),
        shrink_grad,
        own(sums[7]),
    )


def solution(mesh):
    sizes = (mesh.shape["fsdp"], mesh.shape["ctx"])
    return jax.shard_map(
        functools.partial(body, sizes),
        mesh=mesh,
        in_specs=(
            P("fsdp", "ctx", None),
            P("fsdp", "ctx", None),
            P("fsdp", None),
            P(),
            P("fsdp"),
            P("fsdp"),
            P("fsdp", None),
            P("fsdp"),
            P("fsdp"),
            P(None, "fsdp"),
            P("fsdp"),
            P("fsdp"),
            P("fsdp"),
            P("fsdp", None),
            P("fsdp"),
            P(None, "fsdp"),
            P("fsdp"),
        ),
        out_specs=(
            P("fsdp", "ctx", None),
            P("fsdp", "ctx", None),
            P("fsdp"),
            P("fsdp"),
            P("fsdp", None),
            P("fsdp"),
            P("fsdp"),
            P(None, "fsdp"),
            P("fsdp"),
            P("fsdp"),
            P("fsdp"),
            P("fsdp", None),
            P("fsdp"),
            P(None, "fsdp"),
            P("fsdp"),
        ),
        check_vma=False,
    )
```

```python
import functools
import math

import jax
import jax.numpy as jnp
from jax import lax
from jax.experimental import pallas as pl
from jax.experimental.pallas import tpu as pltpu
from jax.sharding import PartitionSpec as P

HEADS = 16
EPSILON = 1e-05
MASKED = -1000000000.0
LANES = 128
WIDTH = 512
MIB = 1024 * 1024
F32 = jnp.float32
BF16 = jnp.bfloat16
TOKEN = jax.ShapeDtypeStruct((8, LANES), F32)

V_G1, V_B1, V_BQ, V_BV, V_BO, V_G2, V_B2, V_BS = range(8)


def bits_of(number):
    return number.bit_length() - 1


def dot(left, right):
    return jnp.dot(left, right, preferred_element_type=F32)


def dot_nt(left, right):
    return lax.dot_general(left, right, (((1,), (1,)), ((), ())), preferred_element_type=F32)


def dot_tn(left, right):
    return lax.dot_general(left, right, (((0,), (0,)), ((), ())), preferred_element_type=F32)


def swap_bit(value, axis, size, bit):
    return lax.ppermute(value, axis, [(i, i ^ (1 << bit)) for i in range(size)])


class Event:
    def __init__(self, keep):
        self.keep = keep


def after(value, event):
    value, event.keep = lax.optimization_barrier((value, event.keep))
    return value


def params(limit_mib=48):
    return pltpu.CompilerParams(vmem_limit_bytes=limit_mib * MIB)


def whole(shape):
    rank = len(shape)
    return pl.BlockSpec(tuple(shape), lambda *_: (0,) * rank)


def cost(flops, moved):
    return pl.CostEstimate(flops=0, bytes_accessed=0, transcendentals=0)


class Gather:
    def __init__(self, weight, dim, place, bits, core=None):
        (fsdp_size, self.ctx_size), y_index, c_index = place
        extent = weight.shape[dim]
        self.bits = bits
        self.stage = 0
        self.two = fsdp_size == 2
        if not self.two:
            self.bits = ()
            self.parts = []
            self.first = lax.all_gather(weight, "fsdp", axis=dim, tiled=True)
            self.offsets = jnp.zeros((1,), jnp.int32)
            self.held = [self.first]
            return
        size = extent >> len(bits)
        mine = jnp.int32(0)
        for number, bit in enumerate(bits):
            mine = mine | (((c_index >> bit) & 1) << number)
        if core is None:
            self.first = lax.dynamic_slice_in_dim(weight, mine * size, size, dim)
        else:
            half = weight.shape[1 - dim] // 2
            begins = (mine * size, core * half) if dim == 0 else (core * half, mine * size)
            self.first = lax.dynamic_slice(
                weight, begins, (size, half) if dim == 0 else (half, size)
            )
        order = y_index * extent + jnp.zeros((1,), jnp.int32)
        numbers = mine ^ jnp.arange(1 << len(bits), dtype=jnp.int32)
        self.offsets = jnp.concatenate([order, (1 - y_index) * extent + numbers * size])
        self.parts = [weight]

    def fetch(self, event=None):
        if not self.two:
            return
        first = self.first if event is None else after(self.first, event)
        self.held = [swap_bit(first, "fsdp", 2, 0)]

    @property
    def keep(self):
        return self.held[-1]

    @keep.setter
    def keep(self, value):
        self.held[-1] = value

    def exchange(self, event=None):
        if self.stage == len(self.bits):
            return
        bit = self.bits[self.stage]
        if event is not None:
            self.keep = after(self.keep, event)
        self.held = self.held + [swap_bit(array, "ctx", self.ctx_size, bit) for array in self.held]
        self.stage += 1

    def result(self):
        return self.parts + self.held, self.offsets


def place_rows(target, offsets, part_refs):
    for number, ref in enumerate(part_refs):
        rows = ref.shape[0]
        target[pl.ds(pl.multiple_of(offsets[number], 32), rows), :] = ref[...]


def place_columns(target, offsets, part_refs):
    for number, ref in enumerate(part_refs):
        columns = ref.shape[1]
        target[:, pl.ds(pl.multiple_of(offsets[number], LANES), columns)] = ref[...]


def norm_stats(values):
    center = values - jnp.mean(values, axis=-1, keepdims=True)
    spread = jnp.mean(center * center, axis=-1, keepdims=True)
    rate = lax.rsqrt(spread + EPSILON)
    return center * rate, rate


def norm_kernel(sc_ref, x_ref, *refs):
    shards = refs[:-3]
    h_ref, v_ref, e_ref = refs[-3:]
    part = v_ref.shape[1] // len(shards)
    hidden = e_ref.shape[1] // len(shards)
    for number, ref in enumerate(shards):
        where = sc_ref[number]
        for row in range(8):
            v_ref[row : row + 1, pl.ds(pl.multiple_of(where * part, LANES), part)] = ref[
                :, row * part : (row + 1) * part
            ].astype(F32)
        e_ref[:, pl.ds(pl.multiple_of(where * hidden, LANES), hidden)] = ref[:, 8 * part :].astype(
            F32
        )
    hat, _ = norm_stats(x_ref[...].astype(F32))
    h_ref[...] = (hat * v_ref[V_G1 : V_G1 + 1, :] + v_ref[V_B1 : V_B1 + 1, :]).astype(BF16)


def first_norm(x, shards, owners, hidden):
    shapes = [
        jax.ShapeDtypeStruct(x.shape, BF16),
        jax.ShapeDtypeStruct((8, x.shape[1]), F32),
        jax.ShapeDtypeStruct((1, hidden), F32),
    ]
    return pl.pallas_call(
        norm_kernel,
        grid_spec=pltpu.PrefetchScalarGridSpec(
            num_scalar_prefetch=1,
            grid=(1,),
            in_specs=[whole(x.shape)] + [whole(shard.shape) for shard in shards],
            out_specs=[whole(shape.shape) for shape in shapes],
        ),
        out_shape=shapes,
        compiler_params=params(),
        cost_estimate=cost(0, 0),
        name="first_norm",
    )(owners, x, *shards)


def qkv_kernel(part_count, seqs, rows, off_ref, h_ref, v_ref, *refs):
    parts = refs[: 3 * part_count]
    out_ref, token_ref, weight = refs[3 * part_count :]
    token_ref[...] = jnp.zeros_like(token_ref)
    group = pl.program_id(0)
    width = weight.shape[-1]
    per = width // LANES
    for kind in range(3):
        place_rows(
            weight.at[kind], off_ref, parts[kind * part_count : (kind + 1) * part_count]
        )
        value = dot(h_ref[...], weight[kind])
        if kind != 1:
            row = V_BQ if kind == 0 else V_BV
            start = pl.multiple_of(group * width, LANES)
            value = value + v_ref[row : row + 1, pl.ds(start, width)]
        value = value.astype(BF16)
        for pair in range(per):
            out_ref[pair, :, :, kind * LANES : (kind + 1) * LANES] = value[
                :, pair * LANES : (pair + 1) * LANES
            ].reshape(seqs, rows, LANES)


def project(h1, vectors, parts, seqs, rows):
    arrays, offsets = parts
    tokens, features = h1.shape
    width = 2 * LANES
    groups = features // width
    pairs = features // LANES
    specs = []
    operands = []
    for kind in range(3):
        for array in arrays:
            specs.append(
                pl.BlockSpec((array.shape[0], width), lambda g, o, k=kind: (0, k * groups + g))
            )
            operands.append(array)
    return pl.pallas_call(
        functools.partial(qkv_kernel, len(arrays), seqs, rows),
        grid_spec=pltpu.PrefetchScalarGridSpec(
            num_scalar_prefetch=1,
            grid=(groups,),
            in_specs=[whole(h1.shape), whole(vectors.shape)] + specs,
            out_specs=[
                pl.BlockSpec((2, seqs, rows, 3 * LANES), lambda g, o: (g, 0, 0, 0)),
                whole(TOKEN.shape),
            ],
            scratch_shapes=[pltpu.VMEM((3, features, width), BF16)],
        ),
        out_shape=[jax.ShapeDtypeStruct((pairs, seqs, rows, 3 * LANES), BF16), TOKEN],
        compiler_params=params(),
        cost_estimate=cost(6 * tokens * features * features, 6 * features * features),
        name="project",
    )(offsets, h1, vectors, *operands)


def to_places(table, ctx_size, half, source, target):
    for device in range(ctx_size):
        pair = table[device]
        early = pl.multiple_of(pair * half, half)
        later = pl.multiple_of((2 * ctx_size - 1 - pair) * half, half)
        target[pl.ds(early, half), :] = source[device, 0, 0:half, :]
        target[pl.ds(later, half), :] = source[device, 0, half : 2 * half, :]


def both_heads(block):
    first = lax.broadcasted_iota(jnp.int32, block.shape, 0) < LANES // 2
    zero = jnp.zeros_like(block)
    return jnp.concatenate([jnp.where(first, block, zero), jnp.where(first, zero, block)], axis=1)


def stacked_heads(block):
    first = lax.broadcasted_iota(jnp.int32, block.shape, 1) < LANES // 2
    zero = jnp.zeros_like(block)
    return jnp.concatenate([jnp.where(first, block, zero), jnp.where(first, zero, block)], axis=0)


def flipped(block):
    return block.astype(F32).T.astype(BF16)


def band_mask(low, high, start_row, size):
    count = high - low
    key = lax.broadcasted_iota(jnp.int32, (count, 2 * size), 0) + low
    query = lax.broadcasted_iota(jnp.int32, (count, 2 * size), 1) % size + (high - size)
    return (key >= start_row) & (key <= query)


def attend_kernel(
    ctx_size, table, seq_ref, qkv_ref, start_ref, out_ref, lse_ref, held, query_t, value_t, mixed
):
    length = held.shape[0]
    half = length // (2 * ctx_size)
    size = LANES
    blocks = length // size
    reach = blocks // 2
    to_places(table, ctx_size, half, qkv_ref, held)
    for block in range(blocks):
        span = slice(block * size, (block + 1) * size)
        query_t[:, span] = (held[span, 0:LANES].astype(F32) * 0.125).T.astype(BF16)
        value_t[:, span] = flipped(held[span, 2 * LANES :])
    for block in range(blocks):
        low = max(0, block - reach) * size
        high = (block + 1) * size
        span = slice(block * size, high)
        scores = dot(held[low:high, LANES : 2 * LANES], both_heads(query_t[:, span]))
        start_row = start_ref[0, :, span]
        start_row = jnp.concatenate([start_row, start_row], axis=1)
        scores = jnp.where(band_mask(low, high, start_row, size), scores, MASKED)
        top = jnp.max(scores, axis=0, keepdims=True)
        weights = jnp.exp(scores - top)
        total = jnp.sum(weights, axis=0, keepdims=True)
        lse = top + jnp.log(total)
        probs = (weights * (1.0 / total)).astype(BF16)
        lse_ref[0, 0:1, span] = lse[:, :size]
        lse_ref[0, 1:2, span] = lse[:, size:]
        mixed_t = dot(value_t[:, low:high], probs)
        both = jnp.concatenate(
            [mixed_t[0 : LANES // 2, :size], mixed_t[LANES // 2 :, size:]], axis=0
        )
        mixed[span, :] = both.T.astype(BF16)
    for device in range(ctx_size):
        pair = table[device]
        early = pl.multiple_of(pair * half, half)
        later = pl.multiple_of((2 * ctx_size - 1 - pair) * half, half)
        out_ref[device, 0, 0:half, :] = mixed[pl.ds(early, half), :]
        out_ref[device, 0, half : 2 * half, :] = mixed[pl.ds(later, half), :]


def attend(table, unit_seqs, qkv, starts):
    ctx_size, units, rows, width = qkv.shape
    length = ctx_size * rows
    return pl.pallas_call(
        functools.partial(attend_kernel, ctx_size),
        grid_spec=pltpu.PrefetchScalarGridSpec(
            num_scalar_prefetch=2,
            grid=(units,),
            in_specs=[
                pl.BlockSpec((ctx_size, 1, rows, width), lambda u, t, s: (0, u, 0, 0)),
                pl.BlockSpec((1, 1, length), lambda u, t, s: (s[u], 0, 0)),
            ],
            out_specs=[
                pl.BlockSpec((ctx_size, 1, rows, LANES), lambda u, t, s: (0, u, 0, 0)),
                pl.BlockSpec((1, 2, length), lambda u, t, s: (u, 0, 0)),
            ],
            scratch_shapes=[
                pltpu.VMEM((length, width), BF16),
                pltpu.VMEM((LANES, length), BF16),
                pltpu.VMEM((LANES, length), BF16),
                pltpu.VMEM((length, LANES), BF16),
            ],
        ),
        out_shape=[
            jax.ShapeDtypeStruct((ctx_size, units, rows, LANES), BF16),
            jax.ShapeDtypeStruct((units, 2, length), F32),
        ],
        compiler_params=params(),
        cost_estimate=cost(units * length * length * 256, qkv.size * 4),
        name="attend",
    )(table, unit_seqs, qkv, starts)


def attend_back_kernel(
    ctx_size,
    table,
    seq_ref,
    qkv_ref,
    grad_ref,
    start_ref,
    lse_ref,
    out_ref,
    token_ref,
    held,
    grad,
    query_t,
    key_t,
    grad_t,
    query_grad,
    key_grad,
    value_grad,
):
    token_ref[...] = jnp.zeros_like(token_ref)
    length = held.shape[0]
    half = length // (2 * ctx_size)
    size = LANES
    blocks = length // size
    reach = blocks // 2
    to_places(table, ctx_size, half, qkv_ref, held)
    to_places(table, ctx_size, half, grad_ref, grad)
    for block in range(blocks):
        span = slice(block * size, (block + 1) * size)
        scaled = (held[span, 0:LANES].astype(F32) * 0.125).astype(BF16)
        held[span, 0:LANES] = scaled
        query_t[:, span] = flipped(scaled)
        key_t[:, span] = flipped(held[span, LANES : 2 * LANES])
        grad_t[:, span] = flipped(grad[span, :])
    for block in range(blocks):
        low = max(0, block - reach) * size
        high = (block + 1) * size
        span = slice(block * size, high)
        scores = dot(held[low:high, LANES : 2 * LANES], both_heads(query_t[:, span]))
        start_row = start_ref[0, :, span]
        start_row = jnp.concatenate([start_row, start_row], axis=1)
        scores = jnp.where(band_mask(low, high, start_row, size), scores, MASKED)
        lse = jnp.concatenate([lse_ref[0, 0:1, span], lse_ref[0, 1:2, span]], axis=1)
        probs = jnp.exp(scores - lse)
        prob_grad = dot(held[low:high, 2 * LANES :], both_heads(grad_t[:, span]))
        delta = jnp.sum(probs * prob_grad, axis=0, keepdims=True)
        score_grad = (probs * (prob_grad - delta)).astype(BF16)
        probs = probs.astype(BF16)
        new_value = dot(probs, stacked_heads(grad[span, :]))
        new_key = dot(score_grad, stacked_heads(held[span, 0:LANES]))
        if low < high - size:
            value_grad[low : high - size, :] += new_value[: high - size - low]
            key_grad[low : high - size, :] += new_key[: high - size - low]
        value_grad[span, :] = new_value[high - size - low :]
        key_grad[span, :] = new_key[high - size - low :]
        query_t_grad = dot(key_t[:, low:high], score_grad)
        both = jnp.concatenate(
            [query_t_grad[0 : LANES // 2, :size], query_t_grad[LANES // 2 :, size:]], axis=0
        )
        query_grad[span, :] = (both.T * 0.125).astype(BF16)
    for device in range(ctx_size):
        pair = table[device]
        early = pl.multiple_of(pair * half, half)
        later = pl.multiple_of((2 * ctx_size - 1 - pair) * half, half)
        for place, source in ((0, early), (half, later)):
            rows = pl.ds(source, half)
            out_ref[device, 0, place : place + half, 0:LANES] = query_grad[rows, :]
            out_ref[device, 0, place : place + half, LANES : 2 * LANES] = key_grad[
                rows, :
            ].astype(BF16)
            out_ref[device, 0, place : place + half, 2 * LANES :] = value_grad[rows, :].astype(
                BF16
            )


def attend_back(table, unit_seqs, qkv, grad, starts, lse):
    ctx_size, units, rows, width = qkv.shape
    length = ctx_size * rows
    return pl.pallas_call(
        functools.partial(attend_back_kernel, ctx_size),
        grid_spec=pltpu.PrefetchScalarGridSpec(
            num_scalar_prefetch=2,
            grid=(units,),
            in_specs=[
                pl.BlockSpec((ctx_size, 1, rows, width), lambda u, t, s: (0, u, 0, 0)),
                pl.BlockSpec((ctx_size, 1, rows, LANES), lambda u, t, s: (0, u, 0, 0)),
                pl.BlockSpec((1, 1, length), lambda u, t, s: (s[u], 0, 0)),
                pl.BlockSpec((1, 2, length), lambda u, t, s: (u, 0, 0)),
            ],
            out_specs=[
                pl.BlockSpec((ctx_size, 1, rows, width), lambda u, t, s: (0, u, 0, 0)),
                whole(TOKEN.shape),
            ],
            scratch_shapes=[
                pltpu.VMEM((length, width), BF16),
                pltpu.VMEM((length, LANES), BF16),
                pltpu.VMEM((LANES, length), BF16),
                pltpu.VMEM((LANES, length), BF16),
                pltpu.VMEM((LANES, length), BF16),
                pltpu.VMEM((length, LANES), BF16),
                pltpu.VMEM((length, LANES), F32),
                pltpu.VMEM((length, LANES), F32),
            ],
        ),
        out_shape=[jax.ShapeDtypeStruct(qkv.shape, BF16), TOKEN],
        compiler_params=params(),
        cost_estimate=cost(units * length * length * 640, qkv.size * 6),
        name="attend_back",
    )(table, unit_seqs, qkv, grad, starts, lse)


def branch_kernel(off_ref, att_ref, x_ref, v_ref, *refs):
    residual_ref, h2_ref, mixed_ref, weight = refs[-4:]
    pairs = att_ref.shape[0]
    tokens = x_ref.shape[0]
    for pair in range(pairs):
        mixed_ref[:, pair * LANES : (pair + 1) * LANES] = att_ref[pair].reshape(tokens, LANES)
    place_columns(weight, off_ref, refs[:-4])
    residual = (
        x_ref[...].astype(F32) + dot(mixed_ref[...], weight[...]) + v_ref[V_BO : V_BO + 1, :]
    )
    residual_ref[...] = residual
    hat, _ = norm_stats(residual)
    h2_ref[...] = (hat * v_ref[V_G2 : V_G2 + 1, :] + v_ref[V_B2 : V_B2 + 1, :]).astype(BF16)


def branch(att, x, vectors, parts):
    arrays, offsets = parts
    tokens, features = x.shape
    return pl.pallas_call(
        branch_kernel,
        grid_spec=pltpu.PrefetchScalarGridSpec(
            num_scalar_prefetch=1,
            grid=(1,),
            in_specs=[whole(att.shape), whole(x.shape), whole(vectors.shape)]
            + [whole(array.shape) for array in arrays],
            out_specs=[whole(x.shape)] * 3,
            scratch_shapes=[pltpu.VMEM((features, features), BF16)],
        ),
        out_shape=[
            jax.ShapeDtypeStruct(x.shape, F32),
            jax.ShapeDtypeStruct(x.shape, BF16),
            jax.ShapeDtypeStruct(x.shape, BF16),
        ],
        compiler_params=params(),
        cost_estimate=cost(2 * tokens * features * features, 2 * features * features),
        name="branch",
    )(offsets, att, x, vectors, *arrays)


def ffn_kernel(
    expand_count,
    shrink_count,
    steps,
    sc_ref,
    residual_ref,
    h2_ref,
    h2_other_ref,
    og_ref,
    og_other_ref,
    v_ref,
    eb_ref,
    *refs,
):
    expand_parts = refs[:expand_count]
    shrink_parts = refs[expand_count : expand_count + shrink_count]
    (
        dh2_send,
        dh2_keep,
        out_send,
        out_keep,
        send_s,
        keep_s,
        send_e,
        keep_e,
        eb_grad_ref,
        sb_grad_ref,
        expand,
        shrink,
        total,
        back,
        h2,
        h2_t,
        og,
    ) = refs[expand_count + shrink_count :]
    step = pl.program_id(0)
    y_index = sc_ref[0]
    low_label = sc_ref[2]
    expand_offsets = [sc_ref[4 + i] for i in range(expand_count)]
    shrink_offsets = [sc_ref[4 + expand_count + i] for i in range(shrink_count)]
    tokens = h2_ref.shape[0]

    @pl.when(step == 0)
    def _():
        total[:tokens] = residual_ref[...] + v_ref[V_BS : V_BS + 1, :]
        total[tokens:] = jnp.zeros_like(residual_ref)
        back[...] = jnp.zeros_like(back)
        h2[:tokens] = h2_ref[...]
        h2[tokens:] = h2_other_ref[...]
        og[:tokens] = og_ref[...]
        og[tokens:] = og_other_ref[...]
        h2_t[...] = h2[...].astype(F32).T.astype(BF16)
        sb_grad_ref[...] = jnp.sum(og_ref[...].astype(F32), axis=0, keepdims=True)

    place_rows(expand, expand_offsets, expand_parts)
    place_columns(shrink, shrink_offsets, shrink_parts)
    pre = dot(h2[...], expand[...]) + eb_ref[...]
    root = math.sqrt(2.0 / math.pi)
    square = pre * pre
    curve = jnp.tanh(root * (pre + 0.044715 * (square * pre)))
    slope = 0.5 * (1.0 + curve)
    active = (pre * slope).astype(BF16)
    slope = slope + (0.5 * root) * pre * (1.0 - curve * curve) * (1.0 + 0.134145 * square)
    total[...] += dot(active, shrink[...])
    dpre = (dot_nt(og[...], shrink[...]) * slope).astype(BF16)
    eb_grad_ref[...] = jnp.sum(dpre.astype(F32), axis=0, keepdims=True)
    back[...] += dot_nt(dpre, expand[...])
    shrink_grad = dot_tn(active, og[...]).astype(BF16)
    expand_grad = dot(h2_t[...], dpre).astype(BF16)

    fsdp_half, _, subs, rows, columns = send_s.shape
    for part in range(2 * fsdp_half):
        there = slice(part * columns, (part + 1) * columns)
        place = part ^ y_index

        def store(target_s, target_e, there=there, place=place):
            for sub in range(subs):
                here = slice(sub * rows, (sub + 1) * rows)
                index = (place & (fsdp_half - 1), 0, sub ^ low_label)
                target_s[index] = shrink_grad[here, there]
                target_e[index] = expand_grad[there, here]

        pl.when(place < fsdp_half)(functools.partial(store, keep_s, keep_e))
        pl.when(place >= fsdp_half)(functools.partial(store, send_s, send_e))

    @pl.when(step == steps - 1)
    def _():
        dh2_keep[...] = back[:tokens]
        out_keep[...] = total[:tokens]
        dh2_send[...] = back[tokens:]
        out_send[...] = total[tokens:]


def feed_scalars(place, hidden, width, expand_offsets, shrink_offsets):
    (_, ctx_size), y_index, c_index = place
    subs = width * ctx_size // hidden
    label = c_index >> 1
    first = [y_index, label >> bits_of(subs), label & (subs - 1), c_index & 1]
    return jnp.concatenate([jnp.stack(first), expand_offsets, shrink_offsets])


def feed_forward(
    scalars, residual, h2, h2_other, og, og_other, vectors, expand_bias, expand, shrink, sizes
):
    fsdp_size, ctx_size = sizes
    expand_arrays = expand[0]
    shrink_arrays = shrink[0]
    tokens, features = h2.shape
    hidden = expand_bias.shape[1]
    rows = hidden // ctx_size
    columns = features // fsdp_size
    width = WIDTH
    subs = width // rows
    steps = hidden // (2 * width)
    def chunk(array, dim):
        if array.shape[dim] == hidden:
            return lambda s, sc: sc[3] * steps + (s ^ sc[1])
        return lambda s, sc: s ^ sc[1]

    def columns_of(array):
        index = chunk(array, 1)
        return pl.BlockSpec((array.shape[0], width), lambda s, sc: (0, index(s, sc)))

    def rows_of(array):
        index = chunk(array, 0)
        return pl.BlockSpec((width, array.shape[1]), lambda s, sc: (index(s, sc), 0))

    grad_s = (fsdp_size // 2, steps, subs, rows, columns)
    grad_e = (fsdp_size // 2, steps, subs, columns, rows)

    def block(shape):
        return pl.BlockSpec((shape[0], 1) + shape[2:], lambda s, sc: (0, s, 0, 0, 0))

    full = whole(h2.shape)
    wide = jax.ShapeDtypeStruct(h2.shape, F32)
    return pl.pallas_call(
        functools.partial(ffn_kernel, len(expand_arrays), len(shrink_arrays), steps),
        grid_spec=pltpu.PrefetchScalarGridSpec(
            num_scalar_prefetch=1,
            grid=(steps,),
            in_specs=[full] * 5
            + [whole(vectors.shape), columns_of(expand_bias)]
            + [columns_of(array) for array in expand_arrays]
            + [rows_of(array) for array in shrink_arrays],
            out_specs=[full] * 4
            + [block(grad_s)] * 2
            + [block(grad_e)] * 2
            + [pl.BlockSpec((1, width), lambda s, sc: (0, s ^ sc[1])), whole((1, features))],
            scratch_shapes=[
                pltpu.VMEM((features, width), BF16),
                pltpu.VMEM((width, features), BF16),
                pltpu.VMEM((2 * tokens, features), F32),
                pltpu.VMEM((2 * tokens, features), F32),
                pltpu.VMEM((2 * tokens, features), BF16),
                pltpu.VMEM((features, 2 * tokens), BF16),
                pltpu.VMEM((2 * tokens, features), BF16),
            ],
        ),
        out_shape=[wide] * 4
        + [jax.ShapeDtypeStruct(grad_s, BF16)] * 2
        + [jax.ShapeDtypeStruct(grad_e, BF16)] * 2
        + [
            jax.ShapeDtypeStruct((1, hidden // 2), F32),
            jax.ShapeDtypeStruct((1, features), F32),
        ],
        compiler_params=params(),
        cost_estimate=cost(0, 0),
        name="feed_forward",
    )(
        scalars,
        residual,
        h2,
        h2_other,
        og,
        og_other,
        vectors,
        expand_bias,
        *expand_arrays,
        *shrink_arrays,
    )


def branch_back_kernel(
    part_count, seqs, rows, sc_ref, dh2_ref, dh2_other_ref, residual_ref, og_ref, mixed_ref, v_ref, *refs
):
    parts = refs[:part_count]
    dres_ref, dmixed_ref, keep_ref, send_ref, vec_ref, weight, rounded = refs[part_count:]
    place_columns(weight, sc_ref, parts)
    hat, rate = norm_stats(residual_ref[...])
    dh2 = dh2_ref[...] + dh2_other_ref[...]
    scaled = dh2 * v_ref[V_G2 : V_G2 + 1, :]
    first = jnp.mean(scaled, axis=-1, keepdims=True)
    second = jnp.mean(scaled * hat, axis=-1, keepdims=True)
    dres = og_ref[...].astype(F32) + rate * (scaled - first - hat * second)
    dres_ref[...] = dres
    rounded[...] = dres.astype(BF16)
    vec_ref[0:1, :] = jnp.sum(dh2 * hat, axis=0, keepdims=True)
    vec_ref[1:2, :] = jnp.sum(dh2, axis=0, keepdims=True)
    vec_ref[2:3, :] = jnp.sum(rounded[...].astype(F32), axis=0, keepdims=True)
    vec_ref[3:, :] = jnp.zeros((vec_ref.shape[0] - 3, vec_ref.shape[1]), F32)
    dmixed = dot_nt(rounded[...], weight[...]).astype(BF16)
    for pair in range(dmixed_ref.shape[0]):
        dmixed_ref[pair] = dmixed[:, pair * LANES : (pair + 1) * LANES].reshape(seqs, rows, LANES)
    fsdp_size, count, size, columns = keep_ref.shape
    grad = dot_tn(mixed_ref[...], rounded[...]).astype(BF16)
    y_index = sc_ref[part_count]
    label = sc_ref[part_count + 1]
    for number in range(2 * count):
        place = number ^ label

        def store(target, number=number, place=place):
            for part in range(fsdp_size):
                target[part ^ y_index, place >> 1] = grad[
                    number * size : (number + 1) * size, part * columns : (part + 1) * columns
                ]

        pl.when((place & 1) == 0)(functools.partial(store, keep_ref))
        pl.when((place & 1) == 1)(functools.partial(store, send_ref))


def branch_back(scalars, dh2, dh2_other, residual, og, mixed, vectors, parts, sizes, seqs, rows):
    fsdp_size, ctx_size = sizes
    arrays, offsets = parts
    tokens, features = residual.shape
    pairs = features // LANES
    grad = (fsdp_size, ctx_size // 2, features // ctx_size, features // fsdp_size)
    full = whole(residual.shape)
    return pl.pallas_call(
        functools.partial(branch_back_kernel, len(arrays), seqs, rows),
        grid_spec=pltpu.PrefetchScalarGridSpec(
            num_scalar_prefetch=1,
            grid=(1,),
            in_specs=[full] * 5 + [whole(vectors.shape)]
            + [whole(array.shape) for array in arrays],
            out_specs=[
                full,
                whole((pairs, seqs, rows, LANES)),
                whole(grad),
                whole(grad),
                whole((8, features)),
            ],
            scratch_shapes=[
                pltpu.VMEM((features, features), BF16),
                pltpu.VMEM((tokens, features), BF16),
            ],
        ),
        out_shape=[
            jax.ShapeDtypeStruct(residual.shape, F32),
            jax.ShapeDtypeStruct((pairs, seqs, rows, LANES), BF16),
            jax.ShapeDtypeStruct(grad, BF16),
            jax.ShapeDtypeStruct(grad, BF16),
            jax.ShapeDtypeStruct((8, features), F32),
        ],
        compiler_params=params(),
        cost_estimate=cost(4 * tokens * features * features, 8 * features * features),
        name="branch_back",
    )(scalars, dh2, dh2_other, residual, og, mixed, vectors, *arrays)


def input_terms_kernel(sc_ref, h_ref, d_ref, keep_ref, send_ref, token_ref):
    token_ref[...] = jnp.zeros_like(token_ref)
    left = h_ref[...].reshape(-1, h_ref.shape[-1])
    right = d_ref[...].reshape(-1, d_ref.shape[-1])
    value = dot_tn(left, right).astype(BF16)
    half, fsdp_size, rows, _ = keep_ref.shape
    per = value.shape[0] // rows
    for number in range(per):
        place = pl.program_id(0) * per + number
        part = (place // (2 * half)) ^ sc_ref[1]
        own = (place & (2 * half - 1)) ^ sc_ref[2]

        def store(target, number=number, part=part, own=own):
            target[own & (half - 1), part] = value[number * rows : (number + 1) * rows]

        pl.when(own < half)(functools.partial(store, keep_ref))
        pl.when(own >= half)(functools.partial(store, send_ref))


def input_weight_terms(gathered, dqkv, scalars, low, fsdp_size):
    ctx_size, units, rows, width = dqkv.shape
    features = gathered.shape[-1]
    block = 2 * LANES
    out = (low // 2, fsdp_size, features // (low * fsdp_size), width)
    return pl.pallas_call(
        input_terms_kernel,
        grid_spec=pltpu.PrefetchScalarGridSpec(
            num_scalar_prefetch=1,
            grid=(features // block,),
            in_specs=[
                pl.BlockSpec((ctx_size, units, rows, block), lambda g, s: (0, s[0], 0, g)),
                whole(dqkv.shape),
            ],
            out_specs=[whole(out), whole(out), whole(TOKEN.shape)],
        ),
        out_shape=[jax.ShapeDtypeStruct(out, BF16)] * 2 + [TOKEN],
        compiler_params=params(),
        cost_estimate=cost(0, 0),
        name="input_weight_terms",
    )(scalars, gathered, dqkv)


def entry_back_kernel(
    part_count,
    groups,
    off_ref,
    d_ref,
    x_ref,
    dres_ref,
    one_ref,
    two_ref,
    second_ref,
    sb_ref,
    eb_ref,
    v_ref,
    *refs,
):
    parts = refs[: 3 * part_count]
    out_ref, layer_ref, vec_ref, weight, back = refs[3 * part_count :]
    group = pl.program_id(0)
    tokens = x_ref.shape[0]
    width = weight.shape[-1]

    @pl.when(group == 0)
    def _():
        back[...] = jnp.zeros_like(back)
        layer_ref[...] = (one_ref[...] + two_ref[...]).astype(BF16)
        vec_ref[4:7, :] = second_ref[0:3, :]
        vec_ref[7:8, :] = sb_ref[...]
        count = vec_ref.shape[0] - 8
        core = off_ref[off_ref.shape[0] - 1]
        for row in range(count):
            here = eb_ref[:, (row % (count // 2)) * LANES * 8 : (row % (count // 2) + 1) * LANES * 8]
            mine = core == row // (count // 2)
            vec_ref[8 + row : 9 + row, :] = jnp.where(mine, here, jnp.zeros_like(here))

    for kind in range(3):
        place_rows(
            weight.at[kind], off_ref, parts[kind * part_count : (kind + 1) * part_count]
        )
        lanes = slice(kind * LANES, (kind + 1) * LANES)
        value = jnp.concatenate(
            [d_ref[pair, :, :, lanes].reshape(tokens, LANES) for pair in range(d_ref.shape[0])],
            axis=1,
        )
        back[...] += dot_nt(value, weight[kind])
        if kind != 1:
            row = 2 if kind == 0 else 3
            start = pl.multiple_of(group * width, LANES)
            vec_ref[row : row + 1, pl.ds(start, width)] = jnp.sum(
                value.astype(F32), axis=0, keepdims=True
            )

    @pl.when(group == groups - 1)
    def _():
        hat, rate = norm_stats(x_ref[...].astype(F32))
        dh1 = back[...]
        scaled = dh1 * v_ref[V_G1 : V_G1 + 1, :]
        first = jnp.mean(scaled, axis=-1, keepdims=True)
        second = jnp.mean(scaled * hat, axis=-1, keepdims=True)
        out_ref[...] = dres_ref[...] + rate * (scaled - first - hat * second)
        vec_ref[0:1, :] = jnp.sum(dh1 * hat, axis=0, keepdims=True)
        vec_ref[1:2, :] = jnp.sum(dh1, axis=0, keepdims=True)


def entry_back(dqkv, x, dres, one, two, sums, vectors, parts):
    arrays, offsets = parts
    tokens, features = x.shape
    pairs, seqs, rows, _ = dqkv.shape
    width = 2 * LANES
    vec = (8 + 2 * sums[2].shape[1] // features, features)
    groups = features // width
    specs = []
    operands = []
    for kind in range(3):
        for array in arrays:
            specs.append(
                pl.BlockSpec((array.shape[0], width), lambda g, o, k=kind: (0, k * groups + g))
            )
            operands.append(array)
    return pl.pallas_call(
        functools.partial(entry_back_kernel, len(arrays), groups),
        grid_spec=pltpu.PrefetchScalarGridSpec(
            num_scalar_prefetch=1,
            grid=(groups,),
            in_specs=[
                pl.BlockSpec((2, seqs, rows, 3 * LANES), lambda g, o: (g, 0, 0, 0)),
                whole(x.shape),
                whole(x.shape),
                whole(x.shape),
                whole(x.shape),
            ]
            + [whole(array.shape) for array in sums]
            + [whole(vectors.shape)]
            + specs,
            out_specs=[whole(x.shape), whole(x.shape), whole(vec)],
            scratch_shapes=[
                pltpu.VMEM((3, features, width), BF16),
                pltpu.VMEM((tokens, features), F32),
            ],
        ),
        out_shape=[
            jax.ShapeDtypeStruct(x.shape, F32),
            jax.ShapeDtypeStruct(x.shape, BF16),
            jax.ShapeDtypeStruct(vec, F32),
        ],
        compiler_params=params(),
        cost_estimate=cost(6 * tokens * features * features, 6 * features * features),
        name="entry_back",
    )(offsets, dqkv, x, dres, one, two, *sums, vectors, *operands)


def combine_kernel(one_ref, two_ref, send_ref, keep_ref):
    total = (one_ref[...].astype(F32) + two_ref[...].astype(F32)).astype(BF16)
    keep_ref[...] = total[:, 0]
    send_ref[...] = total[:, 1]


def last_kernel(one_ref, two_ref, out_ref):
    out_ref[...] = (one_ref[...].astype(F32) + two_ref[...].astype(F32)).astype(BF16)


def combine(one, two, outer):
    rows, columns = one.shape[-2:]
    shape = (outer, 2, one.size // (2 * outer * rows * columns), rows, columns)
    inner = shape[2]
    per = inner
    while per * rows * columns > 256 * 1024 and per % 2 == 0:
        per //= 2
    half = (outer, inner, rows, columns)
    block = pl.BlockSpec((1, 2, per, rows, columns), lambda a, b: (a, 0, b, 0, 0))
    out = pl.BlockSpec((1, per, rows, columns), lambda a, b: (a, b, 0, 0))
    return pl.pallas_call(
        combine_kernel,
        grid=(outer, inner // per),
        in_specs=[block, block],
        out_specs=[out, out],
        out_shape=[jax.ShapeDtypeStruct(half, BF16)] * 2,
        compiler_params=params(),
        cost_estimate=cost(0, 0),
        name="combine",
    )(one.reshape(shape), two.reshape(shape))


def add_last(one, two):
    rows, columns = one.shape[-2:]
    return pl.pallas_call(
        last_kernel,
        out_shape=jax.ShapeDtypeStruct((1, rows, columns), BF16),
        compiler_params=params(),
        cost_estimate=cost(0, 0),
        name="add_last",
    )(one.reshape(1, rows, columns), two.reshape(1, rows, columns))


def merge_kernel(one_ref, two_ref, out_ref):
    out_ref[:, 0] = one_ref[...]
    out_ref[:, 1] = two_ref[...]


def merge(one, two):
    count, rows, columns = one.shape
    block = pl.BlockSpec((1, rows, columns), lambda n: (n, 0, 0))
    return pl.pallas_call(
        merge_kernel,
        grid=(count,),
        in_specs=[block, block],
        out_specs=pl.BlockSpec((1, 2, rows, columns), lambda n: (n, 0, 0, 0)),
        out_shape=jax.ShapeDtypeStruct((count, 2, rows, columns), BF16),
        compiler_params=params(),
        cost_estimate=cost(0, 0),
        name="merge",
    )(one, two).reshape(2 * count, rows, columns)


def tiles(rows, width, columns):
    count = columns // LANES
    height = rows // count
    return height, [
        (across * height, down * LANES, down * height, across * LANES)
        for down in range(width // LANES)
        for across in range(count)
    ]


def pack_kernel(one_ref, two_ref, extra_ref, out_ref):
    rows, columns = one_ref.shape[1:]
    first = out_ref.shape[1] - rows
    out_ref[:, first:] = (one_ref[...].astype(F32) + two_ref[...].astype(F32)).astype(BF16)
    height, moves = tiles(*extra_ref.shape, columns)
    for row, column, to_row, to_column in moves:
        out_ref[0, to_row : to_row + height, to_column : to_column + LANES] = extra_ref[
            row : row + height, column : column + LANES
        ]


def pack(one, two, extra):
    rows, columns = one.shape[-2:]
    return pl.pallas_call(
        pack_kernel,
        out_shape=jax.ShapeDtypeStruct((1, rows + extra.size // columns, columns), BF16),
        compiler_params=params(),
        cost_estimate=cost(0, 0),
        name="pack",
    )(one.reshape(1, rows, columns), two.reshape(1, rows, columns), extra)


def join_kernel(one_ref, two_ref, extra_one_ref, extra_two_ref, send_ref, keep_ref):
    rows, columns = one_ref.shape[-2:]
    height, moves = tiles(*extra_one_ref.shape[-2:], columns)
    first = keep_ref.shape[1] - rows
    for half, target in ((0, keep_ref), (1, send_ref)):
        value = one_ref[0, half].astype(F32) + two_ref[0, half].astype(F32)
        target[0, first:] = value.astype(BF16)
        value = extra_one_ref[0, half].astype(F32) + extra_two_ref[0, half].astype(F32)
        value = value.astype(BF16)
        for row, column, to_row, to_column in moves:
            target[0, to_row : to_row + height, to_column : to_column + LANES] = value[
                row : row + height, column : column + LANES
            ]


def join(one, two, extra_one, extra_two, outer):
    rows, columns = one.shape[-2:]
    extra_rows, extra_columns = extra_one.shape[-2:]
    height = rows + extra_rows * extra_columns // columns
    block = pl.BlockSpec((1, 2, rows, columns), lambda n: (n, 0, 0, 0))
    extra = pl.BlockSpec((1, 2, extra_rows, extra_columns), lambda n: (n, 0, 0, 0))
    out = pl.BlockSpec((1, height, columns), lambda n: (n, 0, 0))
    shape = (outer, 2, rows, columns)
    extra_shape = (outer, 2, extra_rows, extra_columns)
    return pl.pallas_call(
        join_kernel,
        grid=(outer,),
        in_specs=[block, block, extra, extra],
        out_specs=[out, out],
        out_shape=[jax.ShapeDtypeStruct((outer, height, columns), BF16)] * 2,
        compiler_params=params(),
        cost_estimate=cost(0, 0),
        name="join",
    )(
        one.reshape(shape),
        two.reshape(shape),
        extra_one.reshape(extra_shape),
        extra_two.reshape(extra_shape),
    )


class Flow:
    def __init__(self, send, keep, first, labels, order, sizes):
        self.sizes = dict(fsdp=sizes[0], ctx=sizes[1])
        self.labels = list(labels)
        self.order = list(order)
        self.keep = keep
        self.spreading = None
        self.extra = None
        self.received = self.swap(send, first)

    def swap(self, value, label):
        return swap_bit(value, label[0], self.sizes[label[0]], label[1])

    def step(self, event):
        received = after(self.received, event)
        if self.order:
            label = self.order.pop(0)
            place = self.labels.index(label)
            self.labels.pop(place)
            send, self.keep = combine(self.keep, received, 1 << place)
            self.received = self.swap(send, label)
        elif self.spreading is None:
            if self.extra is None:
                self.keep = add_last(self.keep, received)
            else:
                self.keep = pack(self.keep, received, self.extra)
            self.received = None
        else:
            if self.spreading:
                self.keep = merge(self.keep, received)
                self.received = self.swap(self.keep, self.spreading.pop(0))
            else:
                self.far = received
                self.received = None
        return self

    def join(self, other, event):
        received = after(self.received, event)
        label = self.order.pop(0)
        assert self.labels[-1] == label
        self.labels.pop()
        send, self.keep = join(
            self.keep, received, other.keep, other.received, 1 << len(self.labels)
        )
        self.received = self.swap(send, label)
        other.received = None
        return self

    def spread(self, bits):
        self.spreading = [("ctx", bit) for bit in bits]
        self.received = self.swap(self.keep, self.spreading.pop(0))


def places(bits):
    count = len(bits) - 1
    return [
        sum(((number >> (count - 1 - turn)) & 1) << (bits[turn] - 1) for turn in range(count))
        for number in range(1 << count)
    ]


def finish_kernel(dim, order, label_ref, source, *refs):
    out_ref, token_ref = refs[-2:]
    token_ref[...] = jnp.zeros_like(token_ref)
    count, height, _ = source.shape
    rows, columns = out_ref.shape
    if dim == 0:
        rows = rows // count
    else:
        columns = columns // count
    first = height - rows
    low = label_ref[1] & (count - 1)
    for number in range(count):
        place = order[number] ^ low
        value = source[number, first:].astype(F32)
        if dim == 0:
            out_ref[pl.ds(pl.multiple_of(place * rows, LANES), rows), :] = value
        else:
            out_ref[:, pl.ds(pl.multiple_of(place * columns, LANES), columns)] = value


def finish(source, before, other, table, dim, rows, columns, bits, events=()):
    half, height, width = source.shape
    order = places(bits)
    group = half // 2 if bits[0] == max(bits) else half
    count = half // group
    shift = bits_of(group)

    def index(n, t):
        return (other ^ t[0]) * count + (n ^ (t[1] >> shift))

    if dim == 0:
        shape = (2 * half * rows, columns)
        out_spec = pl.BlockSpec((group * rows, columns), lambda n, t: (index(n, t), 0))
    else:
        shape = (rows, 2 * half * columns)
        out_spec = pl.BlockSpec((rows, group * columns), lambda n, t: (0, index(n, t)))
    earlier = [] if before is None else [before]
    return pl.pallas_call(
        functools.partial(finish_kernel, dim, order[:group]),
        grid_spec=pltpu.PrefetchScalarGridSpec(
            num_scalar_prefetch=1,
            grid=(count,),
            in_specs=[pl.BlockSpec((group, height, width), lambda n, t: (n, 0, 0))]
            + [pl.BlockSpec(memory_space=pl.ANY) for _ in earlier]
            + [whole(event.shape) for event in events],
            out_specs=[out_spec, whole(TOKEN.shape)],
        ),
        out_shape=[jax.ShapeDtypeStruct(shape, F32), TOKEN],
        input_output_aliases={2: 0} if earlier else {},
        compiler_params=params(),
        cost_estimate=cost(0, 0),
        name="finish",
    )(table, source, *earlier, *events)


def finish_rows_kernel(rows, width, low_bits, order, label_ref, near_ref, far_ref, *refs):
    out_ref, token_ref = refs[-2:]
    token_ref[...] = jnp.zeros_like(token_ref)
    half, _, columns = near_ref.shape
    height, moves = tiles(rows, width, columns)
    for number in range(2 * half):
        source = far_ref if number & 1 else near_ref
        owner = ((order[number >> 1] << 1) | (number & 1)) ^ ((label_ref[1] << 1) | label_ref[0])
        if low_bits is None:
            place, begin, stride = owner, 0, LANES
        else:
            place = owner & ((1 << low_bits) - 1)
            begin = (owner >> low_bits) * LANES
            stride = out_ref.shape[1] // (width // LANES)
        for row, column, from_row, from_column in moves:
            down = pl.ds(pl.multiple_of(place * rows + row, 32), height)
            across = begin + (column // LANES) * stride
            if low_bits is not None:
                across = pl.multiple_of(across, LANES)
            out_ref[down, pl.ds(across, LANES)] = source[
                number >> 1, from_row : from_row + height, from_column : from_column + LANES
            ].astype(F32)


def finish_rows(near, far, table, rows, width, low_bits, shape, bits, events=()):
    half, _, columns = near.shape
    block = pl.BlockSpec((half, rows * width // columns, columns), lambda n, t: (0, 0, 0))
    return pl.pallas_call(
        functools.partial(finish_rows_kernel, rows, width, low_bits, places(bits)),
        grid_spec=pltpu.PrefetchScalarGridSpec(
            num_scalar_prefetch=1,
            grid=(1,),
            in_specs=[block, block] + [whole(event.keep.shape) for event in events],
            out_specs=[whole(shape), whole(TOKEN.shape)],
        ),
        out_shape=[jax.ShapeDtypeStruct(shape, F32), TOKEN],
        compiler_params=params(),
        cost_estimate=cost(0, 0),
        name="finish_rows",
    )(table, near, far, *[event.keep for event in events])


def finish_extra_kernel(rows, low_bits, order, label_ref, near_ref, far_ref, *refs):
    out_ref, token_ref = refs[-2:]
    token_ref[...] = jnp.zeros_like(token_ref)
    half, height, columns = near_ref.shape
    for number in range(2 * half):
        source = far_ref if number & 1 else near_ref
        owner = ((order[number >> 1] << 1) | (number & 1)) ^ ((label_ref[1] << 1) | label_ref[0])
        if low_bits is None:
            place, begin = owner, 0
        else:
            place = owner & ((1 << low_bits) - 1)
            begin = pl.multiple_of((owner >> low_bits) * LANES, LANES)
        for across in range(columns // LANES):
            down = pl.multiple_of(place * rows + across * height, 32)
            out_ref[pl.ds(down, height), pl.ds(begin, LANES)] = source[
                number >> 1, :, across * LANES : (across + 1) * LANES
            ].astype(F32)


def finish_extra(near, far, table, rows, width, low_bits, shape, bits, events=()):
    half, _, columns = near.shape
    steps = width // LANES
    block = pl.BlockSpec((half, rows * LANES // columns, columns), lambda n, t: (0, n, 0))
    return pl.pallas_call(
        functools.partial(finish_extra_kernel, rows, low_bits, places(bits)),
        grid_spec=pltpu.PrefetchScalarGridSpec(
            num_scalar_prefetch=1,
            grid=(steps,),
            in_specs=[block, block] + [whole(event.keep.shape) for event in events],
            out_specs=[
                pl.BlockSpec((shape[0], shape[1] // steps), lambda n, t: (0, n)),
                whole(TOKEN.shape),
            ],
        ),
        out_shape=[jax.ShapeDtypeStruct(shape, F32), TOKEN],
        compiler_params=params(),
        cost_estimate=cost(0, 0),
        name="finish_extra",
    )(table, near, far, *[event.keep for event in events])


class Total:
    def __init__(self, value, labels, sizes):
        self.keep = value
        self.sizes = dict(fsdp=sizes[0], ctx=sizes[1])
        self.labels = list(labels)
        self.start()

    def start(self):
        self.received = None
        if self.labels:
            name, bit = self.labels.pop(0)
            self.received = swap_bit(self.keep, name, self.sizes[name], bit)

    def step(self, event):
        received = after(self.received, event)
        self.keep = pl.pallas_call(
            total_kernel,
            out_shape=jax.ShapeDtypeStruct(self.keep.shape, F32),
            compiler_params=params(),
            cost_estimate=cost(0, 0),
            name="total",
        )(self.keep, received)
        self.start()
        return self


def total_kernel(one_ref, two_ref, out_ref):
    out_ref[...] = one_ref[...] + two_ref[...]


def body(
    sizes,
    layer_input,
    output_grad,
    segments,
    assignment,
    first_gain,
    first_bias,
    input_weight,
    query_bias,
    value_bias,
    output_weight,
    output_bias,
    second_gain,
    second_bias,
    expand_weight,
    expand_bias,
    shrink_weight,
    shrink_bias,
):
    fsdp_size, ctx_size = sizes
    seqs, rows, features = layer_input.shape
    tokens = seqs * rows
    hidden = expand_weight.shape[1]
    pairs = features // LANES
    units = seqs * pairs // ctx_size
    y_index = lax.axis_index("fsdp").astype(jnp.int32)
    c_index = lax.axis_index("ctx").astype(jnp.int32)
    part = features // fsdp_size
    small = jnp.concatenate(
        [
            first_gain,
            first_bias,
            query_bias,
            value_bias,
            output_bias,
            second_gain,
            second_bias,
            shrink_bias,
            expand_bias,
        ]
    )
    small = small.reshape(1, -1)
    x = layer_input.reshape(tokens, features)
    og = output_grad.reshape(tokens, features)
    place = (sizes, y_index, c_index)
    core = c_index & 1
    starts = jnp.sum(
        (segments[:, None, :] < segments[:, :, None]).astype(jnp.int32), axis=-1
    )[:, None, :]
    unit_seqs = (c_index * units + jnp.arange(units, dtype=jnp.int32)) & (seqs - 1)
    input_gather = Gather(input_weight, 0, place, (1, 0))
    output_gather = Gather(output_weight, 1, place, (0,))
    expand_gather = Gather(expand_weight, 0, place, (1,), core)
    shrink_gather = Gather(shrink_weight, 1, place, (), core)

    group = ((c_index * units) & (seqs - 1)) >> bits_of(units)
    low_bits = bits_of(ctx_size // pairs)
    low = 1 << low_bits
    if fsdp_size == 2:
        owners = jnp.stack([y_index, 1 - y_index])
    else:
        owners = jnp.arange(fsdp_size, dtype=jnp.int32)

    small, expand_gather.first = lax.optimization_barrier((small, expand_gather.first))
    input_gather.fetch()
    if fsdp_size == 2:
        shards = [small, swap_bit(small, "fsdp", 2, 0)]
    else:
        full = lax.all_gather(small, "fsdp", axis=0)
        shards = [full[number] for number in range(fsdp_size)]
    ready = (
        x,
        shards[-1],
        starts,
        [gather.first for gather in (output_gather, shrink_gather)],
        [
            unit_seqs,
            owners,
            input_gather.offsets,
            output_gather.offsets,
            feed_scalars(place, hidden, WIDTH, expand_gather.offsets, shrink_gather.offsets),
            jnp.stack([core, c_index >> 1]),
            jnp.concatenate([output_gather.offsets, jnp.stack([y_index, c_index])]),
            jnp.concatenate([input_gather.offsets, core[None]]),
            jnp.stack([group, y_index, c_index & (low - 1)]),
        ],
    )
    x, shards[-1], starts, firsts, tables = lax.optimization_barrier(ready)
    for gather, first in zip((output_gather, shrink_gather), firsts):
        gather.first = first
    unit_seqs, owners, input_gather.offsets, output_gather.offsets, *tables = tables
    feed_table, finish_table, back_table, entry_table, terms_table = tables

    small_done = Event(shards[-1])
    input_gather.keep = after(input_gather.keep, small_done)
    shards[-1] = small_done.keep
    h1, vectors, expand_vector = first_norm(x, shards, owners, hidden)
    other = Event(swap_bit(og, "ctx", ctx_size, 0))
    expand_gather.fetch(input_gather)
    input_gather.exchange()
    norm_done = Event(h1)
    input_gather.keep = after(input_gather.keep, norm_done)
    h1 = norm_done.keep
    input_gather.exchange()
    expand_first = Event(after(expand_gather.keep, input_gather))
    expand_gather.exchange()
    output_gather.fetch(expand_first)
    h1 = after(h1, expand_first)
    qkv, token = project(h1, vectors, input_gather.result(), seqs, rows)
    expand_gather.held[0] = expand_first.keep
    project_done = Event(token)
    shrink_gather.fetch(output_gather)
    output_gather.exchange()
    output_gather.keep = after(output_gather.keep, project_done)
    qkv = qkv.reshape(ctx_size, units, rows, 3 * LANES)
    qkv = lax.all_to_all(qkv, "ctx", 0, 0, tiled=True)
    qkv = after(after(qkv, output_gather), other)
    og_other = other.keep
    att, lse = attend(assignment, unit_seqs, qkv, starts)
    attend_done = Event(lse)
    shrink_gather.keep = after(shrink_gather.keep, attend_done)
    att = lax.all_to_all(att, "ctx", 0, 0, tiled=True)
    received = Event(after(after(att, expand_gather), shrink_gather))
    gathered = lax.all_gather(
        after(h1, received).reshape(seqs, rows, features), "ctx", axis=0
    )
    att = received.keep.reshape(pairs, seqs, rows, LANES)
    output_parts = output_gather.result()
    residual, h2, mixed = branch(att, x, vectors, output_parts)
    h2_other = swap_bit(h2, "ctx", ctx_size, 0)
    dh2_send, dh2_keep, out_send, out_keep, send_s, keep_s, send_e, keep_e, eb_grad, sb_grad = feed_forward(
        feed_table,
        residual,
        h2,
        h2_other,
        og,
        og_other,
        vectors,
        expand_vector,
        expand_gather.result(),
        shrink_gather.result(),
        sizes,
    )
    dh2_other = swap_bit(dh2_send, "ctx", ctx_size, 0)
    out_other = swap_bit(out_send, "ctx", ctx_size, 0)

    every = [("fsdp", bit) for bit in reversed(range(bits_of(fsdp_size)))]
    high = [("ctx", bit) for bit in reversed(range(1, bits_of(ctx_size)))]
    flow_s = Flow(send_s, keep_s, every[0], every[1:] + high, every[1:] + high[::-1], sizes)
    dres, dmixed, keep_o, send_o, vec_two = branch_back(
        back_table, dh2_keep, dh2_other, residual, og, mixed, vectors, output_parts, sizes, seqs, rows
    )
    branch_done = Event(vec_two)
    send_e = after(send_e, branch_done)
    flow_e = Flow(send_e, keep_e, every[0], every[1:] + high, every[1:] + high[::-1], sizes)
    spread_s = [bit for _, bit in high] + [0]
    spread_e = spread_s
    flow_o = Flow(send_o, keep_o, ("ctx", 0), every + high, every + high[::-1], sizes)
    dmixed = dmixed.reshape(ctx_size, units, rows, LANES)
    dmixed = lax.all_to_all(dmixed, "ctx", 0, 0, tiled=True)
    dqkv, token = attend_back(
        assignment, unit_seqs, qkv, dmixed, starts, attend_done.keep
    )
    back_done = Event(token)
    last = flow_s.step(back_done)
    out_done = Event(out_other)
    held = Event(after(after(dqkv, last), out_done))
    out_other = out_done.keep
    keep_i, send_i, token = input_weight_terms(gathered, held.keep, terms_table, low, fsdp_size)
    terms_done = Event(token)
    low_labels = [("ctx", bit) for bit in reversed(range(low_bits))]
    flow_i = Flow(
        send_i,
        keep_i,
        low_labels[0],
        low_labels[1:] + every,
        low_labels[1:] + every,
        sizes,
    )
    last = flow_i.step(terms_done)
    last = flow_o.step(last)
    last = flow_s.step(last)
    while len(flow_e.order) >= len(high):
        last = flow_e.step(last)
    dqkv = lax.all_to_all(dqkv, "ctx", 0, 0, tiled=True).reshape(pairs, seqs, rows, 3 * LANES)
    last = flow_o.step(last)
    while flow_i.received is not None:
        last = flow_i.step(last)
    last = flow_s.step(last)
    while len(flow_o.order) > len(flow_e.order):
        last = flow_o.step(last)
    flow_o.received = after(flow_o.received, last)
    last = flow_e.join(flow_o, last)
    flow_s.extra = flow_i.keep[0]
    while flow_s.order:
        last = flow_s.step(last)
    last = flow_s.step(last)
    flow_s.spread(spread_s)
    input_grad, out, sums = entry_back(
        after(dqkv, last),
        x,
        dres,
        out_keep,
        out_other,
        [branch_done.keep, sb_grad, eb_grad],
        vectors,
        (input_gather.result()[0], entry_table),
    )
    totals = Total(sums, every + high[::-1] + [("ctx", 0)], sizes)
    last = totals
    while flow_e.order:
        last = flow_e.step(last)
    last = flow_s.step(last)
    for _ in range(len(every) + 2):
        last = totals.step(last)
    last = flow_e.step(last)
    flow_e.spread(spread_e)
    last = flow_s.step(last)
    last = flow_e.step(last)
    while totals.received is not None:
        last = totals.step(last)
    while len(flow_e.spreading) > 1:
        last = flow_e.step(last)
    while flow_s.spreading:
        last = flow_s.step(last)
    rows_s = hidden // ctx_size
    sums = totals.keep
    own_sums = lax.dynamic_slice_in_dim(sums[:8], y_index * part, part, 1)
    hidden_part = hidden // fsdp_size
    own_hidden = lax.dynamic_slice_in_dim(
        sums[8:].reshape(1, hidden), y_index * hidden_part, hidden_part, 1
    )
    shrink_grad, token = finish(
        flow_s.keep,
        None,
        0,
        finish_table,
        0,
        rows_s,
        part,
        spread_s,
        [own_sums, own_hidden],
    )
    flow_s.received = after(flow_s.received, Event(token))
    last = flow_s.step(last)
    shrink_grad, token = finish(
        flow_s.far, shrink_grad, 1, finish_table, 0, rows_s, part, spread_s
    )
    shrink_done = Event(token)
    input_grad_w, token = finish_extra(
        flow_s.keep,
        flow_s.far,
        finish_table,
        part >> low_bits,
        3 * LANES,
        low_bits,
        (part, 3 * features),
        spread_s,
    )
    input_done = Event(token)
    flow_e.received = after(flow_e.received, shrink_done)
    flow_e.received = after(flow_e.received, input_done)
    while flow_e.spreading:
        last = flow_e.step(last)
    expand_grad, token = finish(
        flow_e.keep, None, 0, finish_table, 1, part, rows_s, spread_e
    )
    flow_e.received = after(flow_e.received, Event(token))
    last = flow_e.step(last)
    expand_grad, token = finish(
        flow_e.far, expand_grad, 1, finish_table, 1, part, rows_s, spread_e
    )
    expand_done = Event(token)
    output_grad_w, _ = finish_rows(
        flow_e.keep,
        flow_e.far,
        finish_table,
        features // ctx_size,
        part,
        None,
        (features, part),
        spread_e,
        [project_done, back_done, terms_done, branch_done, shrink_done, input_done, expand_done],
    )
    return (
        out.reshape(seqs, rows, features),
        input_grad.reshape(seqs, rows, features),
        own_sums[0],
        own_sums[1],
        input_grad_w,
        own_sums[2],
        own_sums[3],
        output_grad_w,
        own_sums[6],
        own_sums[4],
        own_sums[5],
        expand_grad,
        own_hidden[0],
        shrink_grad,
        own_sums[7],
    )


def solution(mesh):
    sizes = (mesh.shape["fsdp"], mesh.shape["ctx"])
    return jax.shard_map(
        functools.partial(body, sizes),
        mesh=mesh,
        in_specs=(
            P("fsdp", "ctx", None),
            P("fsdp", "ctx", None),
            P("fsdp", None),
            P(),
            P("fsdp"),
            P("fsdp"),
            P("fsdp", None),
            P("fsdp"),
            P("fsdp"),
            P(None, "fsdp"),
            P("fsdp"),
            P("fsdp"),
            P("fsdp"),
            P("fsdp", None),
            P("fsdp"),
            P(None, "fsdp"),
            P("fsdp"),
        ),
        out_specs=(
            P("fsdp", "ctx", None),
            P("fsdp", "ctx", None),
            P("fsdp"),
            P("fsdp"),
            P("fsdp", None),
            P("fsdp"),
            P("fsdp"),
            P(None, "fsdp"),
            P("fsdp"),
            P("fsdp"),
            P("fsdp"),
            P("fsdp", None),
            P("fsdp"),
            P(None, "fsdp"),
            P("fsdp"),
        ),
        check_vma=False,
    )
```

```python
import functools
import math

import jax
import jax.numpy as jnp
from jax import lax
from jax.experimental import pallas as pl
from jax.experimental.pallas import tpu as pltpu
from jax.sharding import PartitionSpec as P

HEADS = 16
EPSILON = 1e-05
MASKED = -1000000000.0
LANES = 128
WIDTH = 512
MIB = 1024 * 1024
F32 = jnp.float32
BF16 = jnp.bfloat16
TOKEN = jax.ShapeDtypeStruct((8, LANES), F32)

V_G1, V_B1, V_BQ, V_BV, V_BO, V_G2, V_B2, V_BS = range(8)


def bits_of(number):
    return number.bit_length() - 1


def dot(left, right):
    return jnp.dot(left, right, preferred_element_type=F32)


def dot_nt(left, right):
    return lax.dot_general(left, right, (((1,), (1,)), ((), ())), preferred_element_type=F32)


def dot_tn(left, right):
    return lax.dot_general(left, right, (((0,), (0,)), ((), ())), preferred_element_type=F32)


def swap_bit(value, axis, size, bit):
    return lax.ppermute(value, axis, [(i, i ^ (1 << bit)) for i in range(size)])


class Event:
    def __init__(self, keep):
        self.keep = keep


def after(value, event):
    value, event.keep = lax.optimization_barrier((value, event.keep))
    return value


def params(limit_mib=48):
    return pltpu.CompilerParams(vmem_limit_bytes=limit_mib * MIB)


def whole(shape):
    rank = len(shape)
    return pl.BlockSpec(tuple(shape), lambda *_: (0,) * rank)


def cost(flops, moved):
    return pl.CostEstimate(flops=0, bytes_accessed=0, transcendentals=0)


class Gather:
    def __init__(self, weight, dim, place, bits, core=None):
        (fsdp_size, self.ctx_size), y_index, c_index = place
        extent = weight.shape[dim]
        self.bits = bits
        self.stage = 0
        self.two = fsdp_size == 2
        if not self.two:
            self.bits = ()
            self.parts = []
            self.first = lax.all_gather(weight, "fsdp", axis=dim, tiled=True)
            self.offsets = jnp.zeros((1,), jnp.int32)
            self.held = [self.first]
            return
        size = extent >> len(bits)
        mine = jnp.int32(0)
        for number, bit in enumerate(bits):
            mine = mine | (((c_index >> bit) & 1) << number)
        if core is None:
            self.first = lax.dynamic_slice_in_dim(weight, mine * size, size, dim)
        else:
            half = weight.shape[1 - dim] // 2
            begins = (mine * size, core * half) if dim == 0 else (core * half, mine * size)
            self.first = lax.dynamic_slice(
                weight, begins, (size, half) if dim == 0 else (half, size)
            )
        order = y_index * extent + jnp.zeros((1,), jnp.int32)
        numbers = mine ^ jnp.arange(1 << len(bits), dtype=jnp.int32)
        self.offsets = jnp.concatenate([order, (1 - y_index) * extent + numbers * size])
        self.parts = [weight]

    def fetch(self, event=None):
        if not self.two:
            return
        first = self.first if event is None else after(self.first, event)
        self.held = [swap_bit(first, "fsdp", 2, 0)]

    @property
    def keep(self):
        return self.held[-1]

    @keep.setter
    def keep(self, value):
        self.held[-1] = value

    def exchange(self, event=None):
        if self.stage == len(self.bits):
            return
        bit = self.bits[self.stage]
        if event is not None:
            self.keep = after(self.keep, event)
        self.held = self.held + [swap_bit(array, "ctx", self.ctx_size, bit) for array in self.held]
        self.stage += 1

    def result(self):
        return self.parts + self.held, self.offsets


def place_rows(target, offsets, part_refs):
    for number, ref in enumerate(part_refs):
        rows = ref.shape[0]
        target[pl.ds(pl.multiple_of(offsets[number], 32), rows), :] = ref[...]


def place_columns(target, offsets, part_refs):
    for number, ref in enumerate(part_refs):
        columns = ref.shape[1]
        target[:, pl.ds(pl.multiple_of(offsets[number], LANES), columns)] = ref[...]


def norm_stats(values):
    center = values - jnp.mean(values, axis=-1, keepdims=True)
    spread = jnp.mean(center * center, axis=-1, keepdims=True)
    rate = lax.rsqrt(spread + EPSILON)
    return center * rate, rate


def norm_kernel(sc_ref, x_ref, *refs):
    shards = refs[:-3]
    h_ref, v_ref, e_ref = refs[-3:]
    part = v_ref.shape[1] // len(shards)
    hidden = e_ref.shape[1] // len(shards)
    for number, ref in enumerate(shards):
        where = sc_ref[number]
        for row in range(8):
            v_ref[row : row + 1, pl.ds(pl.multiple_of(where * part, LANES), part)] = ref[
                :, row * part : (row + 1) * part
            ].astype(F32)
        e_ref[:, pl.ds(pl.multiple_of(where * hidden, LANES), hidden)] = ref[:, 8 * part :].astype(
            F32
        )
    hat, _ = norm_stats(x_ref[...].astype(F32))
    h_ref[...] = (hat * v_ref[V_G1 : V_G1 + 1, :] + v_ref[V_B1 : V_B1 + 1, :]).astype(BF16)


def first_norm(x, shards, owners, hidden):
    shapes = [
        jax.ShapeDtypeStruct(x.shape, BF16),
        jax.ShapeDtypeStruct((8, x.shape[1]), F32),
        jax.ShapeDtypeStruct((1, hidden), F32),
    ]
    return pl.pallas_call(
        norm_kernel,
        grid_spec=pltpu.PrefetchScalarGridSpec(
            num_scalar_prefetch=1,
            grid=(1,),
            in_specs=[whole(x.shape)] + [whole(shard.shape) for shard in shards],
            out_specs=[whole(shape.shape) for shape in shapes],
        ),
        out_shape=shapes,
        compiler_params=params(),
        cost_estimate=cost(0, 0),
        name="first_norm",
    )(owners, x, *shards)


def qkv_kernel(part_count, seqs, rows, off_ref, h_ref, v_ref, *refs):
    parts = refs[: 3 * part_count]
    out_ref, token_ref, weight = refs[3 * part_count :]
    token_ref[...] = jnp.zeros_like(token_ref)
    group = pl.program_id(0)
    width = weight.shape[-1]
    per = width // LANES
    for kind in range(3):
        place_rows(
            weight.at[kind], off_ref, parts[kind * part_count : (kind + 1) * part_count]
        )
        value = dot(h_ref[...], weight[kind])
        if kind != 1:
            row = V_BQ if kind == 0 else V_BV
            start = pl.multiple_of(group * width, LANES)
            value = value + v_ref[row : row + 1, pl.ds(start, width)]
        value = value.astype(BF16)
        for pair in range(per):
            out_ref[pair, :, :, kind * LANES : (kind + 1) * LANES] = value[
                :, pair * LANES : (pair + 1) * LANES
            ].reshape(seqs, rows, LANES)


def project(h1, vectors, parts, seqs, rows):
    arrays, offsets = parts
    tokens, features = h1.shape
    width = 2 * LANES
    groups = features // width
    pairs = features // LANES
    specs = []
    operands = []
    for kind in range(3):
        for array in arrays:
            specs.append(
                pl.BlockSpec((array.shape[0], width), lambda g, o, k=kind: (0, k * groups + g))
            )
            operands.append(array)
    return pl.pallas_call(
        functools.partial(qkv_kernel, len(arrays), seqs, rows),
        grid_spec=pltpu.PrefetchScalarGridSpec(
            num_scalar_prefetch=1,
            grid=(groups,),
            in_specs=[whole(h1.shape), whole(vectors.shape)] + specs,
            out_specs=[
                pl.BlockSpec((2, seqs, rows, 3 * LANES), lambda g, o: (g, 0, 0, 0)),
                whole(TOKEN.shape),
            ],
            scratch_shapes=[pltpu.VMEM((3, features, width), BF16)],
        ),
        out_shape=[jax.ShapeDtypeStruct((pairs, seqs, rows, 3 * LANES), BF16), TOKEN],
        compiler_params=params(),
        cost_estimate=cost(6 * tokens * features * features, 6 * features * features),
        name="project",
    )(offsets, h1, vectors, *operands)


def to_places(table, ctx_size, half, source, target):
    for device in range(ctx_size):
        pair = table[device]
        early = pl.multiple_of(pair * half, half)
        later = pl.multiple_of((2 * ctx_size - 1 - pair) * half, half)
        target[pl.ds(early, half), :] = source[device, 0, 0:half, :]
        target[pl.ds(later, half), :] = source[device, 0, half : 2 * half, :]


def both_heads(block):
    first = lax.broadcasted_iota(jnp.int32, block.shape, 0) < LANES // 2
    zero = jnp.zeros_like(block)
    return jnp.concatenate([jnp.where(first, block, zero), jnp.where(first, zero, block)], axis=1)


def stacked_heads(block):
    first = lax.broadcasted_iota(jnp.int32, block.shape, 1) < LANES // 2
    zero = jnp.zeros_like(block)
    return jnp.concatenate([jnp.where(first, block, zero), jnp.where(first, zero, block)], axis=0)


def flipped(block):
    return block.astype(F32).T.astype(BF16)


def band_mask(low, high, start_row, size):
    count = high - low
    key = lax.broadcasted_iota(jnp.int32, (count, 2 * size), 0) + low
    query = lax.broadcasted_iota(jnp.int32, (count, 2 * size), 1) % size + (high - size)
    return (key >= start_row) & (key <= query)


def attend_kernel(
    ctx_size, table, seq_ref, qkv_ref, start_ref, out_ref, lse_ref, held, query_t, value_t, mixed
):
    length = held.shape[0]
    half = length // (2 * ctx_size)
    size = LANES
    blocks = length // size
    reach = blocks // 2
    to_places(table, ctx_size, half, qkv_ref, held)
    for block in range(blocks):
        span = slice(block * size, (block + 1) * size)
        query_t[:, span] = (held[span, 0:LANES].astype(F32) * 0.125).T.astype(BF16)
        value_t[:, span] = flipped(held[span, 2 * LANES :])
    for block in range(blocks):
        low = max(0, block - reach) * size
        high = (block + 1) * size
        span = slice(block * size, high)
        scores = dot(held[low:high, LANES : 2 * LANES], both_heads(query_t[:, span]))
        start_row = start_ref[0, :, span]
        start_row = jnp.concatenate([start_row, start_row], axis=1)
        scores = jnp.where(band_mask(low, high, start_row, size), scores, MASKED)
        top = jnp.max(scores, axis=0, keepdims=True)
        weights = jnp.exp(scores - top)
        total = jnp.sum(weights, axis=0, keepdims=True)
        lse = top + jnp.log(total)
        probs = (weights * (1.0 / total)).astype(BF16)
        lse_ref[0, 0:1, span] = lse[:, :size]
        lse_ref[0, 1:2, span] = lse[:, size:]
        mixed_t = dot(value_t[:, low:high], probs)
        both = jnp.concatenate(
            [mixed_t[0 : LANES // 2, :size], mixed_t[LANES // 2 :, size:]], axis=0
        )
        mixed[span, :] = both.T.astype(BF16)
    for device in range(ctx_size):
        pair = table[device]
        early = pl.multiple_of(pair * half, half)
        later = pl.multiple_of((2 * ctx_size - 1 - pair) * half, half)
        out_ref[device, 0, 0:half, :] = mixed[pl.ds(early, half), :]
        out_ref[device, 0, half : 2 * half, :] = mixed[pl.ds(later, half), :]


def attend(table, unit_seqs, qkv, starts):
    ctx_size, units, rows, width = qkv.shape
    length = ctx_size * rows
    return pl.pallas_call(
        functools.partial(attend_kernel, ctx_size),
        grid_spec=pltpu.PrefetchScalarGridSpec(
            num_scalar_prefetch=2,
            grid=(units,),
            in_specs=[
                pl.BlockSpec((ctx_size, 1, rows, width), lambda u, t, s: (0, u, 0, 0)),
                pl.BlockSpec((1, 1, length), lambda u, t, s: (s[u], 0, 0)),
            ],
            out_specs=[
                pl.BlockSpec((ctx_size, 1, rows, LANES), lambda u, t, s: (0, u, 0, 0)),
                pl.BlockSpec((1, 2, length), lambda u, t, s: (u, 0, 0)),
            ],
            scratch_shapes=[
                pltpu.VMEM((length, width), BF16),
                pltpu.VMEM((LANES, length), BF16),
                pltpu.VMEM((LANES, length), BF16),
                pltpu.VMEM((length, LANES), BF16),
            ],
        ),
        out_shape=[
            jax.ShapeDtypeStruct((ctx_size, units, rows, LANES), BF16),
            jax.ShapeDtypeStruct((units, 2, length), F32),
        ],
        compiler_params=params(),
        cost_estimate=cost(units * length * length * 256, qkv.size * 4),
        name="attend",
    )(table, unit_seqs, qkv, starts)


def attend_back_kernel(
    ctx_size,
    table,
    seq_ref,
    qkv_ref,
    grad_ref,
    start_ref,
    lse_ref,
    out_ref,
    token_ref,
    held,
    grad,
    query_t,
    key_t,
    grad_t,
    query_grad,
    key_grad,
    value_grad,
):
    token_ref[...] = jnp.zeros_like(token_ref)
    length = held.shape[0]
    half = length // (2 * ctx_size)
    size = LANES
    blocks = length // size
    reach = blocks // 2
    to_places(table, ctx_size, half, qkv_ref, held)
    to_places(table, ctx_size, half, grad_ref, grad)
    for block in range(blocks):
        span = slice(block * size, (block + 1) * size)
        scaled = (held[span, 0:LANES].astype(F32) * 0.125).astype(BF16)
        held[span, 0:LANES] = scaled
        query_t[:, span] = flipped(scaled)
        key_t[:, span] = flipped(held[span, LANES : 2 * LANES])
        grad_t[:, span] = flipped(grad[span, :])
    for block in range(blocks):
        low = max(0, block - reach) * size
        high = (block + 1) * size
        span = slice(block * size, high)
        scores = dot(held[low:high, LANES : 2 * LANES], both_heads(query_t[:, span]))
        start_row = start_ref[0, :, span]
        start_row = jnp.concatenate([start_row, start_row], axis=1)
        scores = jnp.where(band_mask(low, high, start_row, size), scores, MASKED)
        lse = jnp.concatenate([lse_ref[0, 0:1, span], lse_ref[0, 1:2, span]], axis=1)
        probs = jnp.exp(scores - lse)
        prob_grad = dot(held[low:high, 2 * LANES :], both_heads(grad_t[:, span]))
        delta = jnp.sum(probs * prob_grad, axis=0, keepdims=True)
        score_grad = (probs * (prob_grad - delta)).astype(BF16)
        probs = probs.astype(BF16)
        new_value = dot(probs, stacked_heads(grad[span, :]))
        new_key = dot(score_grad, stacked_heads(held[span, 0:LANES]))
        if low < high - size:
            value_grad[low : high - size, :] += new_value[: high - size - low]
            key_grad[low : high - size, :] += new_key[: high - size - low]
        value_grad[span, :] = new_value[high - size - low :]
        key_grad[span, :] = new_key[high - size - low :]
        query_t_grad = dot(key_t[:, low:high], score_grad)
        both = jnp.concatenate(
            [query_t_grad[0 : LANES // 2, :size], query_t_grad[LANES // 2 :, size:]], axis=0
        )
        query_grad[span, :] = (both.T * 0.125).astype(BF16)
    for device in range(ctx_size):
        pair = table[device]
        early = pl.multiple_of(pair * half, half)
        later = pl.multiple_of((2 * ctx_size - 1 - pair) * half, half)
        for place, source in ((0, early), (half, later)):
            rows = pl.ds(source, half)
            out_ref[device, 0, place : place + half, 0:LANES] = query_grad[rows, :]
            out_ref[device, 0, place : place + half, LANES : 2 * LANES] = key_grad[
                rows, :
            ].astype(BF16)
            out_ref[device, 0, place : place + half, 2 * LANES :] = value_grad[rows, :].astype(
                BF16
            )


def attend_back(table, unit_seqs, qkv, grad, starts, lse):
    ctx_size, units, rows, width = qkv.shape
    length = ctx_size * rows
    return pl.pallas_call(
        functools.partial(attend_back_kernel, ctx_size),
        grid_spec=pltpu.PrefetchScalarGridSpec(
            num_scalar_prefetch=2,
            grid=(units,),
            in_specs=[
                pl.BlockSpec((ctx_size, 1, rows, width), lambda u, t, s: (0, u, 0, 0)),
                pl.BlockSpec((ctx_size, 1, rows, LANES), lambda u, t, s: (0, u, 0, 0)),
                pl.BlockSpec((1, 1, length), lambda u, t, s: (s[u], 0, 0)),
                pl.BlockSpec((1, 2, length), lambda u, t, s: (u, 0, 0)),
            ],
            out_specs=[
                pl.BlockSpec((ctx_size, 1, rows, width), lambda u, t, s: (0, u, 0, 0)),
                whole(TOKEN.shape),
            ],
            scratch_shapes=[
                pltpu.VMEM((length, width), BF16),
                pltpu.VMEM((length, LANES), BF16),
                pltpu.VMEM((LANES, length), BF16),
                pltpu.VMEM((LANES, length), BF16),
                pltpu.VMEM((LANES, length), BF16),
                pltpu.VMEM((length, LANES), BF16),
                pltpu.VMEM((length, LANES), F32),
                pltpu.VMEM((length, LANES), F32),
            ],
        ),
        out_shape=[jax.ShapeDtypeStruct(qkv.shape, BF16), TOKEN],
        compiler_params=params(),
        cost_estimate=cost(units * length * length * 640, qkv.size * 6),
        name="attend_back",
    )(table, unit_seqs, qkv, grad, starts, lse)


def branch_kernel(off_ref, att_ref, x_ref, v_ref, *refs):
    residual_ref, h2_ref, mixed_ref, weight = refs[-4:]
    pairs = att_ref.shape[0]
    tokens = x_ref.shape[0]
    for pair in range(pairs):
        mixed_ref[:, pair * LANES : (pair + 1) * LANES] = att_ref[pair].reshape(tokens, LANES)
    place_columns(weight, off_ref, refs[:-4])
    residual = (
        x_ref[...].astype(F32) + dot(mixed_ref[...], weight[...]) + v_ref[V_BO : V_BO + 1, :]
    )
    residual_ref[...] = residual
    hat, _ = norm_stats(residual)
    h2_ref[...] = (hat * v_ref[V_G2 : V_G2 + 1, :] + v_ref[V_B2 : V_B2 + 1, :]).astype(BF16)


def branch(att, x, vectors, parts):
    arrays, offsets = parts
    tokens, features = x.shape
    return pl.pallas_call(
        branch_kernel,
        grid_spec=pltpu.PrefetchScalarGridSpec(
            num_scalar_prefetch=1,
            grid=(1,),
            in_specs=[whole(att.shape), whole(x.shape), whole(vectors.shape)]
            + [whole(array.shape) for array in arrays],
            out_specs=[whole(x.shape)] * 3,
            scratch_shapes=[pltpu.VMEM((features, features), BF16)],
        ),
        out_shape=[
            jax.ShapeDtypeStruct(x.shape, F32),
            jax.ShapeDtypeStruct(x.shape, BF16),
            jax.ShapeDtypeStruct(x.shape, BF16),
        ],
        compiler_params=params(),
        cost_estimate=cost(2 * tokens * features * features, 2 * features * features),
        name="branch",
    )(offsets, att, x, vectors, *arrays)


def ffn_kernel(
    expand_count,
    shrink_count,
    steps,
    sc_ref,
    residual_ref,
    h2_ref,
    h2_other_ref,
    og_ref,
    og_other_ref,
    v_ref,
    eb_ref,
    *refs,
):
    expand_parts = refs[:expand_count]
    shrink_parts = refs[expand_count : expand_count + shrink_count]
    (
        dh2_send,
        dh2_keep,
        out_send,
        out_keep,
        send_s,
        keep_s,
        send_e,
        keep_e,
        eb_grad_ref,
        sb_grad_ref,
        expand,
        shrink,
        total,
        back,
        h2,
        h2_t,
        og,
    ) = refs[expand_count + shrink_count :]
    step = pl.program_id(0)
    y_index = sc_ref[0]
    low_label = sc_ref[2]
    expand_offsets = [sc_ref[4 + i] for i in range(expand_count)]
    shrink_offsets = [sc_ref[4 + expand_count + i] for i in range(shrink_count)]
    tokens = h2_ref.shape[0]

    @pl.when(step == 0)
    def _():
        total[:tokens] = residual_ref[...] + v_ref[V_BS : V_BS + 1, :]
        total[tokens:] = jnp.zeros_like(residual_ref)
        back[...] = jnp.zeros_like(back)
        h2[:tokens] = h2_ref[...]
        h2[tokens:] = h2_other_ref[...]
        og[:tokens] = og_ref[...]
        og[tokens:] = og_other_ref[...]
        h2_t[...] = h2[...].astype(F32).T.astype(BF16)
        sb_grad_ref[...] = jnp.sum(og_ref[...].astype(F32), axis=0, keepdims=True)

    place_rows(expand, expand_offsets, expand_parts)
    place_columns(shrink, shrink_offsets, shrink_parts)
    pre = dot(h2[...], expand[...]) + eb_ref[...]
    root = math.sqrt(2.0 / math.pi)
    square = pre * pre
    curve = jnp.tanh(root * (pre + 0.044715 * (square * pre)))
    slope = 0.5 * (1.0 + curve)
    active = (pre * slope).astype(BF16)
    slope = slope + (0.5 * root) * pre * (1.0 - curve * curve) * (1.0 + 0.134145 * square)
    total[...] += dot(active, shrink[...])
    dpre = (dot_nt(og[...], shrink[...]) * slope).astype(BF16)
    eb_grad_ref[...] = jnp.sum(dpre.astype(F32), axis=0, keepdims=True)
    back[...] += dot_nt(dpre, expand[...])
    shrink_grad = dot_tn(active, og[...]).astype(BF16)
    expand_grad = dot(h2_t[...], dpre).astype(BF16)

    fsdp_half, _, subs, rows, columns = send_s.shape
    for part in range(2 * fsdp_half):
        there = slice(part * columns, (part + 1) * columns)
        place = part ^ y_index

        def store(target_s, target_e, there=there, place=place):
            for sub in range(subs):
                here = slice(sub * rows, (sub + 1) * rows)
                index = (place & (fsdp_half - 1), 0, sub ^ low_label)
                target_s[index] = shrink_grad[here, there]
                target_e[index] = expand_grad[there, here]

        pl.when(place < fsdp_half)(functools.partial(store, keep_s, keep_e))
        pl.when(place >= fsdp_half)(functools.partial(store, send_s, send_e))

    @pl.when(step == steps - 1)
    def _():
        dh2_keep[...] = back[:tokens]
        out_keep[...] = total[:tokens]
        dh2_send[...] = back[tokens:]
        out_send[...] = total[tokens:]


def feed_scalars(place, hidden, width, expand_offsets, shrink_offsets):
    (_, ctx_size), y_index, c_index = place
    subs = width * ctx_size // hidden
    label = c_index >> 1
    first = [y_index, label >> bits_of(subs), label & (subs - 1), c_index & 1]
    return jnp.concatenate([jnp.stack(first), expand_offsets, shrink_offsets])


def feed_forward(
    scalars, residual, h2, h2_other, og, og_other, vectors, expand_bias, expand, shrink, sizes
):
    fsdp_size, ctx_size = sizes
    expand_arrays = expand[0]
    shrink_arrays = shrink[0]
    tokens, features = h2.shape
    hidden = expand_bias.shape[1]
    rows = hidden // ctx_size
    columns = features // fsdp_size
    width = WIDTH
    subs = width // rows
    steps = hidden // (2 * width)
    def chunk(array, dim):
        if array.shape[dim] == hidden:
            return lambda s, sc: sc[3] * steps + (s ^ sc[1])
        return lambda s, sc: s ^ sc[1]

    def columns_of(array):
        index = chunk(array, 1)
        return pl.BlockSpec((array.shape[0], width), lambda s, sc: (0, index(s, sc)))

    def rows_of(array):
        index = chunk(array, 0)
        return pl.BlockSpec((width, array.shape[1]), lambda s, sc: (index(s, sc), 0))

    grad_s = (fsdp_size // 2, steps, subs, rows, columns)
    grad_e = (fsdp_size // 2, steps, subs, columns, rows)

    def block(shape):
        return pl.BlockSpec((shape[0], 1) + shape[2:], lambda s, sc: (0, s, 0, 0, 0))

    full = whole(h2.shape)
    wide = jax.ShapeDtypeStruct(h2.shape, F32)
    return pl.pallas_call(
        functools.partial(ffn_kernel, len(expand_arrays), len(shrink_arrays), steps),
        grid_spec=pltpu.PrefetchScalarGridSpec(
            num_scalar_prefetch=1,
            grid=(steps,),
            in_specs=[full] * 5
            + [whole(vectors.shape), columns_of(expand_bias)]
            + [columns_of(array) for array in expand_arrays]
            + [rows_of(array) for array in shrink_arrays],
            out_specs=[full] * 4
            + [block(grad_s)] * 2
            + [block(grad_e)] * 2
            + [pl.BlockSpec((1, width), lambda s, sc: (0, s ^ sc[1])), whole((1, features))],
            scratch_shapes=[
                pltpu.VMEM((features, width), BF16),
                pltpu.VMEM((width, features), BF16),
                pltpu.VMEM((2 * tokens, features), F32),
                pltpu.VMEM((2 * tokens, features), F32),
                pltpu.VMEM((2 * tokens, features), BF16),
                pltpu.VMEM((features, 2 * tokens), BF16),
                pltpu.VMEM((2 * tokens, features), BF16),
            ],
        ),
        out_shape=[wide] * 4
        + [jax.ShapeDtypeStruct(grad_s, BF16)] * 2
        + [jax.ShapeDtypeStruct(grad_e, BF16)] * 2
        + [
            jax.ShapeDtypeStruct((1, hidden // 2), F32),
            jax.ShapeDtypeStruct((1, features), F32),
        ],
        compiler_params=params(),
        cost_estimate=cost(0, 0),
        name="feed_forward",
    )(
        scalars,
        residual,
        h2,
        h2_other,
        og,
        og_other,
        vectors,
        expand_bias,
        *expand_arrays,
        *shrink_arrays,
    )


def branch_back_kernel(
    part_count, seqs, rows, sc_ref, dh2_ref, dh2_other_ref, residual_ref, og_ref, mixed_ref, v_ref, *refs
):
    parts = refs[:part_count]
    dres_ref, dmixed_ref, keep_ref, send_ref, vec_ref, weight, rounded = refs[part_count:]
    place_columns(weight, sc_ref, parts)
    hat, rate = norm_stats(residual_ref[...])
    dh2 = dh2_ref[...] + dh2_other_ref[...]
    scaled = dh2 * v_ref[V_G2 : V_G2 + 1, :]
    first = jnp.mean(scaled, axis=-1, keepdims=True)
    second = jnp.mean(scaled * hat, axis=-1, keepdims=True)
    dres = og_ref[...].astype(F32) + rate * (scaled - first - hat * second)
    dres_ref[...] = dres
    rounded[...] = dres.astype(BF16)
    vec_ref[0:1, :] = jnp.sum(dh2 * hat, axis=0, keepdims=True)
    vec_ref[1:2, :] = jnp.sum(dh2, axis=0, keepdims=True)
    vec_ref[2:3, :] = jnp.sum(rounded[...].astype(F32), axis=0, keepdims=True)
    vec_ref[3:, :] = jnp.zeros((vec_ref.shape[0] - 3, vec_ref.shape[1]), F32)
    dmixed = dot_nt(rounded[...], weight[...]).astype(BF16)
    for pair in range(dmixed_ref.shape[0]):
        dmixed_ref[pair] = dmixed[:, pair * LANES : (pair + 1) * LANES].reshape(seqs, rows, LANES)
    fsdp_size, count, size, columns = keep_ref.shape
    grad = dot_tn(mixed_ref[...], rounded[...]).astype(BF16)
    y_index = sc_ref[part_count]
    label = sc_ref[part_count + 1]
    for number in range(2 * count):
        place = number ^ label

        def store(target, number=number, place=place):
            for part in range(fsdp_size):
                target[part ^ y_index, place >> 1] = grad[
                    number * size : (number + 1) * size, part * columns : (part + 1) * columns
                ]

        pl.when((place & 1) == 0)(functools.partial(store, keep_ref))
        pl.when((place & 1) == 1)(functools.partial(store, send_ref))


def branch_back(scalars, dh2, dh2_other, residual, og, mixed, vectors, parts, sizes, seqs, rows):
    fsdp_size, ctx_size = sizes
    arrays, offsets = parts
    tokens, features = residual.shape
    pairs = features // LANES
    grad = (fsdp_size, ctx_size // 2, features // ctx_size, features // fsdp_size)
    full = whole(residual.shape)
    return pl.pallas_call(
        functools.partial(branch_back_kernel, len(arrays), seqs, rows),
        grid_spec=pltpu.PrefetchScalarGridSpec(
            num_scalar_prefetch=1,
            grid=(1,),
            in_specs=[full] * 5 + [whole(vectors.shape)]
            + [whole(array.shape) for array in arrays],
            out_specs=[
                full,
                whole((pairs, seqs, rows, LANES)),
                whole(grad),
                whole(grad),
                whole((8, features)),
            ],
            scratch_shapes=[
                pltpu.VMEM((features, features), BF16),
                pltpu.VMEM((tokens, features), BF16),
            ],
        ),
        out_shape=[
            jax.ShapeDtypeStruct(residual.shape, F32),
            jax.ShapeDtypeStruct((pairs, seqs, rows, LANES), BF16),
            jax.ShapeDtypeStruct(grad, BF16),
            jax.ShapeDtypeStruct(grad, BF16),
            jax.ShapeDtypeStruct((8, features), F32),
        ],
        compiler_params=params(),
        cost_estimate=cost(4 * tokens * features * features, 8 * features * features),
        name="branch_back",
    )(scalars, dh2, dh2_other, residual, og, mixed, vectors, *arrays)


def input_terms_kernel(sc_ref, h_ref, d_ref, keep_ref, send_ref, token_ref):
    token_ref[...] = jnp.zeros_like(token_ref)
    left = h_ref[...].reshape(-1, h_ref.shape[-1])
    right = d_ref[...].reshape(-1, d_ref.shape[-1])
    value = dot_tn(left, right).astype(BF16)
    half, fsdp_size, rows, _ = keep_ref.shape
    per = value.shape[0] // rows
    for number in range(per):
        place = pl.program_id(0) * per + number
        part = (place // (2 * half)) ^ sc_ref[1]
        own = (place & (2 * half - 1)) ^ sc_ref[2]

        def store(target, number=number, part=part, own=own):
            target[own & (half - 1), part] = value[number * rows : (number + 1) * rows]

        pl.when(own < half)(functools.partial(store, keep_ref))
        pl.when(own >= half)(functools.partial(store, send_ref))


def input_weight_terms(gathered, dqkv, scalars, low, fsdp_size):
    ctx_size, units, rows, width = dqkv.shape
    features = gathered.shape[-1]
    block = 2 * LANES
    out = (low // 2, fsdp_size, features // (low * fsdp_size), width)
    return pl.pallas_call(
        input_terms_kernel,
        grid_spec=pltpu.PrefetchScalarGridSpec(
            num_scalar_prefetch=1,
            grid=(features // block,),
            in_specs=[
                pl.BlockSpec((ctx_size, units, rows, block), lambda g, s: (0, s[0], 0, g)),
                whole(dqkv.shape),
            ],
            out_specs=[whole(out), whole(out), whole(TOKEN.shape)],
        ),
        out_shape=[jax.ShapeDtypeStruct(out, BF16)] * 2 + [TOKEN],
        compiler_params=params(),
        cost_estimate=cost(0, 0),
        name="input_weight_terms",
    )(scalars, gathered, dqkv)


def entry_back_kernel(
    part_count,
    groups,
    off_ref,
    d_ref,
    x_ref,
    dres_ref,
    one_ref,
    two_ref,
    second_ref,
    sb_ref,
    eb_ref,
    v_ref,
    *refs,
):
    parts = refs[: 3 * part_count]
    out_ref, layer_ref, vec_ref, weight, back = refs[3 * part_count :]
    group = pl.program_id(0)
    tokens = x_ref.shape[0]
    width = weight.shape[-1]

    @pl.when(group == 0)
    def _():
        back[...] = jnp.zeros_like(back)
        layer_ref[...] = (one_ref[...] + two_ref[...]).astype(BF16)
        vec_ref[4:7, :] = second_ref[0:3, :]
        vec_ref[7:8, :] = sb_ref[...]
        count = vec_ref.shape[0] - 8
        core = off_ref[off_ref.shape[0] - 1]
        for row in range(count):
            here = eb_ref[:, (row % (count // 2)) * LANES * 8 : (row % (count // 2) + 1) * LANES * 8]
            mine = core == row // (count // 2)
            vec_ref[8 + row : 9 + row, :] = jnp.where(mine, here, jnp.zeros_like(here))

    for kind in range(3):
        place_rows(
            weight.at[kind], off_ref, parts[kind * part_count : (kind + 1) * part_count]
        )
        lanes = slice(kind * LANES, (kind + 1) * LANES)
        value = jnp.concatenate(
            [d_ref[pair, :, :, lanes].reshape(tokens, LANES) for pair in range(d_ref.shape[0])],
            axis=1,
        )
        back[...] += dot_nt(value, weight[kind])
        if kind != 1:
            row = 2 if kind == 0 else 3
            start = pl.multiple_of(group * width, LANES)
            vec_ref[row : row + 1, pl.ds(start, width)] = jnp.sum(
                value.astype(F32), axis=0, keepdims=True
            )

    @pl.when(group == groups - 1)
    def _():
        hat, rate = norm_stats(x_ref[...].astype(F32))
        dh1 = back[...]
        scaled = dh1 * v_ref[V_G1 : V_G1 + 1, :]
        first = jnp.mean(scaled, axis=-1, keepdims=True)
        second = jnp.mean(scaled * hat, axis=-1, keepdims=True)
        out_ref[...] = dres_ref[...] + rate * (scaled - first - hat * second)
        vec_ref[0:1, :] = jnp.sum(dh1 * hat, axis=0, keepdims=True)
        vec_ref[1:2, :] = jnp.sum(dh1, axis=0, keepdims=True)


def entry_back(dqkv, x, dres, one, two, sums, vectors, parts):
    arrays, offsets = parts
    tokens, features = x.shape
    pairs, seqs, rows, _ = dqkv.shape
    width = 2 * LANES
    vec = (8 + 2 * sums[2].shape[1] // features, features)
    groups = features // width
    specs = []
    operands = []
    for kind in range(3):
        for array in arrays:
            specs.append(
                pl.BlockSpec((array.shape[0], width), lambda g, o, k=kind: (0, k * groups + g))
            )
            operands.append(array)
    return pl.pallas_call(
        functools.partial(entry_back_kernel, len(arrays), groups),
        grid_spec=pltpu.PrefetchScalarGridSpec(
            num_scalar_prefetch=1,
            grid=(groups,),
            in_specs=[
                pl.BlockSpec((2, seqs, rows, 3 * LANES), lambda g, o: (g, 0, 0, 0)),
                whole(x.shape),
                whole(x.shape),
                whole(x.shape),
                whole(x.shape),
            ]
            + [whole(array.shape) for array in sums]
            + [whole(vectors.shape)]
            + specs,
            out_specs=[whole(x.shape), whole(x.shape), whole(vec)],
            scratch_shapes=[
                pltpu.VMEM((3, features, width), BF16),
                pltpu.VMEM((tokens, features), F32),
            ],
        ),
        out_shape=[
            jax.ShapeDtypeStruct(x.shape, F32),
            jax.ShapeDtypeStruct(x.shape, BF16),
            jax.ShapeDtypeStruct(vec, F32),
        ],
        compiler_params=params(),
        cost_estimate=cost(6 * tokens * features * features, 6 * features * features),
        name="entry_back",
    )(offsets, dqkv, x, dres, one, two, *sums, vectors, *operands)


def combine_kernel(one_ref, two_ref, send_ref, keep_ref):
    total = (one_ref[...].astype(F32) + two_ref[...].astype(F32)).astype(BF16)
    keep_ref[...] = total[:, 0]
    send_ref[...] = total[:, 1]


def last_kernel(one_ref, two_ref, out_ref):
    out_ref[...] = (one_ref[...].astype(F32) + two_ref[...].astype(F32)).astype(BF16)


def combine(one, two, outer):
    rows, columns = one.shape[-2:]
    shape = (outer, 2, one.size // (2 * outer * rows * columns), rows, columns)
    inner = shape[2]
    per = inner
    while per * rows * columns > 256 * 1024 and per % 2 == 0:
        per //= 2
    half = (outer, inner, rows, columns)
    block = pl.BlockSpec((1, 2, per, rows, columns), lambda a, b: (a, 0, b, 0, 0))
    out = pl.BlockSpec((1, per, rows, columns), lambda a, b: (a, b, 0, 0))
    return pl.pallas_call(
        combine_kernel,
        grid=(outer, inner // per),
        in_specs=[block, block],
        out_specs=[out, out],
        out_shape=[jax.ShapeDtypeStruct(half, BF16)] * 2,
        compiler_params=params(),
        cost_estimate=cost(0, 0),
        name="combine",
    )(one.reshape(shape), two.reshape(shape))


def add_last(one, two):
    rows, columns = one.shape[-2:]
    return pl.pallas_call(
        last_kernel,
        out_shape=jax.ShapeDtypeStruct((1, rows, columns), BF16),
        compiler_params=params(),
        cost_estimate=cost(0, 0),
        name="add_last",
    )(one.reshape(1, rows, columns), two.reshape(1, rows, columns))


def merge_kernel(one_ref, two_ref, out_ref):
    out_ref[:, 0] = one_ref[...]
    out_ref[:, 1] = two_ref[...]


def merge(one, two):
    count, rows, columns = one.shape
    block = pl.BlockSpec((1, rows, columns), lambda n: (n, 0, 0))
    return pl.pallas_call(
        merge_kernel,
        grid=(count,),
        in_specs=[block, block],
        out_specs=pl.BlockSpec((1, 2, rows, columns), lambda n: (n, 0, 0, 0)),
        out_shape=jax.ShapeDtypeStruct((count, 2, rows, columns), BF16),
        compiler_params=params(),
        cost_estimate=cost(0, 0),
        name="merge",
    )(one, two).reshape(2 * count, rows, columns)


def tiles(rows, width, columns):
    count = columns // LANES
    height = rows // count
    return height, [
        (across * height, down * LANES, down * height, across * LANES)
        for down in range(width // LANES)
        for across in range(count)
    ]


def pack_kernel(one_ref, two_ref, extra_ref, out_ref):
    rows, columns = one_ref.shape[1:]
    first = out_ref.shape[1] - rows
    out_ref[:, first:] = (one_ref[...].astype(F32) + two_ref[...].astype(F32)).astype(BF16)
    height, moves = tiles(*extra_ref.shape, columns)
    for row, column, to_row, to_column in moves:
        out_ref[0, to_row : to_row + height, to_column : to_column + LANES] = extra_ref[
            row : row + height, column : column + LANES
        ]


def pack(one, two, extra):
    rows, columns = one.shape[-2:]
    return pl.pallas_call(
        pack_kernel,
        out_shape=jax.ShapeDtypeStruct((1, rows + extra.size // columns, columns), BF16),
        compiler_params=params(),
        cost_estimate=cost(0, 0),
        name="pack",
    )(one.reshape(1, rows, columns), two.reshape(1, rows, columns), extra)


def join_kernel(one_ref, two_ref, extra_one_ref, extra_two_ref, send_ref, keep_ref):
    rows, columns = one_ref.shape[-2:]
    height, moves = tiles(*extra_one_ref.shape[-2:], columns)
    first = keep_ref.shape[1] - rows
    for half, target in ((0, keep_ref), (1, send_ref)):
        value = one_ref[0, half].astype(F32) + two_ref[0, half].astype(F32)
        target[0, first:] = value.astype(BF16)
        value = extra_one_ref[0, half].astype(F32) + extra_two_ref[0, half].astype(F32)
        value = value.astype(BF16)
        for row, column, to_row, to_column in moves:
            target[0, to_row : to_row + height, to_column : to_column + LANES] = value[
                row : row + height, column : column + LANES
            ]


def join(one, two, extra_one, extra_two, outer):
    rows, columns = one.shape[-2:]
    extra_rows, extra_columns = extra_one.shape[-2:]
    height = rows + extra_rows * extra_columns // columns
    block = pl.BlockSpec((1, 2, rows, columns), lambda n: (n, 0, 0, 0))
    extra = pl.BlockSpec((1, 2, extra_rows, extra_columns), lambda n: (n, 0, 0, 0))
    out = pl.BlockSpec((1, height, columns), lambda n: (n, 0, 0))
    shape = (outer, 2, rows, columns)
    extra_shape = (outer, 2, extra_rows, extra_columns)
    return pl.pallas_call(
        join_kernel,
        grid=(outer,),
        in_specs=[block, block, extra, extra],
        out_specs=[out, out],
        out_shape=[jax.ShapeDtypeStruct((outer, height, columns), BF16)] * 2,
        compiler_params=params(),
        cost_estimate=cost(0, 0),
        name="join",
    )(
        one.reshape(shape),
        two.reshape(shape),
        extra_one.reshape(extra_shape),
        extra_two.reshape(extra_shape),
    )


class Flow:
    def __init__(self, send, keep, first, labels, order, sizes):
        self.sizes = dict(fsdp=sizes[0], ctx=sizes[1])
        self.labels = list(labels)
        self.order = list(order)
        self.keep = keep
        self.spreading = None
        self.extra = None
        self.received = self.swap(send, first)

    def swap(self, value, label):
        return swap_bit(value, label[0], self.sizes[label[0]], label[1])

    def step(self, event):
        received = after(self.received, event)
        if self.order:
            label = self.order.pop(0)
            place = self.labels.index(label)
            self.labels.pop(place)
            send, self.keep = combine(self.keep, received, 1 << place)
            self.received = self.swap(send, label)
        elif self.spreading is None:
            if self.extra is None:
                self.keep = add_last(self.keep, received)
            else:
                self.keep = pack(self.keep, received, self.extra)
            self.received = None
        else:
            if self.spreading:
                self.keep = merge(self.keep, received)
                self.received = self.swap(self.keep, self.spreading.pop(0))
            else:
                self.far = received
                self.received = None
        return self

    def join(self, other, event):
        received = after(self.received, event)
        label = self.order.pop(0)
        assert self.labels[-1] == label
        self.labels.pop()
        send, self.keep = join(
            self.keep, received, other.keep, other.received, 1 << len(self.labels)
        )
        self.received = self.swap(send, label)
        other.received = None
        return self

    def spread(self, bits):
        self.spreading = [("ctx", bit) for bit in bits]
        self.received = self.swap(self.keep, self.spreading.pop(0))


def places(bits):
    count = len(bits) - 1
    return [
        sum(((number >> (count - 1 - turn)) & 1) << (bits[turn] - 1) for turn in range(count))
        for number in range(1 << count)
    ]


def finish_kernel(dim, order, label_ref, source, *refs):
    out_ref, token_ref = refs[-2:]
    token_ref[...] = jnp.zeros_like(token_ref)
    count, height, _ = source.shape
    rows, columns = out_ref.shape
    if dim == 0:
        rows = rows // count
    else:
        columns = columns // count
    first = height - rows
    low = label_ref[1] & (count - 1)
    for number in range(count):
        place = order[number] ^ low
        value = source[number, first:].astype(F32)
        if dim == 0:
            out_ref[pl.ds(pl.multiple_of(place * rows, LANES), rows), :] = value
        else:
            out_ref[:, pl.ds(pl.multiple_of(place * columns, LANES), columns)] = value


def finish(source, before, other, table, dim, rows, columns, bits, events=()):
    half, height, width = source.shape
    order = places(bits)
    group = half // 2 if bits[0] == max(bits) else half
    count = half // group
    shift = bits_of(group)

    def index(n, t):
        return (other ^ t[0]) * count + (n ^ (t[1] >> shift))

    if dim == 0:
        shape = (2 * half * rows, columns)
        out_spec = pl.BlockSpec((group * rows, columns), lambda n, t: (index(n, t), 0))
    else:
        shape = (rows, 2 * half * columns)
        out_spec = pl.BlockSpec((rows, group * columns), lambda n, t: (0, index(n, t)))
    earlier = [] if before is None else [before]
    return pl.pallas_call(
        functools.partial(finish_kernel, dim, order[:group]),
        grid_spec=pltpu.PrefetchScalarGridSpec(
            num_scalar_prefetch=1,
            grid=(count,),
            in_specs=[pl.BlockSpec((group, height, width), lambda n, t: (n, 0, 0))]
            + [pl.BlockSpec(memory_space=pl.ANY) for _ in earlier]
            + [whole(event.shape) for event in events],
            out_specs=[out_spec, whole(TOKEN.shape)],
        ),
        out_shape=[jax.ShapeDtypeStruct(shape, F32), TOKEN],
        input_output_aliases={2: 0} if earlier else {},
        compiler_params=params(),
        cost_estimate=cost(0, 0),
        name="finish",
    )(table, source, *earlier, *events)


def finish_rows_kernel(rows, width, low_bits, order, label_ref, near_ref, far_ref, *refs):
    out_ref, token_ref = refs[-2:]
    token_ref[...] = jnp.zeros_like(token_ref)
    half, _, columns = near_ref.shape
    height, moves = tiles(rows, width, columns)
    for number in range(2 * half):
        source = far_ref if number & 1 else near_ref
        owner = ((order[number >> 1] << 1) | (number & 1)) ^ ((label_ref[1] << 1) | label_ref[0])
        if low_bits is None:
            place, begin, stride = owner, 0, LANES
        else:
            place = owner & ((1 << low_bits) - 1)
            begin = (owner >> low_bits) * LANES
            stride = out_ref.shape[1] // (width // LANES)
        for row, column, from_row, from_column in moves:
            down = pl.ds(pl.multiple_of(place * rows + row, 32), height)
            across = begin + (column // LANES) * stride
            if low_bits is not None:
                across = pl.multiple_of(across, LANES)
            out_ref[down, pl.ds(across, LANES)] = source[
                number >> 1, from_row : from_row + height, from_column : from_column + LANES
            ].astype(F32)


def finish_rows(near, far, table, rows, width, low_bits, shape, bits, events=()):
    half, _, columns = near.shape
    block = pl.BlockSpec((half, rows * width // columns, columns), lambda n, t: (0, 0, 0))
    return pl.pallas_call(
        functools.partial(finish_rows_kernel, rows, width, low_bits, places(bits)),
        grid_spec=pltpu.PrefetchScalarGridSpec(
            num_scalar_prefetch=1,
            grid=(1,),
            in_specs=[block, block] + [whole(event.keep.shape) for event in events],
            out_specs=[whole(shape), whole(TOKEN.shape)],
        ),
        out_shape=[jax.ShapeDtypeStruct(shape, F32), TOKEN],
        compiler_params=params(),
        cost_estimate=cost(0, 0),
        name="finish_rows",
    )(table, near, far, *[event.keep for event in events])


def finish_extra_kernel(rows, low_bits, order, label_ref, near_ref, far_ref, *refs):
    out_ref, token_ref = refs[-2:]
    token_ref[...] = jnp.zeros_like(token_ref)
    half, height, columns = near_ref.shape
    for number in range(2 * half):
        source = far_ref if number & 1 else near_ref
        owner = ((order[number >> 1] << 1) | (number & 1)) ^ ((label_ref[1] << 1) | label_ref[0])
        if low_bits is None:
            place, begin = owner, 0
        else:
            place = owner & ((1 << low_bits) - 1)
            begin = pl.multiple_of((owner >> low_bits) * LANES, LANES)
        for across in range(columns // LANES):
            down = pl.multiple_of(place * rows + across * height, 32)
            out_ref[pl.ds(down, height), pl.ds(begin, LANES)] = source[
                number >> 1, :, across * LANES : (across + 1) * LANES
            ].astype(F32)


def finish_extra(near, far, table, rows, width, low_bits, shape, bits, events=()):
    half, _, columns = near.shape
    steps = width // LANES
    block = pl.BlockSpec((half, rows * LANES // columns, columns), lambda n, t: (0, n, 0))
    return pl.pallas_call(
        functools.partial(finish_extra_kernel, rows, low_bits, places(bits)),
        grid_spec=pltpu.PrefetchScalarGridSpec(
            num_scalar_prefetch=1,
            grid=(steps,),
            in_specs=[block, block] + [whole(event.keep.shape) for event in events],
            out_specs=[
                pl.BlockSpec((shape[0], shape[1] // steps), lambda n, t: (0, n)),
                whole(TOKEN.shape),
            ],
        ),
        out_shape=[jax.ShapeDtypeStruct(shape, F32), TOKEN],
        compiler_params=params(),
        cost_estimate=cost(0, 0),
        name="finish_extra",
    )(table, near, far, *[event.keep for event in events])


class Total:
    def __init__(self, value, labels, sizes):
        self.keep = value
        self.sizes = dict(fsdp=sizes[0], ctx=sizes[1])
        self.labels = list(labels)
        self.start()

    def start(self):
        self.received = None
        if self.labels:
            name, bit = self.labels.pop(0)
            self.received = swap_bit(self.keep, name, self.sizes[name], bit)

    def step(self, event):
        received = after(self.received, event)
        self.keep = pl.pallas_call(
            total_kernel,
            out_shape=jax.ShapeDtypeStruct(self.keep.shape, F32),
            compiler_params=params(),
            cost_estimate=cost(0, 0),
            name="total",
        )(self.keep, received)
        self.start()
        return self


def total_kernel(one_ref, two_ref, out_ref):
    out_ref[...] = one_ref[...] + two_ref[...]


def body(
    sizes,
    layer_input,
    output_grad,
    segments,
    assignment,
    first_gain,
    first_bias,
    input_weight,
    query_bias,
    value_bias,
    output_weight,
    output_bias,
    second_gain,
    second_bias,
    expand_weight,
    expand_bias,
    shrink_weight,
    shrink_bias,
):
    fsdp_size, ctx_size = sizes
    seqs, rows, features = layer_input.shape
    tokens = seqs * rows
    hidden = expand_weight.shape[1]
    pairs = features // LANES
    units = seqs * pairs // ctx_size
    y_index = lax.axis_index("fsdp").astype(jnp.int32)
    c_index = lax.axis_index("ctx").astype(jnp.int32)
    part = features // fsdp_size
    small = jnp.concatenate(
        [
            first_gain,
            first_bias,
            query_bias,
            value_bias,
            output_bias,
            second_gain,
            second_bias,
            shrink_bias,
            expand_bias,
        ]
    )
    small = small.reshape(1, -1)
    x = layer_input.reshape(tokens, features)
    og = output_grad.reshape(tokens, features)
    place = (sizes, y_index, c_index)
    core = c_index & 1
    starts = jnp.sum(
        (segments[:, None, :] < segments[:, :, None]).astype(jnp.int32), axis=-1
    )[:, None, :]
    unit_seqs = (c_index * units + jnp.arange(units, dtype=jnp.int32)) & (seqs - 1)
    input_gather = Gather(input_weight, 0, place, (1, 0))
    output_gather = Gather(output_weight, 1, place, (0,))
    expand_gather = Gather(expand_weight, 0, place, (1,), core)
    shrink_gather = Gather(shrink_weight, 1, place, (), core)

    group = ((c_index * units) & (seqs - 1)) >> bits_of(units)
    low_bits = bits_of(ctx_size // pairs)
    low = 1 << low_bits
    if fsdp_size == 2:
        owners = jnp.stack([y_index, 1 - y_index])
    else:
        owners = jnp.arange(fsdp_size, dtype=jnp.int32)

    small, expand_gather.first = lax.optimization_barrier((small, expand_gather.first))
    input_gather.fetch()
    if fsdp_size == 2:
        shards = [small, swap_bit(small, "fsdp", 2, 0)]
    else:
        full = lax.all_gather(small, "fsdp", axis=0)
        shards = [full[number] for number in range(fsdp_size)]
    ready = (
        x,
        shards[-1],
        starts,
        [gather.first for gather in (output_gather, shrink_gather)],
        [
            unit_seqs,
            owners,
            input_gather.offsets,
            output_gather.offsets,
            feed_scalars(place, hidden, WIDTH, expand_gather.offsets, shrink_gather.offsets),
            jnp.stack([core, c_index >> 1]),
            jnp.concatenate([output_gather.offsets, jnp.stack([y_index, c_index])]),
            jnp.concatenate([input_gather.offsets, core[None]]),
            jnp.stack([group, y_index, c_index & (low - 1)]),
        ],
    )
    x, shards[-1], starts, firsts, tables = lax.optimization_barrier(ready)
    for gather, first in zip((output_gather, shrink_gather), firsts):
        gather.first = first
    unit_seqs, owners, input_gather.offsets, output_gather.offsets, *tables = tables
    feed_table, finish_table, back_table, entry_table, terms_table = tables

    small_done = Event(shards[-1])
    input_gather.keep = after(input_gather.keep, small_done)
    shards[-1] = small_done.keep
    h1, vectors, expand_vector = first_norm(x, shards, owners, hidden)
    other = Event(swap_bit(og, "ctx", ctx_size, 0))
    expand_gather.fetch(input_gather)
    input_gather.exchange()
    norm_done = Event(h1)
    input_gather.keep = after(input_gather.keep, norm_done)
    h1 = norm_done.keep
    input_gather.exchange()
    expand_first = Event(after(expand_gather.keep, input_gather))
    expand_gather.exchange()
    output_gather.fetch(expand_first)
    h1 = after(h1, expand_first)
    qkv, token = project(h1, vectors, input_gather.result(), seqs, rows)
    expand_gather.held[0] = expand_first.keep
    project_done = Event(token)
    shrink_gather.fetch(output_gather)
    output_gather.exchange()
    output_gather.keep = after(output_gather.keep, project_done)
    qkv = qkv.reshape(ctx_size, units, rows, 3 * LANES)
    qkv = lax.all_to_all(qkv, "ctx", 0, 0, tiled=True)
    qkv = after(after(qkv, output_gather), other)
    og_other = other.keep
    att, lse = attend(assignment, unit_seqs, qkv, starts)
    attend_done = Event(lse)
    shrink_gather.keep = after(shrink_gather.keep, attend_done)
    att = lax.all_to_all(att, "ctx", 0, 0, tiled=True)
    received = Event(after(after(att, expand_gather), shrink_gather))
    gathered = lax.all_gather(
        after(h1, received).reshape(seqs, rows, features), "ctx", axis=0
    )
    att = received.keep.reshape(pairs, seqs, rows, LANES)
    output_parts = output_gather.result()
    residual, h2, mixed = branch(att, x, vectors, output_parts)
    h2_other = swap_bit(h2, "ctx", ctx_size, 0)
    dh2_send, dh2_keep, out_send, out_keep, send_s, keep_s, send_e, keep_e, eb_grad, sb_grad = feed_forward(
        feed_table,
        residual,
        h2,
        h2_other,
        og,
        og_other,
        vectors,
        expand_vector,
        expand_gather.result(),
        shrink_gather.result(),
        sizes,
    )
    dh2_other = swap_bit(dh2_send, "ctx", ctx_size, 0)
    out_other = swap_bit(out_send, "ctx", ctx_size, 0)

    every = [("fsdp", bit) for bit in reversed(range(bits_of(fsdp_size)))]
    high = [("ctx", bit) for bit in reversed(range(1, bits_of(ctx_size)))]
    flow_s = Flow(send_s, keep_s, every[0], every[1:] + high, every[1:] + high[::-1], sizes)
    dres, dmixed, keep_o, send_o, vec_two = branch_back(
        back_table, dh2_keep, dh2_other, residual, og, mixed, vectors, output_parts, sizes, seqs, rows
    )
    branch_done = Event(vec_two)
    send_e = after(send_e, branch_done)
    flow_e = Flow(send_e, keep_e, every[0], every[1:] + high, every[1:] + high[::-1], sizes)
    spread_s = [bit for _, bit in high] + [0]
    spread_e = spread_s
    flow_o = Flow(send_o, keep_o, ("ctx", 0), every + high, every + high[::-1], sizes)
    dmixed = dmixed.reshape(ctx_size, units, rows, LANES)
    dmixed = lax.all_to_all(dmixed, "ctx", 0, 0, tiled=True)
    dqkv, token = attend_back(
        assignment, unit_seqs, qkv, dmixed, starts, attend_done.keep
    )
    back_done = Event(token)
    last = flow_s.step(back_done)
    out_done = Event(out_other)
    held = Event(after(after(dqkv, last), out_done))
    out_other = out_done.keep
    keep_i, send_i, token = input_weight_terms(gathered, held.keep, terms_table, low, fsdp_size)
    terms_done = Event(token)
    low_labels = [("ctx", bit) for bit in reversed(range(low_bits))]
    flow_i = Flow(
        send_i,
        keep_i,
        low_labels[0],
        low_labels[1:] + every,
        low_labels[1:] + every,
        sizes,
    )
    last = flow_i.step(terms_done)
    last = flow_o.step(last)
    while len(flow_e.order) >= len(high):
        last = flow_e.step(last)
    last = flow_s.step(last)
    dqkv = lax.all_to_all(dqkv, "ctx", 0, 0, tiled=True).reshape(pairs, seqs, rows, 3 * LANES)
    last = flow_o.step(last)
    while flow_i.received is not None:
        last = flow_i.step(last)
    last = flow_s.step(last)
    while len(flow_o.order) > len(flow_e.order):
        last = flow_o.step(last)
    flow_o.received = after(flow_o.received, last)
    last = flow_e.join(flow_o, last)
    flow_s.extra = flow_i.keep[0]
    while flow_s.order:
        last = flow_s.step(last)
    last = flow_s.step(last)
    flow_s.spread(spread_s)
    input_grad, out, sums = entry_back(
        after(dqkv, last),
        x,
        dres,
        out_keep,
        out_other,
        [branch_done.keep, sb_grad, eb_grad],
        vectors,
        (input_gather.result()[0], entry_table),
    )
    totals = Total(sums, every + high[::-1] + [("ctx", 0)], sizes)
    last = totals
    while flow_e.order:
        last = flow_e.step(last)
    last = flow_s.step(last)
    for _ in range(len(every) + 2):
        last = totals.step(last)
    last = flow_e.step(last)
    flow_e.spread(spread_e)
    last = flow_s.step(last)
    last = flow_e.step(last)
    while totals.received is not None:
        last = totals.step(last)
    while len(flow_e.spreading) > 1:
        last = flow_e.step(last)
    while flow_s.spreading:
        last = flow_s.step(last)
    rows_s = hidden // ctx_size
    sums = totals.keep
    own_sums = lax.dynamic_slice_in_dim(sums[:8], y_index * part, part, 1)
    hidden_part = hidden // fsdp_size
    own_hidden = lax.dynamic_slice_in_dim(
        sums[8:].reshape(1, hidden), y_index * hidden_part, hidden_part, 1
    )
    shrink_grad, token = finish(
        flow_s.keep,
        None,
        0,
        finish_table,
        0,
        rows_s,
        part,
        spread_s,
        [own_sums, own_hidden],
    )
    flow_s.received = after(flow_s.received, Event(token))
    last = flow_s.step(last)
    shrink_grad, token = finish(
        flow_s.far, shrink_grad, 1, finish_table, 0, rows_s, part, spread_s
    )
    shrink_done = Event(token)
    input_grad_w, token = finish_extra(
        flow_s.keep,
        flow_s.far,
        finish_table,
        part >> low_bits,
        3 * LANES,
        low_bits,
        (part, 3 * features),
        spread_s,
    )
    input_done = Event(token)
    flow_e.received = after(flow_e.received, shrink_done)
    flow_e.received = after(flow_e.received, input_done)
    while flow_e.spreading:
        last = flow_e.step(last)
    expand_grad, token = finish(
        flow_e.keep, None, 0, finish_table, 1, part, rows_s, spread_e
    )
    flow_e.received = after(flow_e.received, Event(token))
    last = flow_e.step(last)
    expand_grad, token = finish(
        flow_e.far, expand_grad, 1, finish_table, 1, part, rows_s, spread_e
    )
    expand_done = Event(token)
    output_grad_w, _ = finish_rows(
        flow_e.keep,
        flow_e.far,
        finish_table,
        features // ctx_size,
        part,
        None,
        (features, part),
        spread_e,
        [project_done, back_done, terms_done, branch_done, shrink_done, input_done, expand_done],
    )
    return (
        out.reshape(seqs, rows, features),
        input_grad.reshape(seqs, rows, features),
        own_sums[0],
        own_sums[1],
        input_grad_w,
        own_sums[2],
        own_sums[3],
        output_grad_w,
        own_sums[6],
        own_sums[4],
        own_sums[5],
        expand_grad,
        own_hidden[0],
        shrink_grad,
        own_sums[7],
    )


def solution(mesh):
    sizes = (mesh.shape["fsdp"], mesh.shape["ctx"])
    return jax.shard_map(
        functools.partial(body, sizes),
        mesh=mesh,
        in_specs=(
            P("fsdp", "ctx", None),
            P("fsdp", "ctx", None),
            P("fsdp", None),
            P(),
            P("fsdp"),
            P("fsdp"),
            P("fsdp", None),
            P("fsdp"),
            P("fsdp"),
            P(None, "fsdp"),
            P("fsdp"),
            P("fsdp"),
            P("fsdp"),
            P("fsdp", None),
            P("fsdp"),
            P(None, "fsdp"),
            P("fsdp"),
        ),
        out_specs=(
            P("fsdp", "ctx", None),
            P("fsdp", "ctx", None),
            P("fsdp"),
            P("fsdp"),
            P("fsdp", None),
            P("fsdp"),
            P("fsdp"),
            P(None, "fsdp"),
            P("fsdp"),
            P("fsdp"),
            P("fsdp"),
            P("fsdp", None),
            P("fsdp"),
            P(None, "fsdp"),
            P("fsdp"),
        ),
        check_vma=False,
    )
```

```python
import functools
import math

import jax
import jax.numpy as jnp
from jax import lax
from jax.experimental import pallas as pl
from jax.experimental.pallas import tpu as pltpu
from jax.sharding import PartitionSpec as P

HEADS = 16
EPSILON = 1e-05
MASKED = -1000000000.0
LANES = 128
WIDTH = 256
MIB = 1024 * 1024
F32 = jnp.float32
BF16 = jnp.bfloat16
TOKEN = jax.ShapeDtypeStruct((8, LANES), F32)

V_G1, V_B1, V_BQ, V_BV, V_BO, V_G2, V_B2, V_BS = range(8)


def bits_of(number):
    return number.bit_length() - 1


def dot(left, right):
    return jnp.dot(left, right, preferred_element_type=F32)


def dot_nt(left, right):
    return lax.dot_general(left, right, (((1,), (1,)), ((), ())), preferred_element_type=F32)


def dot_tn(left, right):
    return lax.dot_general(left, right, (((0,), (0,)), ((), ())), preferred_element_type=F32)


def swap_bit(value, axis, size, bit):
    return lax.ppermute(value, axis, [(i, i ^ (1 << bit)) for i in range(size)])


class Event:
    def __init__(self, keep):
        self.keep = keep


def after(value, event):
    value, event.keep = lax.optimization_barrier((value, event.keep))
    return value


def params(limit_mib=48):
    return pltpu.CompilerParams(vmem_limit_bytes=limit_mib * MIB)


def whole(shape):
    rank = len(shape)
    return pl.BlockSpec(tuple(shape), lambda *_: (0,) * rank)


def cost(flops, moved):
    return pl.CostEstimate(flops=0, bytes_accessed=0, transcendentals=0)


class Gather:
    def __init__(self, weight, dim, place, bits, core=None):
        (fsdp_size, self.ctx_size), y_index, c_index = place
        extent = weight.shape[dim]
        self.bits = bits
        self.stage = 0
        self.two = fsdp_size == 2
        if not self.two:
            self.bits = ()
            self.parts = []
            self.first = lax.all_gather(weight, "fsdp", axis=dim, tiled=True)
            self.offsets = jnp.zeros((1,), jnp.int32)
            self.held = [self.first]
            return
        size = extent >> len(bits)
        mine = jnp.int32(0)
        for number, bit in enumerate(bits):
            mine = mine | (((c_index >> bit) & 1) << number)
        if core is None:
            self.first = lax.dynamic_slice_in_dim(weight, mine * size, size, dim)
        else:
            half = weight.shape[1 - dim] // 2
            begins = (mine * size, core * half) if dim == 0 else (core * half, mine * size)
            self.first = lax.dynamic_slice(
                weight, begins, (size, half) if dim == 0 else (half, size)
            )
        order = y_index * extent + jnp.zeros((1,), jnp.int32)
        numbers = mine ^ jnp.arange(1 << len(bits), dtype=jnp.int32)
        self.offsets = jnp.concatenate([order, (1 - y_index) * extent + numbers * size])
        self.parts = [weight]

    def fetch(self, event=None):
        if not self.two:
            return
        first = self.first if event is None else after(self.first, event)
        self.held = [swap_bit(first, "fsdp", 2, 0)]

    @property
    def keep(self):
        return self.held[-1]

    @keep.setter
    def keep(self, value):
        self.held[-1] = value

    def exchange(self, event=None):
        if self.stage == len(self.bits):
            return
        bit = self.bits[self.stage]
        if event is not None:
            self.keep = after(self.keep, event)
        self.held = self.held + [swap_bit(array, "ctx", self.ctx_size, bit) for array in self.held]
        self.stage += 1

    def result(self):
        return self.parts + self.held, self.offsets


def place_rows(target, offsets, part_refs):
    for number, ref in enumerate(part_refs):
        rows = ref.shape[0]
        target[pl.ds(pl.multiple_of(offsets[number], 32), rows), :] = ref[...]


def place_columns(target, offsets, part_refs):
    for number, ref in enumerate(part_refs):
        columns = ref.shape[1]
        target[:, pl.ds(pl.multiple_of(offsets[number], LANES), columns)] = ref[...]


def norm_stats(values):
    center = values - jnp.mean(values, axis=-1, keepdims=True)
    spread = jnp.mean(center * center, axis=-1, keepdims=True)
    rate = lax.rsqrt(spread + EPSILON)
    return center * rate, rate


def norm_kernel(sc_ref, x_ref, *refs):
    shards = refs[:-3]
    h_ref, v_ref, e_ref = refs[-3:]
    part = v_ref.shape[1] // len(shards)
    hidden = e_ref.shape[1] // len(shards)
    for number, ref in enumerate(shards):
        where = sc_ref[number]
        for row in range(8):
            v_ref[row : row + 1, pl.ds(pl.multiple_of(where * part, LANES), part)] = ref[
                :, row * part : (row + 1) * part
            ].astype(F32)
        e_ref[:, pl.ds(pl.multiple_of(where * hidden, LANES), hidden)] = ref[:, 8 * part :].astype(
            F32
        )
    hat, _ = norm_stats(x_ref[...].astype(F32))
    h_ref[...] = (hat * v_ref[V_G1 : V_G1 + 1, :] + v_ref[V_B1 : V_B1 + 1, :]).astype(BF16)


def first_norm(x, shards, owners, hidden):
    shapes = [
        jax.ShapeDtypeStruct(x.shape, BF16),
        jax.ShapeDtypeStruct((8, x.shape[1]), F32),
        jax.ShapeDtypeStruct((1, hidden), F32),
    ]
    return pl.pallas_call(
        norm_kernel,
        grid_spec=pltpu.PrefetchScalarGridSpec(
            num_scalar_prefetch=1,
            grid=(1,),
            in_specs=[whole(x.shape)] + [whole(shard.shape) for shard in shards],
            out_specs=[whole(shape.shape) for shape in shapes],
        ),
        out_shape=shapes,
        compiler_params=params(),
        cost_estimate=cost(0, 0),
        name="first_norm",
    )(owners, x, *shards)


def qkv_kernel(part_count, seqs, rows, off_ref, h_ref, v_ref, *refs):
    parts = refs[: 3 * part_count]
    out_ref, token_ref, weight = refs[3 * part_count :]
    token_ref[...] = jnp.zeros_like(token_ref)
    group = pl.program_id(0)
    width = weight.shape[-1]
    per = width // LANES
    for kind in range(3):
        place_rows(
            weight.at[kind], off_ref, parts[kind * part_count : (kind + 1) * part_count]
        )
        value = dot(h_ref[...], weight[kind])
        if kind != 1:
            row = V_BQ if kind == 0 else V_BV
            start = pl.multiple_of(group * width, LANES)
            value = value + v_ref[row : row + 1, pl.ds(start, width)]
        value = value.astype(BF16)
        for pair in range(per):
            out_ref[pair, :, :, kind * LANES : (kind + 1) * LANES] = value[
                :, pair * LANES : (pair + 1) * LANES
            ].reshape(seqs, rows, LANES)


def project(h1, vectors, parts, seqs, rows):
    arrays, offsets = parts
    tokens, features = h1.shape
    width = 2 * LANES
    groups = features // width
    pairs = features // LANES
    specs = []
    operands = []
    for kind in range(3):
        for array in arrays:
            specs.append(
                pl.BlockSpec((array.shape[0], width), lambda g, o, k=kind: (0, k * groups + g))
            )
            operands.append(array)
    return pl.pallas_call(
        functools.partial(qkv_kernel, len(arrays), seqs, rows),
        grid_spec=pltpu.PrefetchScalarGridSpec(
            num_scalar_prefetch=1,
            grid=(groups,),
            in_specs=[whole(h1.shape), whole(vectors.shape)] + specs,
            out_specs=[
                pl.BlockSpec((2, seqs, rows, 3 * LANES), lambda g, o: (g, 0, 0, 0)),
                whole(TOKEN.shape),
            ],
            scratch_shapes=[pltpu.VMEM((3, features, width), BF16)],
        ),
        out_shape=[jax.ShapeDtypeStruct((pairs, seqs, rows, 3 * LANES), BF16), TOKEN],
        compiler_params=params(),
        cost_estimate=cost(6 * tokens * features * features, 6 * features * features),
        name="project",
    )(offsets, h1, vectors, *operands)


def to_places(table, ctx_size, half, source, target):
    for device in range(ctx_size):
        pair = table[device]
        early = pl.multiple_of(pair * half, half)
        later = pl.multiple_of((2 * ctx_size - 1 - pair) * half, half)
        target[pl.ds(early, half), :] = source[device, 0, 0:half, :]
        target[pl.ds(later, half), :] = source[device, 0, half : 2 * half, :]


def both_heads(block):
    first = lax.broadcasted_iota(jnp.int32, block.shape, 0) < LANES // 2
    zero = jnp.zeros_like(block)
    return jnp.concatenate([jnp.where(first, block, zero), jnp.where(first, zero, block)], axis=1)


def stacked_heads(block):
    first = lax.broadcasted_iota(jnp.int32, block.shape, 1) < LANES // 2
    zero = jnp.zeros_like(block)
    return jnp.concatenate([jnp.where(first, block, zero), jnp.where(first, zero, block)], axis=0)


def flipped(block):
    return block.astype(F32).T.astype(BF16)


def band_mask(low, high, start_row, size):
    count = high - low
    key = lax.broadcasted_iota(jnp.int32, (count, 2 * size), 0) + low
    query = lax.broadcasted_iota(jnp.int32, (count, 2 * size), 1) % size + (high - size)
    return (key >= start_row) & (key <= query)


def attend_kernel(
    ctx_size, table, seq_ref, qkv_ref, start_ref, out_ref, lse_ref, held, query_t, value_t, mixed
):
    length = held.shape[0]
    half = length // (2 * ctx_size)
    size = LANES
    blocks = length // size
    reach = blocks // 2
    to_places(table, ctx_size, half, qkv_ref, held)
    for block in range(blocks):
        span = slice(block * size, (block + 1) * size)
        query_t[:, span] = (held[span, 0:LANES].astype(F32) * 0.125).T.astype(BF16)
        value_t[:, span] = flipped(held[span, 2 * LANES :])
    for block in range(blocks):
        low = max(0, block - reach) * size
        high = (block + 1) * size
        span = slice(block * size, high)
        scores = dot(held[low:high, LANES : 2 * LANES], both_heads(query_t[:, span]))
        start_row = start_ref[0, :, span]
        start_row = jnp.concatenate([start_row, start_row], axis=1)
        scores = jnp.where(band_mask(low, high, start_row, size), scores, MASKED)
        top = jnp.max(scores, axis=0, keepdims=True)
        weights = jnp.exp(scores - top)
        total = jnp.sum(weights, axis=0, keepdims=True)
        lse = top + jnp.log(total)
        probs = (weights * (1.0 / total)).astype(BF16)
        lse_ref[0, 0:1, span] = lse[:, :size]
        lse_ref[0, 1:2, span] = lse[:, size:]
        mixed_t = dot(value_t[:, low:high], probs)
        both = jnp.concatenate(
            [mixed_t[0 : LANES // 2, :size], mixed_t[LANES // 2 :, size:]], axis=0
        )
        mixed[span, :] = both.T.astype(BF16)
    for device in range(ctx_size):
        pair = table[device]
        early = pl.multiple_of(pair * half, half)
        later = pl.multiple_of((2 * ctx_size - 1 - pair) * half, half)
        out_ref[device, 0, 0:half, :] = mixed[pl.ds(early, half), :]
        out_ref[device, 0, half : 2 * half, :] = mixed[pl.ds(later, half), :]


def attend(table, unit_seqs, qkv, starts):
    ctx_size, units, rows, width = qkv.shape
    length = ctx_size * rows
    return pl.pallas_call(
        functools.partial(attend_kernel, ctx_size),
        grid_spec=pltpu.PrefetchScalarGridSpec(
            num_scalar_prefetch=2,
            grid=(units,),
            in_specs=[
                pl.BlockSpec((ctx_size, 1, rows, width), lambda u, t, s: (0, u, 0, 0)),
                pl.BlockSpec((1, 1, length), lambda u, t, s: (s[u], 0, 0)),
            ],
            out_specs=[
                pl.BlockSpec((ctx_size, 1, rows, LANES), lambda u, t, s: (0, u, 0, 0)),
                pl.BlockSpec((1, 2, length), lambda u, t, s: (u, 0, 0)),
            ],
            scratch_shapes=[
                pltpu.VMEM((length, width), BF16),
                pltpu.VMEM((LANES, length), BF16),
                pltpu.VMEM((LANES, length), BF16),
                pltpu.VMEM((length, LANES), BF16),
            ],
        ),
        out_shape=[
            jax.ShapeDtypeStruct((ctx_size, units, rows, LANES), BF16),
            jax.ShapeDtypeStruct((units, 2, length), F32),
        ],
        compiler_params=params(),
        cost_estimate=cost(units * length * length * 256, qkv.size * 4),
        name="attend",
    )(table, unit_seqs, qkv, starts)


def attend_back_kernel(
    ctx_size,
    table,
    seq_ref,
    qkv_ref,
    grad_ref,
    start_ref,
    lse_ref,
    out_ref,
    token_ref,
    held,
    grad,
    query_t,
    key_t,
    grad_t,
    query_grad,
    key_grad,
    value_grad,
):
    token_ref[...] = jnp.zeros_like(token_ref)
    length = held.shape[0]
    half = length // (2 * ctx_size)
    size = LANES
    blocks = length // size
    reach = blocks // 2
    to_places(table, ctx_size, half, qkv_ref, held)
    to_places(table, ctx_size, half, grad_ref, grad)
    for block in range(blocks):
        span = slice(block * size, (block + 1) * size)
        scaled = (held[span, 0:LANES].astype(F32) * 0.125).astype(BF16)
        held[span, 0:LANES] = scaled
        query_t[:, span] = flipped(scaled)
        key_t[:, span] = flipped(held[span, LANES : 2 * LANES])
        grad_t[:, span] = flipped(grad[span, :])
    for block in range(blocks):
        low = max(0, block - reach) * size
        high = (block + 1) * size
        span = slice(block * size, high)
        scores = dot(held[low:high, LANES : 2 * LANES], both_heads(query_t[:, span]))
        start_row = start_ref[0, :, span]
        start_row = jnp.concatenate([start_row, start_row], axis=1)
        scores = jnp.where(band_mask(low, high, start_row, size), scores, MASKED)
        lse = jnp.concatenate([lse_ref[0, 0:1, span], lse_ref[0, 1:2, span]], axis=1)
        probs = jnp.exp(scores - lse)
        prob_grad = dot(held[low:high, 2 * LANES :], both_heads(grad_t[:, span]))
        delta = jnp.sum(probs * prob_grad, axis=0, keepdims=True)
        score_grad = (probs * (prob_grad - delta)).astype(BF16)
        probs = probs.astype(BF16)
        new_value = dot(probs, stacked_heads(grad[span, :]))
        new_key = dot(score_grad, stacked_heads(held[span, 0:LANES]))
        if low < high - size:
            value_grad[low : high - size, :] += new_value[: high - size - low]
            key_grad[low : high - size, :] += new_key[: high - size - low]
        value_grad[span, :] = new_value[high - size - low :]
        key_grad[span, :] = new_key[high - size - low :]
        query_t_grad = dot(key_t[:, low:high], score_grad)
        both = jnp.concatenate(
            [query_t_grad[0 : LANES // 2, :size], query_t_grad[LANES // 2 :, size:]], axis=0
        )
        query_grad[span, :] = (both.T * 0.125).astype(BF16)
    for device in range(ctx_size):
        pair = table[device]
        early = pl.multiple_of(pair * half, half)
        later = pl.multiple_of((2 * ctx_size - 1 - pair) * half, half)
        for place, source in ((0, early), (half, later)):
            rows = pl.ds(source, half)
            out_ref[device, 0, place : place + half, 0:LANES] = query_grad[rows, :]
            out_ref[device, 0, place : place + half, LANES : 2 * LANES] = key_grad[
                rows, :
            ].astype(BF16)
            out_ref[device, 0, place : place + half, 2 * LANES :] = value_grad[rows, :].astype(
                BF16
            )


def attend_back(table, unit_seqs, qkv, grad, starts, lse):
    ctx_size, units, rows, width = qkv.shape
    length = ctx_size * rows
    return pl.pallas_call(
        functools.partial(attend_back_kernel, ctx_size),
        grid_spec=pltpu.PrefetchScalarGridSpec(
            num_scalar_prefetch=2,
            grid=(units,),
            in_specs=[
                pl.BlockSpec((ctx_size, 1, rows, width), lambda u, t, s: (0, u, 0, 0)),
                pl.BlockSpec((ctx_size, 1, rows, LANES), lambda u, t, s: (0, u, 0, 0)),
                pl.BlockSpec((1, 1, length), lambda u, t, s: (s[u], 0, 0)),
                pl.BlockSpec((1, 2, length), lambda u, t, s: (u, 0, 0)),
            ],
            out_specs=[
                pl.BlockSpec((ctx_size, 1, rows, width), lambda u, t, s: (0, u, 0, 0)),
                whole(TOKEN.shape),
            ],
            scratch_shapes=[
                pltpu.VMEM((length, width), BF16),
                pltpu.VMEM((length, LANES), BF16),
                pltpu.VMEM((LANES, length), BF16),
                pltpu.VMEM((LANES, length), BF16),
                pltpu.VMEM((LANES, length), BF16),
                pltpu.VMEM((length, LANES), BF16),
                pltpu.VMEM((length, LANES), F32),
                pltpu.VMEM((length, LANES), F32),
            ],
        ),
        out_shape=[jax.ShapeDtypeStruct(qkv.shape, BF16), TOKEN],
        compiler_params=params(),
        cost_estimate=cost(units * length * length * 640, qkv.size * 6),
        name="attend_back",
    )(table, unit_seqs, qkv, grad, starts, lse)


def branch_kernel(off_ref, att_ref, x_ref, v_ref, *refs):
    residual_ref, h2_ref, mixed_ref, weight = refs[-4:]
    pairs = att_ref.shape[0]
    tokens = x_ref.shape[0]
    for pair in range(pairs):
        mixed_ref[:, pair * LANES : (pair + 1) * LANES] = att_ref[pair].reshape(tokens, LANES)
    place_columns(weight, off_ref, refs[:-4])
    residual = (
        x_ref[...].astype(F32) + dot(mixed_ref[...], weight[...]) + v_ref[V_BO : V_BO + 1, :]
    )
    residual_ref[...] = residual
    hat, _ = norm_stats(residual)
    h2_ref[...] = (hat * v_ref[V_G2 : V_G2 + 1, :] + v_ref[V_B2 : V_B2 + 1, :]).astype(BF16)


def branch(att, x, vectors, parts):
    arrays, offsets = parts
    tokens, features = x.shape
    return pl.pallas_call(
        branch_kernel,
        grid_spec=pltpu.PrefetchScalarGridSpec(
            num_scalar_prefetch=1,
            grid=(1,),
            in_specs=[whole(att.shape), whole(x.shape), whole(vectors.shape)]
            + [whole(array.shape) for array in arrays],
            out_specs=[whole(x.shape)] * 3,
            scratch_shapes=[pltpu.VMEM((features, features), BF16)],
        ),
        out_shape=[
            jax.ShapeDtypeStruct(x.shape, F32),
            jax.ShapeDtypeStruct(x.shape, BF16),
            jax.ShapeDtypeStruct(x.shape, BF16),
        ],
        compiler_params=params(),
        cost_estimate=cost(2 * tokens * features * features, 2 * features * features),
        name="branch",
    )(offsets, att, x, vectors, *arrays)


def ffn_kernel(
    expand_count,
    shrink_count,
    steps,
    sc_ref,
    residual_ref,
    h2_ref,
    h2_other_ref,
    og_ref,
    og_other_ref,
    v_ref,
    eb_ref,
    *refs,
):
    expand_parts = refs[:expand_count]
    shrink_parts = refs[expand_count : expand_count + shrink_count]
    (
        dh2_send,
        dh2_keep,
        out_send,
        out_keep,
        send_s,
        keep_s,
        send_e,
        keep_e,
        eb_grad_ref,
        sb_grad_ref,
        expand,
        shrink,
        total,
        back,
        h2,
        h2_t,
        og,
    ) = refs[expand_count + shrink_count :]
    step = pl.program_id(0)
    y_index = sc_ref[0]
    low_label = sc_ref[2]
    expand_offsets = [sc_ref[4 + i] for i in range(expand_count)]
    shrink_offsets = [sc_ref[4 + expand_count + i] for i in range(shrink_count)]
    tokens = h2_ref.shape[0]

    @pl.when(step == 0)
    def _():
        total[:tokens] = residual_ref[...] + v_ref[V_BS : V_BS + 1, :]
        total[tokens:] = jnp.zeros_like(residual_ref)
        back[...] = jnp.zeros_like(back)
        h2[:tokens] = h2_ref[...]
        h2[tokens:] = h2_other_ref[...]
        og[:tokens] = og_ref[...]
        og[tokens:] = og_other_ref[...]
        h2_t[...] = h2[...].astype(F32).T.astype(BF16)
        sb_grad_ref[...] = jnp.sum(og_ref[...].astype(F32), axis=0, keepdims=True)

    place_rows(expand, expand_offsets, expand_parts)
    place_columns(shrink, shrink_offsets, shrink_parts)
    pre = dot(h2[...], expand[...]) + eb_ref[...]
    root = math.sqrt(2.0 / math.pi)
    square = pre * pre
    curve = jnp.tanh(root * (pre + 0.044715 * (square * pre)))
    slope = 0.5 * (1.0 + curve)
    active = (pre * slope).astype(BF16)
    slope = slope + (0.5 * root) * pre * (1.0 - curve * curve) * (1.0 + 0.134145 * square)
    total[...] += dot(active, shrink[...])
    dpre = (dot_nt(og[...], shrink[...]) * slope).astype(BF16)
    eb_grad_ref[...] = jnp.sum(dpre.astype(F32), axis=0, keepdims=True)
    back[...] += dot_nt(dpre, expand[...])
    shrink_grad = dot_tn(active, og[...]).astype(BF16)
    expand_grad = dot(h2_t[...], dpre).astype(BF16)

    fsdp_half, _, subs, rows, columns = send_s.shape
    for part in range(2 * fsdp_half):
        there = slice(part * columns, (part + 1) * columns)
        place = part ^ y_index

        def store(target_s, target_e, there=there, place=place):
            for sub in range(subs):
                here = slice(sub * rows, (sub + 1) * rows)
                index = (place & (fsdp_half - 1), 0, sub ^ low_label)
                target_s[index] = shrink_grad[here, there]
                target_e[index] = expand_grad[there, here]

        pl.when(place < fsdp_half)(functools.partial(store, keep_s, keep_e))
        pl.when(place >= fsdp_half)(functools.partial(store, send_s, send_e))

    @pl.when(step == steps - 1)
    def _():
        dh2_keep[...] = back[:tokens]
        out_keep[...] = total[:tokens]
        dh2_send[...] = back[tokens:]
        out_send[...] = total[tokens:]


def feed_scalars(place, hidden, width, expand_offsets, shrink_offsets):
    (_, ctx_size), y_index, c_index = place
    subs = width * ctx_size // hidden
    label = c_index >> 1
    first = [y_index, label >> bits_of(subs), label & (subs - 1), c_index & 1]
    return jnp.concatenate([jnp.stack(first), expand_offsets, shrink_offsets])


def feed_forward(
    scalars, residual, h2, h2_other, og, og_other, vectors, expand_bias, expand, shrink, sizes
):
    fsdp_size, ctx_size = sizes
    expand_arrays = expand[0]
    shrink_arrays = shrink[0]
    tokens, features = h2.shape
    hidden = expand_bias.shape[1]
    rows = hidden // ctx_size
    columns = features // fsdp_size
    width = WIDTH
    subs = width // rows
    steps = hidden // (2 * width)
    def chunk(array, dim):
        if array.shape[dim] == hidden:
            return lambda s, sc: sc[3] * steps + (s ^ sc[1])
        return lambda s, sc: s ^ sc[1]

    def columns_of(array):
        index = chunk(array, 1)
        return pl.BlockSpec((array.shape[0], width), lambda s, sc: (0, index(s, sc)))

    def rows_of(array):
        index = chunk(array, 0)
        return pl.BlockSpec((width, array.shape[1]), lambda s, sc: (index(s, sc), 0))

    grad_s = (fsdp_size // 2, steps, subs, rows, columns)
    grad_e = (fsdp_size // 2, steps, subs, columns, rows)

    def block(shape):
        return pl.BlockSpec((shape[0], 1) + shape[2:], lambda s, sc: (0, s, 0, 0, 0))

    full = whole(h2.shape)
    wide = jax.ShapeDtypeStruct(h2.shape, F32)
    return pl.pallas_call(
        functools.partial(ffn_kernel, len(expand_arrays), len(shrink_arrays), steps),
        grid_spec=pltpu.PrefetchScalarGridSpec(
            num_scalar_prefetch=1,
            grid=(steps,),
            in_specs=[full] * 5
            + [whole(vectors.shape), columns_of(expand_bias)]
            + [columns_of(array) for array in expand_arrays]
            + [rows_of(array) for array in shrink_arrays],
            out_specs=[full] * 4
            + [block(grad_s)] * 2
            + [block(grad_e)] * 2
            + [pl.BlockSpec((1, width), lambda s, sc: (0, s ^ sc[1])), whole((1, features))],
            scratch_shapes=[
                pltpu.VMEM((features, width), BF16),
                pltpu.VMEM((width, features), BF16),
                pltpu.VMEM((2 * tokens, features), F32),
                pltpu.VMEM((2 * tokens, features), F32),
                pltpu.VMEM((2 * tokens, features), BF16),
                pltpu.VMEM((features, 2 * tokens), BF16),
                pltpu.VMEM((2 * tokens, features), BF16),
            ],
        ),
        out_shape=[wide] * 4
        + [jax.ShapeDtypeStruct(grad_s, BF16)] * 2
        + [jax.ShapeDtypeStruct(grad_e, BF16)] * 2
        + [
            jax.ShapeDtypeStruct((1, hidden // 2), F32),
            jax.ShapeDtypeStruct((1, features), F32),
        ],
        compiler_params=params(),
        cost_estimate=cost(0, 0),
        name="feed_forward",
    )(
        scalars,
        residual,
        h2,
        h2_other,
        og,
        og_other,
        vectors,
        expand_bias,
        *expand_arrays,
        *shrink_arrays,
    )


def branch_back_kernel(
    part_count, seqs, rows, sc_ref, dh2_ref, dh2_other_ref, residual_ref, og_ref, mixed_ref, v_ref, *refs
):
    parts = refs[:part_count]
    dres_ref, dmixed_ref, keep_ref, send_ref, vec_ref, weight, rounded = refs[part_count:]
    place_columns(weight, sc_ref, parts)
    hat, rate = norm_stats(residual_ref[...])
    dh2 = dh2_ref[...] + dh2_other_ref[...]
    scaled = dh2 * v_ref[V_G2 : V_G2 + 1, :]
    first = jnp.mean(scaled, axis=-1, keepdims=True)
    second = jnp.mean(scaled * hat, axis=-1, keepdims=True)
    dres = og_ref[...].astype(F32) + rate * (scaled - first - hat * second)
    dres_ref[...] = dres
    rounded[...] = dres.astype(BF16)
    vec_ref[0:1, :] = jnp.sum(dh2 * hat, axis=0, keepdims=True)
    vec_ref[1:2, :] = jnp.sum(dh2, axis=0, keepdims=True)
    vec_ref[2:3, :] = jnp.sum(rounded[...].astype(F32), axis=0, keepdims=True)
    vec_ref[3:, :] = jnp.zeros((vec_ref.shape[0] - 3, vec_ref.shape[1]), F32)
    dmixed = dot_nt(rounded[...], weight[...]).astype(BF16)
    for pair in range(dmixed_ref.shape[0]):
        dmixed_ref[pair] = dmixed[:, pair * LANES : (pair + 1) * LANES].reshape(seqs, rows, LANES)
    fsdp_size, count, size, columns = keep_ref.shape
    grad = dot_tn(mixed_ref[...], rounded[...]).astype(BF16)
    y_index = sc_ref[part_count]
    label = sc_ref[part_count + 1]
    for number in range(2 * count):
        place = number ^ label

        def store(target, number=number, place=place):
            for part in range(fsdp_size):
                target[part ^ y_index, place >> 1] = grad[
                    number * size : (number + 1) * size, part * columns : (part + 1) * columns
                ]

        pl.when((place & 1) == 0)(functools.partial(store, keep_ref))
        pl.when((place & 1) == 1)(functools.partial(store, send_ref))


def branch_back(scalars, dh2, dh2_other, residual, og, mixed, vectors, parts, sizes, seqs, rows):
    fsdp_size, ctx_size = sizes
    arrays, offsets = parts
    tokens, features = residual.shape
    pairs = features // LANES
    grad = (fsdp_size, ctx_size // 2, features // ctx_size, features // fsdp_size)
    full = whole(residual.shape)
    return pl.pallas_call(
        functools.partial(branch_back_kernel, len(arrays), seqs, rows),
        grid_spec=pltpu.PrefetchScalarGridSpec(
            num_scalar_prefetch=1,
            grid=(1,),
            in_specs=[full] * 5 + [whole(vectors.shape)]
            + [whole(array.shape) for array in arrays],
            out_specs=[
                full,
                whole((pairs, seqs, rows, LANES)),
                whole(grad),
                whole(grad),
                whole((8, features)),
            ],
            scratch_shapes=[
                pltpu.VMEM((features, features), BF16),
                pltpu.VMEM((tokens, features), BF16),
            ],
        ),
        out_shape=[
            jax.ShapeDtypeStruct(residual.shape, F32),
            jax.ShapeDtypeStruct((pairs, seqs, rows, LANES), BF16),
            jax.ShapeDtypeStruct(grad, BF16),
            jax.ShapeDtypeStruct(grad, BF16),
            jax.ShapeDtypeStruct((8, features), F32),
        ],
        compiler_params=params(),
        cost_estimate=cost(4 * tokens * features * features, 8 * features * features),
        name="branch_back",
    )(scalars, dh2, dh2_other, residual, og, mixed, vectors, *arrays)


def input_terms_kernel(sc_ref, h_ref, d_ref, keep_ref, send_ref, token_ref):
    token_ref[...] = jnp.zeros_like(token_ref)
    left = h_ref[...].reshape(-1, h_ref.shape[-1])
    right = d_ref[...].reshape(-1, d_ref.shape[-1])
    value = dot_tn(left, right).astype(BF16)
    half, fsdp_size, rows, _ = keep_ref.shape
    per = value.shape[0] // rows
    for number in range(per):
        place = pl.program_id(0) * per + number
        part = (place // (2 * half)) ^ sc_ref[1]
        own = (place & (2 * half - 1)) ^ sc_ref[2]

        def store(target, number=number, part=part, own=own):
            target[own & (half - 1), part] = value[number * rows : (number + 1) * rows]

        pl.when(own < half)(functools.partial(store, keep_ref))
        pl.when(own >= half)(functools.partial(store, send_ref))


def input_weight_terms(gathered, dqkv, scalars, low, fsdp_size):
    ctx_size, units, rows, width = dqkv.shape
    features = gathered.shape[-1]
    block = 2 * LANES
    out = (low // 2, fsdp_size, features // (low * fsdp_size), width)
    return pl.pallas_call(
        input_terms_kernel,
        grid_spec=pltpu.PrefetchScalarGridSpec(
            num_scalar_prefetch=1,
            grid=(features // block,),
            in_specs=[
                pl.BlockSpec((ctx_size, units, rows, block), lambda g, s: (0, s[0], 0, g)),
                whole(dqkv.shape),
            ],
            out_specs=[whole(out), whole(out), whole(TOKEN.shape)],
        ),
        out_shape=[jax.ShapeDtypeStruct(out, BF16)] * 2 + [TOKEN],
        compiler_params=params(),
        cost_estimate=cost(0, 0),
        name="input_weight_terms",
    )(scalars, gathered, dqkv)


def entry_back_kernel(
    part_count,
    groups,
    off_ref,
    d_ref,
    x_ref,
    dres_ref,
    one_ref,
    two_ref,
    second_ref,
    sb_ref,
    eb_ref,
    v_ref,
    *refs,
):
    parts = refs[: 3 * part_count]
    out_ref, layer_ref, vec_ref, weight, back = refs[3 * part_count :]
    group = pl.program_id(0)
    tokens = x_ref.shape[0]
    width = weight.shape[-1]

    @pl.when(group == 0)
    def _():
        back[...] = jnp.zeros_like(back)
        layer_ref[...] = (one_ref[...] + two_ref[...]).astype(BF16)
        vec_ref[4:7, :] = second_ref[0:3, :]
        vec_ref[7:8, :] = sb_ref[...]
        count = vec_ref.shape[0] - 8
        core = off_ref[off_ref.shape[0] - 1]
        for row in range(count):
            here = eb_ref[:, (row % (count // 2)) * LANES * 8 : (row % (count // 2) + 1) * LANES * 8]
            mine = core == row // (count // 2)
            vec_ref[8 + row : 9 + row, :] = jnp.where(mine, here, jnp.zeros_like(here))

    for kind in range(3):
        place_rows(
            weight.at[kind], off_ref, parts[kind * part_count : (kind + 1) * part_count]
        )
        lanes = slice(kind * LANES, (kind + 1) * LANES)
        value = jnp.concatenate(
            [d_ref[pair, :, :, lanes].reshape(tokens, LANES) for pair in range(d_ref.shape[0])],
            axis=1,
        )
        back[...] += dot_nt(value, weight[kind])
        if kind != 1:
            row = 2 if kind == 0 else 3
            start = pl.multiple_of(group * width, LANES)
            vec_ref[row : row + 1, pl.ds(start, width)] = jnp.sum(
                value.astype(F32), axis=0, keepdims=True
            )

    @pl.when(group == groups - 1)
    def _():
        hat, rate = norm_stats(x_ref[...].astype(F32))
        dh1 = back[...]
        scaled = dh1 * v_ref[V_G1 : V_G1 + 1, :]
        first = jnp.mean(scaled, axis=-1, keepdims=True)
        second = jnp.mean(scaled * hat, axis=-1, keepdims=True)
        out_ref[...] = dres_ref[...] + rate * (scaled - first - hat * second)
        vec_ref[0:1, :] = jnp.sum(dh1 * hat, axis=0, keepdims=True)
        vec_ref[1:2, :] = jnp.sum(dh1, axis=0, keepdims=True)


def entry_back(dqkv, x, dres, one, two, sums, vectors, parts):
    arrays, offsets = parts
    tokens, features = x.shape
    pairs, seqs, rows, _ = dqkv.shape
    width = 2 * LANES
    vec = (8 + 2 * sums[2].shape[1] // features, features)
    groups = features // width
    specs = []
    operands = []
    for kind in range(3):
        for array in arrays:
            specs.append(
                pl.BlockSpec((array.shape[0], width), lambda g, o, k=kind: (0, k * groups + g))
            )
            operands.append(array)
    return pl.pallas_call(
        functools.partial(entry_back_kernel, len(arrays), groups),
        grid_spec=pltpu.PrefetchScalarGridSpec(
            num_scalar_prefetch=1,
            grid=(groups,),
            in_specs=[
                pl.BlockSpec((2, seqs, rows, 3 * LANES), lambda g, o: (g, 0, 0, 0)),
                whole(x.shape),
                whole(x.shape),
                whole(x.shape),
                whole(x.shape),
            ]
            + [whole(array.shape) for array in sums]
            + [whole(vectors.shape)]
            + specs,
            out_specs=[whole(x.shape), whole(x.shape), whole(vec)],
            scratch_shapes=[
                pltpu.VMEM((3, features, width), BF16),
                pltpu.VMEM((tokens, features), F32),
            ],
        ),
        out_shape=[
            jax.ShapeDtypeStruct(x.shape, F32),
            jax.ShapeDtypeStruct(x.shape, BF16),
            jax.ShapeDtypeStruct(vec, F32),
        ],
        compiler_params=params(),
        cost_estimate=cost(6 * tokens * features * features, 6 * features * features),
        name="entry_back",
    )(offsets, dqkv, x, dres, one, two, *sums, vectors, *operands)


def combine_kernel(one_ref, two_ref, send_ref, keep_ref):
    total = (one_ref[...].astype(F32) + two_ref[...].astype(F32)).astype(BF16)
    keep_ref[...] = total[:, 0]
    send_ref[...] = total[:, 1]


def last_kernel(one_ref, two_ref, out_ref):
    out_ref[...] = (one_ref[...].astype(F32) + two_ref[...].astype(F32)).astype(BF16)


def combine(one, two, outer):
    rows, columns = one.shape[-2:]
    shape = (outer, 2, one.size // (2 * outer * rows * columns), rows, columns)
    inner = shape[2]
    per = inner
    while per * rows * columns > 256 * 1024 and per % 2 == 0:
        per //= 2
    half = (outer, inner, rows, columns)
    block = pl.BlockSpec((1, 2, per, rows, columns), lambda a, b: (a, 0, b, 0, 0))
    out = pl.BlockSpec((1, per, rows, columns), lambda a, b: (a, b, 0, 0))
    return pl.pallas_call(
        combine_kernel,
        grid=(outer, inner // per),
        in_specs=[block, block],
        out_specs=[out, out],
        out_shape=[jax.ShapeDtypeStruct(half, BF16)] * 2,
        compiler_params=params(),
        cost_estimate=cost(0, 0),
        name="combine",
    )(one.reshape(shape), two.reshape(shape))


def add_last(one, two):
    rows, columns = one.shape[-2:]
    return pl.pallas_call(
        last_kernel,
        out_shape=jax.ShapeDtypeStruct((1, rows, columns), BF16),
        compiler_params=params(),
        cost_estimate=cost(0, 0),
        name="add_last",
    )(one.reshape(1, rows, columns), two.reshape(1, rows, columns))


def merge_kernel(one_ref, two_ref, out_ref):
    out_ref[:, 0] = one_ref[...]
    out_ref[:, 1] = two_ref[...]


def merge(one, two):
    count, rows, columns = one.shape
    block = pl.BlockSpec((1, rows, columns), lambda n: (n, 0, 0))
    return pl.pallas_call(
        merge_kernel,
        grid=(count,),
        in_specs=[block, block],
        out_specs=pl.BlockSpec((1, 2, rows, columns), lambda n: (n, 0, 0, 0)),
        out_shape=jax.ShapeDtypeStruct((count, 2, rows, columns), BF16),
        compiler_params=params(),
        cost_estimate=cost(0, 0),
        name="merge",
    )(one, two).reshape(2 * count, rows, columns)


def tiles(rows, width, columns):
    count = columns // LANES
    height = rows // count
    return height, [
        (across * height, down * LANES, down * height, across * LANES)
        for down in range(width // LANES)
        for across in range(count)
    ]


def pack_kernel(one_ref, two_ref, extra_ref, out_ref):
    rows, columns = one_ref.shape[1:]
    first = out_ref.shape[1] - rows
    out_ref[:, first:] = (one_ref[...].astype(F32) + two_ref[...].astype(F32)).astype(BF16)
    height, moves = tiles(*extra_ref.shape, columns)
    for row, column, to_row, to_column in moves:
        out_ref[0, to_row : to_row + height, to_column : to_column + LANES] = extra_ref[
            row : row + height, column : column + LANES
        ]


def pack(one, two, extra):
    rows, columns = one.shape[-2:]
    return pl.pallas_call(
        pack_kernel,
        out_shape=jax.ShapeDtypeStruct((1, rows + extra.size // columns, columns), BF16),
        compiler_params=params(),
        cost_estimate=cost(0, 0),
        name="pack",
    )(one.reshape(1, rows, columns), two.reshape(1, rows, columns), extra)


def join_kernel(one_ref, two_ref, extra_one_ref, extra_two_ref, send_ref, keep_ref):
    rows, columns = one_ref.shape[-2:]
    height, moves = tiles(*extra_one_ref.shape[-2:], columns)
    first = keep_ref.shape[1] - rows
    for half, target in ((0, keep_ref), (1, send_ref)):
        value = one_ref[0, half].astype(F32) + two_ref[0, half].astype(F32)
        target[0, first:] = value.astype(BF16)
        value = extra_one_ref[0, half].astype(F32) + extra_two_ref[0, half].astype(F32)
        value = value.astype(BF16)
        for row, column, to_row, to_column in moves:
            target[0, to_row : to_row + height, to_column : to_column + LANES] = value[
                row : row + height, column : column + LANES
            ]


def join(one, two, extra_one, extra_two, outer):
    rows, columns = one.shape[-2:]
    extra_rows, extra_columns = extra_one.shape[-2:]
    height = rows + extra_rows * extra_columns // columns
    block = pl.BlockSpec((1, 2, rows, columns), lambda n: (n, 0, 0, 0))
    extra = pl.BlockSpec((1, 2, extra_rows, extra_columns), lambda n: (n, 0, 0, 0))
    out = pl.BlockSpec((1, height, columns), lambda n: (n, 0, 0))
    shape = (outer, 2, rows, columns)
    extra_shape = (outer, 2, extra_rows, extra_columns)
    return pl.pallas_call(
        join_kernel,
        grid=(outer,),
        in_specs=[block, block, extra, extra],
        out_specs=[out, out],
        out_shape=[jax.ShapeDtypeStruct((outer, height, columns), BF16)] * 2,
        compiler_params=params(),
        cost_estimate=cost(0, 0),
        name="join",
    )(
        one.reshape(shape),
        two.reshape(shape),
        extra_one.reshape(extra_shape),
        extra_two.reshape(extra_shape),
    )


class Flow:
    def __init__(self, send, keep, first, labels, order, sizes):
        self.sizes = dict(fsdp=sizes[0], ctx=sizes[1])
        self.labels = list(labels)
        self.order = list(order)
        self.keep = keep
        self.spreading = None
        self.extra = None
        self.received = self.swap(send, first)

    def swap(self, value, label):
        return swap_bit(value, label[0], self.sizes[label[0]], label[1])

    def step(self, event):
        received = after(self.received, event)
        if self.order:
            label = self.order.pop(0)
            place = self.labels.index(label)
            self.labels.pop(place)
            send, self.keep = combine(self.keep, received, 1 << place)
            self.received = self.swap(send, label)
        elif self.spreading is None:
            if self.extra is None:
                self.keep = add_last(self.keep, received)
            else:
                self.keep = pack(self.keep, received, self.extra)
            self.received = None
        else:
            if self.spreading:
                self.keep = merge(self.keep, received)
                self.received = self.swap(self.keep, self.spreading.pop(0))
            else:
                self.far = received
                self.received = None
        return self

    def join(self, other, event):
        received = after(self.received, event)
        label = self.order.pop(0)
        assert self.labels[-1] == label
        self.labels.pop()
        send, self.keep = join(
            self.keep, received, other.keep, other.received, 1 << len(self.labels)
        )
        self.received = self.swap(send, label)
        other.received = None
        return self

    def spread(self, bits):
        self.spreading = [("ctx", bit) for bit in bits]
        self.received = self.swap(self.keep, self.spreading.pop(0))


def places(bits):
    count = len(bits) - 1
    return [
        sum(((number >> (count - 1 - turn)) & 1) << (bits[turn] - 1) for turn in range(count))
        for number in range(1 << count)
    ]


def finish_kernel(dim, order, label_ref, source, *refs):
    out_ref, token_ref = refs[-2:]
    token_ref[...] = jnp.zeros_like(token_ref)
    count, height, _ = source.shape
    rows, columns = out_ref.shape
    if dim == 0:
        rows = rows // count
    else:
        columns = columns // count
    first = height - rows
    low = label_ref[1] & (count - 1)
    for number in range(count):
        place = order[number] ^ low
        value = source[number, first:].astype(F32)
        if dim == 0:
            out_ref[pl.ds(pl.multiple_of(place * rows, LANES), rows), :] = value
        else:
            out_ref[:, pl.ds(pl.multiple_of(place * columns, LANES), columns)] = value


def finish(source, before, other, table, dim, rows, columns, bits, events=()):
    half, height, width = source.shape
    order = places(bits)
    group = half // 2 if bits[0] == max(bits) else half
    count = half // group
    shift = bits_of(group)

    def index(n, t):
        return (other ^ t[0]) * count + (n ^ (t[1] >> shift))

    if dim == 0:
        shape = (2 * half * rows, columns)
        out_spec = pl.BlockSpec((group * rows, columns), lambda n, t: (index(n, t), 0))
    else:
        shape = (rows, 2 * half * columns)
        out_spec = pl.BlockSpec((rows, group * columns), lambda n, t: (0, index(n, t)))
    earlier = [] if before is None else [before]
    return pl.pallas_call(
        functools.partial(finish_kernel, dim, order[:group]),
        grid_spec=pltpu.PrefetchScalarGridSpec(
            num_scalar_prefetch=1,
            grid=(count,),
            in_specs=[pl.BlockSpec((group, height, width), lambda n, t: (n, 0, 0))]
            + [pl.BlockSpec(memory_space=pl.ANY) for _ in earlier]
            + [whole(event.shape) for event in events],
            out_specs=[out_spec, whole(TOKEN.shape)],
        ),
        out_shape=[jax.ShapeDtypeStruct(shape, F32), TOKEN],
        input_output_aliases={2: 0} if earlier else {},
        compiler_params=params(),
        cost_estimate=cost(0, 0),
        name="finish",
    )(table, source, *earlier, *events)


def finish_rows_kernel(rows, width, low_bits, order, label_ref, near_ref, far_ref, *refs):
    out_ref, token_ref = refs[-2:]
    token_ref[...] = jnp.zeros_like(token_ref)
    half, _, columns = near_ref.shape
    height, moves = tiles(rows, width, columns)
    for number in range(2 * half):
        source = far_ref if number & 1 else near_ref
        owner = ((order[number >> 1] << 1) | (number & 1)) ^ ((label_ref[1] << 1) | label_ref[0])
        if low_bits is None:
            place, begin, stride = owner, 0, LANES
        else:
            place = owner & ((1 << low_bits) - 1)
            begin = (owner >> low_bits) * LANES
            stride = out_ref.shape[1] // (width // LANES)
        for row, column, from_row, from_column in moves:
            down = pl.ds(pl.multiple_of(place * rows + row, 32), height)
            across = begin + (column // LANES) * stride
            if low_bits is not None:
                across = pl.multiple_of(across, LANES)
            out_ref[down, pl.ds(across, LANES)] = source[
                number >> 1, from_row : from_row + height, from_column : from_column + LANES
            ].astype(F32)


def finish_rows(near, far, table, rows, width, low_bits, shape, bits, events=()):
    half, _, columns = near.shape
    block = pl.BlockSpec((half, rows * width // columns, columns), lambda n, t: (0, 0, 0))
    return pl.pallas_call(
        functools.partial(finish_rows_kernel, rows, width, low_bits, places(bits)),
        grid_spec=pltpu.PrefetchScalarGridSpec(
            num_scalar_prefetch=1,
            grid=(1,),
            in_specs=[block, block] + [whole(event.keep.shape) for event in events],
            out_specs=[whole(shape), whole(TOKEN.shape)],
        ),
        out_shape=[jax.ShapeDtypeStruct(shape, F32), TOKEN],
        compiler_params=params(),
        cost_estimate=cost(0, 0),
        name="finish_rows",
    )(table, near, far, *[event.keep for event in events])


def finish_extra_kernel(rows, low_bits, order, label_ref, near_ref, far_ref, *refs):
    out_ref, token_ref = refs[-2:]
    token_ref[...] = jnp.zeros_like(token_ref)
    half, height, columns = near_ref.shape
    for number in range(2 * half):
        source = far_ref if number & 1 else near_ref
        owner = ((order[number >> 1] << 1) | (number & 1)) ^ ((label_ref[1] << 1) | label_ref[0])
        if low_bits is None:
            place, begin = owner, 0
        else:
            place = owner & ((1 << low_bits) - 1)
            begin = pl.multiple_of((owner >> low_bits) * LANES, LANES)
        for across in range(columns // LANES):
            down = pl.multiple_of(place * rows + across * height, 32)
            out_ref[pl.ds(down, height), pl.ds(begin, LANES)] = source[
                number >> 1, :, across * LANES : (across + 1) * LANES
            ].astype(F32)


def finish_extra(near, far, table, rows, width, low_bits, shape, bits, events=()):
    half, _, columns = near.shape
    steps = width // LANES
    block = pl.BlockSpec((half, rows * LANES // columns, columns), lambda n, t: (0, n, 0))
    return pl.pallas_call(
        functools.partial(finish_extra_kernel, rows, low_bits, places(bits)),
        grid_spec=pltpu.PrefetchScalarGridSpec(
            num_scalar_prefetch=1,
            grid=(steps,),
            in_specs=[block, block] + [whole(event.keep.shape) for event in events],
            out_specs=[
                pl.BlockSpec((shape[0], shape[1] // steps), lambda n, t: (0, n)),
                whole(TOKEN.shape),
            ],
        ),
        out_shape=[jax.ShapeDtypeStruct(shape, F32), TOKEN],
        compiler_params=params(),
        cost_estimate=cost(0, 0),
        name="finish_extra",
    )(table, near, far, *[event.keep for event in events])


class Total:
    def __init__(self, value, labels, sizes):
        self.keep = value
        self.sizes = dict(fsdp=sizes[0], ctx=sizes[1])
        self.labels = list(labels)
        self.start()

    def start(self):
        self.received = None
        if self.labels:
            name, bit = self.labels.pop(0)
            self.received = swap_bit(self.keep, name, self.sizes[name], bit)

    def step(self, event):
        received = after(self.received, event)
        self.keep = pl.pallas_call(
            total_kernel,
            out_shape=jax.ShapeDtypeStruct(self.keep.shape, F32),
            compiler_params=params(),
            cost_estimate=cost(0, 0),
            name="total",
        )(self.keep, received)
        self.start()
        return self


def total_kernel(one_ref, two_ref, out_ref):
    out_ref[...] = one_ref[...] + two_ref[...]


def body(
    sizes,
    layer_input,
    output_grad,
    segments,
    assignment,
    first_gain,
    first_bias,
    input_weight,
    query_bias,
    value_bias,
    output_weight,
    output_bias,
    second_gain,
    second_bias,
    expand_weight,
    expand_bias,
    shrink_weight,
    shrink_bias,
):
    fsdp_size, ctx_size = sizes
    seqs, rows, features = layer_input.shape
    tokens = seqs * rows
    hidden = expand_weight.shape[1]
    pairs = features // LANES
    units = seqs * pairs // ctx_size
    y_index = lax.axis_index("fsdp").astype(jnp.int32)
    c_index = lax.axis_index("ctx").astype(jnp.int32)
    part = features // fsdp_size
    small = jnp.concatenate(
        [
            first_gain,
            first_bias,
            query_bias,
            value_bias,
            output_bias,
            second_gain,
            second_bias,
            shrink_bias,
            expand_bias,
        ]
    )
    small = small.reshape(1, -1)
    x = layer_input.reshape(tokens, features)
    og = output_grad.reshape(tokens, features)
    place = (sizes, y_index, c_index)
    core = c_index & 1
    starts = jnp.sum(
        (segments[:, None, :] < segments[:, :, None]).astype(jnp.int32), axis=-1
    )[:, None, :]
    unit_seqs = (c_index * units + jnp.arange(units, dtype=jnp.int32)) & (seqs - 1)
    input_gather = Gather(input_weight, 0, place, (1, 0))
    output_gather = Gather(output_weight, 1, place, (0,))
    expand_gather = Gather(expand_weight, 0, place, (1,), core)
    shrink_gather = Gather(shrink_weight, 1, place, (), core)

    group = ((c_index * units) & (seqs - 1)) >> bits_of(units)
    low_bits = bits_of(ctx_size // pairs)
    low = 1 << low_bits
    if fsdp_size == 2:
        owners = jnp.stack([y_index, 1 - y_index])
    else:
        owners = jnp.arange(fsdp_size, dtype=jnp.int32)

    small, expand_gather.first = lax.optimization_barrier((small, expand_gather.first))
    input_gather.fetch()
    if fsdp_size == 2:
        shards = [small, swap_bit(small, "fsdp", 2, 0)]
    else:
        full = lax.all_gather(small, "fsdp", axis=0)
        shards = [full[number] for number in range(fsdp_size)]
    ready = (
        x,
        shards[-1],
        starts,
        [gather.first for gather in (output_gather, shrink_gather)],
        [
            unit_seqs,
            owners,
            input_gather.offsets,
            output_gather.offsets,
            feed_scalars(place, hidden, WIDTH, expand_gather.offsets, shrink_gather.offsets),
            jnp.stack([core, c_index >> 1]),
            jnp.concatenate([output_gather.offsets, jnp.stack([y_index, c_index])]),
            jnp.concatenate([input_gather.offsets, core[None]]),
            jnp.stack([group, y_index, c_index & (low - 1)]),
        ],
    )
    x, shards[-1], starts, firsts, tables = lax.optimization_barrier(ready)
    for gather, first in zip((output_gather, shrink_gather), firsts):
        gather.first = first
    unit_seqs, owners, input_gather.offsets, output_gather.offsets, *tables = tables
    feed_table, finish_table, back_table, entry_table, terms_table = tables

    small_done = Event(shards[-1])
    input_gather.keep = after(input_gather.keep, small_done)
    shards[-1] = small_done.keep
    h1, vectors, expand_vector = first_norm(x, shards, owners, hidden)
    other = Event(swap_bit(og, "ctx", ctx_size, 0))
    expand_gather.fetch(input_gather)
    input_gather.exchange()
    norm_done = Event(h1)
    input_gather.keep = after(input_gather.keep, norm_done)
    h1 = norm_done.keep
    input_gather.exchange()
    expand_first = Event(after(expand_gather.keep, input_gather))
    expand_gather.exchange()
    output_gather.fetch(expand_first)
    h1 = after(h1, expand_first)
    qkv, token = project(h1, vectors, input_gather.result(), seqs, rows)
    expand_gather.held[0] = expand_first.keep
    project_done = Event(token)
    shrink_gather.fetch(output_gather)
    output_gather.exchange()
    output_gather.keep = after(output_gather.keep, project_done)
    qkv = qkv.reshape(ctx_size, units, rows, 3 * LANES)
    qkv = lax.all_to_all(qkv, "ctx", 0, 0, tiled=True)
    qkv = after(after(qkv, output_gather), other)
    og_other = other.keep
    att, lse = attend(assignment, unit_seqs, qkv, starts)
    attend_done = Event(lse)
    shrink_gather.keep = after(shrink_gather.keep, attend_done)
    att = lax.all_to_all(att, "ctx", 0, 0, tiled=True)
    received = Event(after(after(att, expand_gather), shrink_gather))
    gathered = lax.all_gather(
        after(h1, received).reshape(seqs, rows, features), "ctx", axis=0
    )
    att = received.keep.reshape(pairs, seqs, rows, LANES)
    output_parts = output_gather.result()
    residual, h2, mixed = branch(att, x, vectors, output_parts)
    h2_other = swap_bit(h2, "ctx", ctx_size, 0)
    dh2_send, dh2_keep, out_send, out_keep, send_s, keep_s, send_e, keep_e, eb_grad, sb_grad = feed_forward(
        feed_table,
        residual,
        h2,
        h2_other,
        og,
        og_other,
        vectors,
        expand_vector,
        expand_gather.result(),
        shrink_gather.result(),
        sizes,
    )
    dh2_other = swap_bit(dh2_send, "ctx", ctx_size, 0)
    out_other = swap_bit(out_send, "ctx", ctx_size, 0)

    every = [("fsdp", bit) for bit in reversed(range(bits_of(fsdp_size)))]
    high = [("ctx", bit) for bit in reversed(range(1, bits_of(ctx_size)))]
    flow_s = Flow(send_s, keep_s, every[0], every[1:] + high, every[1:] + high[::-1], sizes)
    dres, dmixed, keep_o, send_o, vec_two = branch_back(
        back_table, dh2_keep, dh2_other, residual, og, mixed, vectors, output_parts, sizes, seqs, rows
    )
    branch_done = Event(vec_two)
    send_e = after(send_e, branch_done)
    flow_e = Flow(send_e, keep_e, every[0], every[1:] + high, every[1:] + high[::-1], sizes)
    spread_s = [bit for _, bit in high] + [0]
    spread_e = spread_s
    flow_o = Flow(send_o, keep_o, ("ctx", 0), every + high, every + high[::-1], sizes)
    dmixed = dmixed.reshape(ctx_size, units, rows, LANES)
    dmixed = lax.all_to_all(dmixed, "ctx", 0, 0, tiled=True)
    dqkv, token = attend_back(
        assignment, unit_seqs, qkv, dmixed, starts, attend_done.keep
    )
    back_done = Event(token)
    last = flow_s.step(back_done)
    out_done = Event(out_other)
    held = Event(after(after(dqkv, last), out_done))
    out_other = out_done.keep
    keep_i, send_i, token = input_weight_terms(gathered, held.keep, terms_table, low, fsdp_size)
    terms_done = Event(token)
    low_labels = [("ctx", bit) for bit in reversed(range(low_bits))]
    flow_i = Flow(
        send_i,
        keep_i,
        low_labels[0],
        low_labels[1:] + every,
        low_labels[1:] + every,
        sizes,
    )
    last = flow_i.step(terms_done)
    last = flow_o.step(last)
    while len(flow_e.order) >= len(high):
        last = flow_e.step(last)
    last = flow_s.step(last)
    dqkv = lax.all_to_all(dqkv, "ctx", 0, 0, tiled=True).reshape(pairs, seqs, rows, 3 * LANES)
    last = flow_o.step(last)
    while flow_i.received is not None:
        last = flow_i.step(last)
    last = flow_s.step(last)
    while len(flow_o.order) > len(flow_e.order):
        last = flow_o.step(last)
    flow_o.received = after(flow_o.received, last)
    last = flow_e.join(flow_o, last)
    flow_s.extra = flow_i.keep[0]
    while flow_s.order:
        last = flow_s.step(last)
    last = flow_s.step(last)
    flow_s.spread(spread_s)
    input_grad, out, sums = entry_back(
        after(dqkv, last),
        x,
        dres,
        out_keep,
        out_other,
        [branch_done.keep, sb_grad, eb_grad],
        vectors,
        (input_gather.result()[0], entry_table),
    )
    totals = Total(sums, every + high[::-1] + [("ctx", 0)], sizes)
    last = totals
    while flow_e.order:
        last = flow_e.step(last)
    last = flow_s.step(last)
    for _ in range(len(every) + 2):
        last = totals.step(last)
    last = flow_e.step(last)
    flow_e.spread(spread_e)
    last = flow_s.step(last)
    last = flow_e.step(last)
    while totals.received is not None:
        last = totals.step(last)
    while len(flow_e.spreading) > 1:
        last = flow_e.step(last)
    while flow_s.spreading:
        last = flow_s.step(last)
    rows_s = hidden // ctx_size
    sums = totals.keep
    own_sums = lax.dynamic_slice_in_dim(sums[:8], y_index * part, part, 1)
    hidden_part = hidden // fsdp_size
    own_hidden = lax.dynamic_slice_in_dim(
        sums[8:].reshape(1, hidden), y_index * hidden_part, hidden_part, 1
    )
    shrink_grad, token = finish(
        flow_s.keep,
        None,
        0,
        finish_table,
        0,
        rows_s,
        part,
        spread_s,
        [own_sums, own_hidden],
    )
    flow_s.received = after(flow_s.received, Event(token))
    last = flow_s.step(last)
    shrink_grad, token = finish(
        flow_s.far, shrink_grad, 1, finish_table, 0, rows_s, part, spread_s
    )
    shrink_done = Event(token)
    input_grad_w, token = finish_extra(
        flow_s.keep,
        flow_s.far,
        finish_table,
        part >> low_bits,
        3 * LANES,
        low_bits,
        (part, 3 * features),
        spread_s,
    )
    input_done = Event(token)
    flow_e.received = after(flow_e.received, shrink_done)
    flow_e.received = after(flow_e.received, input_done)
    while flow_e.spreading:
        last = flow_e.step(last)
    expand_grad, token = finish(
        flow_e.keep, None, 0, finish_table, 1, part, rows_s, spread_e
    )
    flow_e.received = after(flow_e.received, Event(token))
    last = flow_e.step(last)
    expand_grad, token = finish(
        flow_e.far, expand_grad, 1, finish_table, 1, part, rows_s, spread_e
    )
    expand_done = Event(token)
    output_grad_w, _ = finish_rows(
        flow_e.keep,
        flow_e.far,
        finish_table,
        features // ctx_size,
        part,
        None,
        (features, part),
        spread_e,
        [project_done, back_done, terms_done, branch_done, shrink_done, input_done, expand_done],
    )
    return (
        out.reshape(seqs, rows, features),
        input_grad.reshape(seqs, rows, features),
        own_sums[0],
        own_sums[1],
        input_grad_w,
        own_sums[2],
        own_sums[3],
        output_grad_w,
        own_sums[6],
        own_sums[4],
        own_sums[5],
        expand_grad,
        own_hidden[0],
        shrink_grad,
        own_sums[7],
    )


def solution(mesh):
    sizes = (mesh.shape["fsdp"], mesh.shape["ctx"])
    return jax.shard_map(
        functools.partial(body, sizes),
        mesh=mesh,
        in_specs=(
            P("fsdp", "ctx", None),
            P("fsdp", "ctx", None),
            P("fsdp", None),
            P(),
            P("fsdp"),
            P("fsdp"),
            P("fsdp", None),
            P("fsdp"),
            P("fsdp"),
            P(None, "fsdp"),
            P("fsdp"),
            P("fsdp"),
            P("fsdp"),
            P("fsdp", None),
            P("fsdp"),
            P(None, "fsdp"),
            P("fsdp"),
        ),
        out_specs=(
            P("fsdp", "ctx", None),
            P("fsdp", "ctx", None),
            P("fsdp"),
            P("fsdp"),
            P("fsdp", None),
            P("fsdp"),
            P("fsdp"),
            P(None, "fsdp"),
            P("fsdp"),
            P("fsdp"),
            P("fsdp"),
            P("fsdp", None),
            P("fsdp"),
            P(None, "fsdp"),
            P("fsdp"),
        ),
        check_vma=False,
    )
```
